32 devices in a mesh: seq: 4 (over y, x), ep: 8 (over z, core).
Axes of the slice: x: 2, y: 2, z: 4, core: 2. Of those that a mesh axis runs over, the one named last changes fastest.
Arguments:
- tokens: bfloat16 [24, 576, 768], P('ep', 'seq'), may hold values from -6 to 6
- routes: int32 [24, 576, 2], P('ep', 'seq'), may hold values from 0 to 31, all different within a row
- priority: int32 [24, 576], P('ep', 'seq'), may hold values from 0 to 431, as said below
- hires: int32 [8], P('ep'), may hold values from 0 to 3
- gain_one: float32 [768], replicated, may hold values from 0.1 to 1.9
- shift_one: float32 [768], replicated, may hold values from -1.8 to 1.8
- w_qkv: bfloat16 [768, 2304], replicated, may hold values from -0.21875 to 0.21875
- w_proj: bfloat16 [768, 768], replicated, may hold values from -6 to 6
- gain_two: float32 [768], replicated, may hold values from 0.1 to 1.9
- shift_two: float32 [768], replicated, may hold values from -1.8 to 1.8
- w_router: bfloat16 [768, 32], replicated, may hold values from -0.15917969 to 0.15917969
- expert_in: bfloat16 [98304, 768], P('ep'), may hold values from -0.21875 to 0.21875
- expert_out: bfloat16 [98304, 768], P('ep'), may hold values from -2.5 to 2.5
- cotangent: bfloat16 [24, 576, 768], P('ep', 'seq'), may hold values from -6 to 6
Outputs:
- output: bfloat16 [24, 576, 768], P('ep', 'seq')
- input_grad: bfloat16 [24, 576, 768], P('ep', 'seq')
- gain_one_grad: float32 [768], replicated
- shift_one_grad: float32 [768], replicated
- qkv_grad: float32 [768, 2304], replicated
- proj_grad: float32 [768, 768], replicated
- gain_two_grad: float32 [768], replicated
- shift_two_grad: float32 [768], replicated
- router_grad: float32 [768, 32], replicated
- expert_in_grad: float32 [98304, 768], P('ep')
- expert_out_grad: float32 [98304, 768], P('ep')
- rms_stats: float32 [3], replicated
The draws below stay inside these ranges and needn't reach their ends.
Inputs may be any that keep to these rules, and one draw needn't show every extreme that they name: `priority`: within each device block of 3 images times 144 positions, the priorities are a permutation of 0 to 431.
All inputs are finite; a program needn't handle non-finite values.
Results may differ from the reference program's by a relative error of at most 0.015.
Values may be sent and summed in bfloat16 or wider, within the bound.
No kernel may reach another device: no remote copies, remote signals or barrier semaphores. Data moves between devices by JAX's collectives and lax.ppermute only.
A program may use at most 320 MiB of HBM per device.

```python
from functools import partial
import jax
import jax.numpy as jnp
from jax import lax

D = 768
HEADS = 12
HEAD_DIM = 64
FF = 3072
EXPERTS = 32
TOP = 2
PATCHES = 576
SHORT = 196
IMG_DEV = 3
IMAGES = 24
SROW = 144
ROWS_DEV = 432
SPLIT = 1
FF_LOC = 3072
CAP = 29
N_SEQ = 4
N_EP = 8


def draw_priority(key, part):
    group_count = IMAGES // IMG_DEV
    seq_count = PATCHES // SROW
    block_keys = jax.random.split(key, group_count * seq_count)
    orders = jax.vmap(lambda block_key: jax.random.permutation(block_key, ROWS_DEV))(block_keys)
    arranged = orders.reshape(group_count, seq_count, IMG_DEV, SROW)
    return jnp.transpose(arranged, (0, 2, 1, 3)).reshape(IMAGES, PATCHES).astype(jnp.int32)


def place_ends(result, own_key, least, high):
    place = [jax.random.randint(jax.random.fold_in(own_key, axis), (), 0, length) for axis, length in enumerate(result.shape)]
    widest = result.shape.index(max(result.shape))
    neighbour = place[:widest] + [(place[widest] + 1) % result.shape[widest]] + place[widest + 1:]
    return result.at[tuple(place)].set(least).at[tuple(neighbour)].set(high)


def shard_levels(own_key, shape, cuts, smallest, high):
    level = 1.0
    for axis_at, shards_of in cuts:
        heights = jax.random.uniform(jax.random.fold_in(jax.random.fold_in(own_key, 6), axis_at), (shards_of,), jnp.float32, smallest / len(cuts), high / len(cuts))
        level = level * jnp.repeat(jnp.exp(heights), shape[axis_at] // shards_of).reshape((-1,) + (1,) * (len(shape) - 1 - axis_at))
    return level


def different_ones(rng, rows, count, top, lift):
    sequence = jax.random.permutation(jax.random.fold_in(rng, 1), count)
    boost = sequence
    for power in range(3):
        boost = boost * boost // count
    boost = boost * lift // count
    tickets = jax.random.randint(jax.random.fold_in(rng, 2), (rows, count), 0, 4096) + boost
    fixed_rows = jax.random.permutation(jax.random.fold_in(rng, 3), rows)[jnp.arange(count) % rows]
    tickets = jnp.where(jnp.arange(rows)[:, None] == fixed_rows[None, :], 1 << 14, tickets)
    score = tickets * count + jnp.arange(count)
    return lax.top_k(score.astype(jnp.int32), top)[1].astype(jnp.int32)


def normal_values(key, dims, width, limit, cuts=(), held_as=jnp.bfloat16):
    entries = width * jax.random.normal(key, dims, jnp.float32)
    if cuts:
        entries = entries * shard_levels(key, dims, cuts, -0.22, 0.18)
    return jnp.clip(entries, -limit, limit).astype(held_as)


def setup_inputs(seed: int = 0) -> dict:
    arg_keys = jax.random.split(jax.random.key(seed), 15)
    tokens = normal_values(arg_keys[0], (IMAGES, PATCHES, D), 1.0, 6.0, ((0, 8), (1, 4)))
    routes = different_ones(arg_keys[1], IMAGES * PATCHES, EXPERTS, TOP, 512).reshape((IMAGES, PATCHES, TOP))
    priority = draw_priority(jax.random.fold_in(arg_keys[14], 71), 0)
    hires = place_ends(jax.random.randint(arg_keys[3], (IMAGES // IMG_DEV,), 0, IMG_DEV + 1), jax.random.fold_in(arg_keys[3], 1), 0, IMG_DEV).astype(jnp.int32)
    gain_one = jnp.clip(1.0 + 0.18 * jax.random.normal(arg_keys[4], (D,), jnp.float32), 0.1, 1.9)
    shift_one = normal_values(arg_keys[5], (D,), 0.3, 1.8, (), jnp.float32)
    w_qkv = normal_values(arg_keys[6], (D, 3 * D), D ** -0.5, 0.21875)
    w_proj = normal_values(arg_keys[7], (D, D), (max(1, 2 * D // (PATCHES + SHORT))) ** -0.5, 6.0)
    gain_two = jnp.clip(1.0 + 0.18 * jax.random.normal(arg_keys[8], (D,), jnp.float32), 0.1, 1.9)
    shift_two = normal_values(arg_keys[9], (D,), 0.3, 1.8, (), jnp.float32)
    w_router = normal_values(arg_keys[10], (D, EXPERTS), 0.027, 0.15917969)
    expert_in = normal_values(arg_keys[11], (EXPERTS * FF, D), D ** -0.5, 0.21875, ((0, 8),))
    expert_out = normal_values(arg_keys[12], (EXPERTS * FF, D), (max(1, FF // 600)) ** -0.5, 2.5, ((0, 8),))
    cotangent = normal_values(arg_keys[13], (IMAGES, PATCHES, D), 1.0, 6.0, ((0, 8), (1, 4)))
    return dict(tokens=tokens, routes=routes, priority=priority, hires=hires, gain_one=gain_one, shift_one=shift_one, w_qkv=w_qkv, w_proj=w_proj, gain_two=gain_two, shift_two=shift_two, w_router=w_router, expert_in=expert_in, expert_out=expert_out, cotangent=cotangent)


@jax.custom_vjp
def low(v):
    return lax.optimization_barrier(v.astype(jnp.bfloat16)).astype(jnp.float32)

@jax.custom_vjp
def low_back(v):
    return v

def low_keep(v):
    return (low(v), None)

def low_pass(kept, grad):
    return (grad,)

def back_keep(v):
    return (v, None)

def back_low(kept, grad):
    return (low(grad),)
low.defvjp(low_keep, low_pass)
low_back.defvjp(back_keep, back_low)

def round_both(values):
    return low(low_back(values))

def layer_norm(values, norm_gain, norm_bias):
    row_mean = lax.optimization_barrier(jnp.mean(values, axis=-1, keepdims=True))
    centred = values - row_mean
    inv_root = lax.rsqrt(lax.optimization_barrier(jnp.mean(centred * centred, axis=-1, keepdims=True)) + 1e-06)
    return centred * inv_root * norm_gain + norm_bias

def to_blocks(values):
    shape_tail = values.shape[2:]
    grouped = values.reshape((N_EP, IMG_DEV, N_SEQ, SROW) + shape_tail)
    grouped = jnp.swapaxes(grouped, 1, 2)
    return grouped.reshape((N_EP * N_SEQ, ROWS_DEV) + shape_tail)

def from_blocks(values):
    shape_tail = values.shape[2:]
    grouped = values.reshape((N_EP, N_SEQ, IMG_DEV, SROW) + shape_tail)
    return jnp.swapaxes(grouped, 1, 2).reshape((IMAGES, PATCHES) + shape_tail)

def routing(route_rows, priority_rows, row_valid, capacity):
    row_total = route_rows.shape[0]
    by_priority = jnp.zeros((row_total,), jnp.int32).at[priority_rows].set(jnp.arange(row_total, dtype=jnp.int32))
    ordered = jnp.concatenate([route_rows[by_priority, route_rank] for route_rank in range(TOP)])
    ordered_valid = jnp.concatenate([row_valid[by_priority]] * TOP)
    expert_hits = (ordered[:, None] == jnp.arange(EXPERTS, dtype=jnp.int32)[None, :]) & ordered_valid[:, None]
    running = jnp.cumsum(expert_hits.astype(jnp.int32), axis=0).astype(jnp.int32)
    ordered_slot = (lax.optimization_barrier(jnp.sum(jnp.where(expert_hits, running, 0), axis=1)) - 1).astype(jnp.int32)
    pair_slot = ordered_slot.reshape(TOP, row_total)[:, priority_rows].T
    is_kept = (pair_slot >= 0) & (pair_slot < capacity)
    return jnp.where(is_kept, route_rows * capacity + pair_slot, EXPERTS * capacity).astype(jnp.int32)

def slot_sources(slot_dest, fill_value, capacity, divisor):
    flat_dest = slot_dest.reshape(-1)
    source_ids = (jnp.arange(flat_dest.shape[0], dtype=jnp.int32) // divisor).astype(jnp.int32)
    table_ids = jnp.full((EXPERTS * capacity + 1,), fill_value, jnp.int32).at[flat_dest].set(source_ids)
    return table_ids[:EXPERTS * capacity]

def take_rows(source_rows, row_index):
    return source_rows[row_index]

def attend(attn_group, valid_group, qkv_weight):
    packed = round_both(jnp.einsum('ipd,de->ipe', attn_group, qkv_weight, precision=lax.Precision.HIGHEST))
    head_shape = (IMG_DEV, PATCHES, HEADS, HEAD_DIM)
    query_heads = packed[..., :D].reshape(head_shape)
    key_heads = packed[..., D:2 * D].reshape(head_shape)
    value_heads = packed[..., 2 * D:].reshape(head_shape)
    scores = low_back(jnp.einsum('ishd,ithd->ihst', query_heads, key_heads, precision=lax.Precision.HIGHEST) * HEAD_DIM ** (-0.5))
    scores = jnp.where(valid_group[:, None, None, :], scores, -1e+30)
    probs = low(jax.nn.softmax(scores, axis=-1))
    attended = jnp.einsum('ihst,ithd->ishd', probs, value_heads, precision=lax.Precision.HIGHEST)
    return round_both(attended.reshape(IMG_DEV, PATCHES, D))

def expert_block(expert_args):
    rows_in, first_rows, second_rows = expert_args
    expert_value = jnp.zeros(rows_in.shape, jnp.float32)
    for part_index in range(SPLIT):
        part_start = part_index * FF_LOC
        part_in = low_back(rows_in)
        pre_act = low_back(jnp.einsum('ncd,fd->ncf', part_in, first_rows[part_start:part_start + FF_LOC], precision=lax.Precision.HIGHEST))
        hidden = low(jax.nn.gelu(pre_act, approximate=False))
        part_out = round_both(jnp.einsum('ncf,fd->ncd', hidden, second_rows[part_start:part_start + FF_LOC], precision=lax.Precision.HIGHEST))
        expert_value = expert_value + part_out
    return expert_value

def to_float(array_in):
    return array_in.astype(jnp.float32)

def reference(tokens, routes, priority, hires, gain_one, shift_one, w_qkv, w_proj, gain_two, shift_two, w_router, expert_in, expert_out, cotangent):
    block_count = N_EP * N_SEQ
    image_ids = jnp.arange(IMAGES, dtype=jnp.int32)
    image_length = jnp.where(image_ids % IMG_DEV < hires[image_ids // IMG_DEV], PATCHES, SHORT)
    patch_valid = jnp.arange(PATCHES, dtype=jnp.int32)[None, :] < image_length[:, None]
    block_valid = to_blocks(patch_valid)
    block_routes = to_blocks(routes)
    block_priority = to_blocks(priority)
    slot_dest = jax.vmap(partial(routing, capacity=CAP))(block_routes, block_priority, block_valid)
    token_src = jax.vmap(partial(slot_sources, fill_value=ROWS_DEV, capacity=CAP, divisor=TOP))(slot_dest)

    def forward(inputs, norm_gain_one, norm_shift_one, qkv_weight, proj_weight, norm_gain_two, norm_shift_two, router_weight, first_weight, second_weight):
        attn_in = low(layer_norm(inputs, norm_gain_one, norm_shift_one))

        def attend_group(group_args):
            return attend(group_args[0], group_args[1], qkv_weight)
        grouped_in = attn_in.reshape(N_EP, IMG_DEV, PATCHES, D)
        grouped_valid = patch_valid.reshape(N_EP, IMG_DEV, PATCHES)
        attended = lax.map(jax.checkpoint(attend_group), (grouped_in, grouped_valid)).reshape(IMAGES, PATCHES, D)
        attn_out = low_back(jnp.einsum('ipd,de->ipe', attended, proj_weight, precision=lax.Precision.HIGHEST))
        middle = inputs + attn_out
        moe_in = low(layer_norm(middle, norm_gain_two, norm_shift_two))
        logits = low_back(jnp.einsum('ipd,de->ipe', moe_in, router_weight, precision=lax.Precision.HIGHEST))
        gate_probs = jax.nn.softmax(logits, axis=-1)
        block_in = to_blocks(moe_in)
        padded_in = jnp.concatenate([block_in, jnp.zeros((block_count, 1, D), jnp.float32)], axis=1)
        dispatched = jax.vmap(take_rows)(padded_in, token_src).reshape(block_count, EXPERTS, CAP, D)
        per_expert = jnp.swapaxes(dispatched, 0, 1)
        first_split = first_weight.reshape(EXPERTS, FF, D)
        second_split = second_weight.reshape(EXPERTS, FF, D)
        expert_values = lax.map(jax.checkpoint(expert_block), (per_expert, first_split, second_split))
        value_table = jnp.swapaxes(expert_values, 0, 1).reshape(block_count, EXPERTS * CAP, D)
        padded_values = jnp.concatenate([value_table, jnp.zeros((block_count, 1, D), jnp.float32)], axis=1)
        pair_values = jax.vmap(take_rows)(padded_values, slot_dest.reshape(block_count, ROWS_DEV * TOP))
        pair_values = pair_values.reshape(block_count, ROWS_DEV, TOP, D)
        chosen = jnp.take_along_axis(to_blocks(gate_probs), block_routes, axis=2)
        moe_block = lax.optimization_barrier(jnp.sum(chosen[..., None] * pair_values, axis=2))
        moe_out = from_blocks(moe_block)
        total = middle + moe_out
        output = total * patch_valid[..., None].astype(jnp.float32)
        return (output, (attn_out, moe_out, total))
    params = tuple((to_float(array_in) for array_in in (tokens, gain_one, shift_one, w_qkv, w_proj, gain_two, shift_two, w_router, expert_in, expert_out)))
    output, pullback, side_values = jax.vjp(forward, *params, has_aux=True)
    grads = pullback(cotangent.astype(jnp.float32))
    attn_out, moe_out, total = side_values
    count = jnp.sum(patch_valid.astype(jnp.float32)) * D
    mask_cube = patch_valid[..., None]
    squares = jnp.stack([jnp.sum(jnp.where(mask_cube, attn_out * attn_out, 0.0)), jnp.sum(jnp.where(mask_cube, moe_out * moe_out, 0.0)), jnp.sum(jnp.where(mask_cube, total * total, 0.0))])
    rms_stats = jnp.sqrt(squares / count)
    return (output.astype(jnp.bfloat16), grads[0].astype(jnp.bfloat16), grads[1], grads[2], grads[3], grads[4], grads[5], grads[6], grads[7], grads[8], grads[9], rms_stats)
```

```python
import jax
import jax.numpy as jnp
from jax import lax
from jax.sharding import PartitionSpec as P

HEADS = 12
EXPERTS = 32
TOP = 2
PATCHES = 576
SHORT = 196


norm_eps = 1e-06
neg_big = -1e30


def norm_forward(values, norm_gain, norm_bias):
    row_mean = jnp.mean(values, axis=-1, keepdims=True)
    centred = values - row_mean
    inv_root = lax.rsqrt(jnp.mean(centred * centred, axis=-1, keepdims=True) + norm_eps)
    normed = centred * inv_root
    return (normed * norm_gain + norm_bias, normed, inv_root)


def norm_backward(grad_out, normed, inv_root, norm_gain):
    gain_grad = jnp.sum(grad_out * normed, axis=0)
    bias_grad = jnp.sum(grad_out, axis=0)
    scaled = grad_out * norm_gain
    grad_in = inv_root * (
        scaled
        - jnp.mean(scaled, axis=-1, keepdims=True)
        - normed * jnp.mean(scaled * normed, axis=-1, keepdims=True)
    )
    return (grad_in, gain_grad, bias_grad)


def gelu_slope(values):
    return (
        0.5 * (1.0 + lax.erf(values * 0.7071067811865476))
        + values * jnp.exp(-0.5 * values * values) * 0.3989422804014327
    )


def routing(route_rows, priority_rows, row_valid, capacity):
    row_total = route_rows.shape[0]
    by_priority = (
        jnp.zeros((row_total,), jnp.int32)
        .at[priority_rows]
        .set(jnp.arange(row_total, dtype=jnp.int32))
    )
    ordered = jnp.concatenate([route_rows[by_priority, route_rank] for route_rank in range(TOP)])
    ordered_valid = jnp.concatenate([row_valid[by_priority]] * TOP)
    expert_hits = (
        ordered[:, None] == jnp.arange(EXPERTS, dtype=jnp.int32)[None, :]
    ) & ordered_valid[:, None]
    running = jnp.cumsum(expert_hits.astype(jnp.int32), axis=0)
    ordered_slot = jnp.sum(jnp.where(expert_hits, running, 0), axis=1) - 1
    pair_slot = ordered_slot.reshape(TOP, row_total)[:, priority_rows].T
    is_kept = (pair_slot >= 0) & (pair_slot < capacity)
    return jnp.where(is_kept, route_rows * capacity + pair_slot, EXPERTS * capacity)


def slot_sources(slot_dest, fill_value, capacity, divisor):
    flat_dest = slot_dest.reshape(-1)
    source_ids = jnp.arange(flat_dest.shape[0], dtype=jnp.int32) // divisor
    table_ids = (
        jnp.full((EXPERTS * capacity + 1,), fill_value, jnp.int32).at[flat_dest].set(source_ids)
    )
    return table_ids[: EXPERTS * capacity]


def fan_out(slot_table, ep_count, split_count, local_experts, capacity):
    feature_width = slot_table.shape[-1]
    grouped = slot_table.reshape(ep_count // split_count, 1, local_experts, capacity, feature_width)
    spread = jnp.broadcast_to(
        grouped, (ep_count // split_count, split_count, local_experts, capacity, feature_width)
    )
    return spread.reshape(ep_count, local_experts, capacity, feature_width)


def fan_in(arrived, split_count):
    ep_count, local_experts, capacity, feature_width = arrived.shape
    grouped = arrived.reshape(
        ep_count // split_count, split_count, local_experts, capacity, feature_width
    )
    return jnp.sum(grouped.astype(jnp.float32), axis=1).reshape(-1, feature_width)


def score_block(query_heads, key_heads, key_mask, score_scale):
    raw_scores = (
        jnp.einsum("ishd,ithd->ihst", query_heads, key_heads, preferred_element_type=jnp.float32)
        * score_scale
    )
    return jnp.where(key_mask[:, None, None, :], raw_scores, neg_big)


def per_device(
    tokens,
    routes,
    priority,
    hires,
    gain_one,
    shift_one,
    w_qkv,
    w_proj,
    gain_two,
    shift_two,
    w_router,
    expert_in,
    expert_out,
    cotangent,
):
    image_count, patch_rows, model_width = tokens.shape
    row_count = image_count * patch_rows
    seq_count = lax.axis_size("seq")
    ep_count = lax.axis_size("ep")
    full_patches = patch_rows * seq_count
    head_width = model_width // HEADS
    score_scale = head_width ** (-0.5)
    local_experts = max(1, EXPERTS // ep_count)
    split_count = max(1, ep_count // EXPERTS)
    local_hidden = expert_in.shape[0] // local_experts
    capacity = max(2, (105 * TOP * row_count + 100 * EXPERTS - 1) // (100 * EXPERTS))
    seq_place = lax.axis_index("seq")

    def send_slots(slot_table):
        outgoing = fan_out(slot_table, ep_count, split_count, local_experts, capacity)
        return lax.all_to_all(outgoing, "ep", split_axis=0, concat_axis=0, tiled=True)

    def return_slots(part_rows):
        returned = lax.all_to_all(part_rows, "ep", split_axis=0, concat_axis=0, tiled=True)
        return fan_in(returned, split_count)

    image_length = jnp.where(jnp.arange(image_count, dtype=jnp.int32) < hires[0], PATCHES, SHORT)
    key_mask = jnp.arange(full_patches, dtype=jnp.int32)[None, :] < image_length[:, None]
    own_mask = (seq_place * patch_rows + jnp.arange(patch_rows, dtype=jnp.int32))[
        None, :
    ] < image_length[:, None]
    row_valid = own_mask.reshape(row_count)
    valid_col = row_valid.astype(jnp.float32)[:, None]
    inputs = tokens.reshape(row_count, model_width).astype(jnp.float32)
    head_shape = (image_count, -1, HEADS, head_width)
    first_out, normed_one, inv_one = norm_forward(inputs, gain_one, shift_one)
    attn_in = first_out.astype(jnp.bfloat16)
    packed = jnp.dot(attn_in, w_qkv, preferred_element_type=jnp.float32).astype(jnp.bfloat16)
    query_rows = packed[:, :model_width].reshape(image_count, patch_rows, model_width)
    key_rows = packed[:, model_width : 2 * model_width].reshape(
        image_count, patch_rows, model_width
    )
    value_rows = packed[:, 2 * model_width :].reshape(image_count, patch_rows, model_width)
    query_heads = query_rows.reshape(head_shape)
    keys_all, values_all = (
        lax.all_gather(key_rows, "seq", axis=1, tiled=True),
        lax.all_gather(value_rows, "seq", axis=1, tiled=True),
    )
    scores = score_block(query_heads, keys_all.reshape(head_shape), key_mask, score_scale)
    row_max = jnp.max(scores, axis=-1, keepdims=True)
    exp_scores = jnp.exp(scores - row_max)
    row_total = jnp.sum(exp_scores, axis=-1, keepdims=True)
    probs = exp_scores / row_total
    log_total = row_max + jnp.log(row_total)
    attended = (
        jnp.einsum(
            "ihst,ithd->ishd",
            probs.astype(jnp.bfloat16),
            values_all.reshape(head_shape),
            preferred_element_type=jnp.float32,
        )
        .reshape(row_count, model_width)
        .astype(jnp.bfloat16)
    )
    attn_out = jnp.dot(attended, w_proj, preferred_element_type=jnp.float32)
    middle = inputs + attn_out
    second_out, normed_two, inv_two = norm_forward(middle, gain_two, shift_two)
    moe_in = second_out.astype(jnp.bfloat16)
    logits = jnp.dot(moe_in, w_router, preferred_element_type=jnp.float32)
    gate_probs = jax.nn.softmax(logits, axis=-1)
    route_rows = routes.reshape(row_count, TOP)
    slot_dest = routing(route_rows, priority.reshape(row_count), row_valid, capacity)
    token_src = slot_sources(slot_dest, row_count, capacity, TOP)
    pair_src = slot_sources(slot_dest, row_count * TOP, capacity, 1)
    padded_in = jnp.concatenate([moe_in, jnp.zeros((1, model_width), jnp.bfloat16)], axis=0)
    arrived = send_slots(padded_in[token_src])
    w_first = expert_in.reshape(local_experts, local_hidden, model_width)
    w_second = expert_out.reshape(local_experts, local_hidden, model_width)
    pre_act = jnp.einsum("secd,efd->secf", arrived, w_first, preferred_element_type=jnp.float32)
    hidden = jax.nn.gelu(pre_act, approximate=False).astype(jnp.bfloat16)
    partial_out = jnp.einsum(
        "secf,efd->secd", hidden, w_second, preferred_element_type=jnp.float32
    ).astype(jnp.bfloat16)
    value_table = return_slots(partial_out)
    padded_values = jnp.concatenate([value_table, jnp.zeros((1, model_width), jnp.float32)], axis=0)
    pair_values = padded_values[slot_dest.reshape(-1)].reshape(row_count, TOP, model_width)
    chosen = jnp.take_along_axis(gate_probs, route_rows, axis=1)
    moe_out = jnp.sum(chosen[:, :, None] * pair_values, axis=1)
    total = middle + moe_out
    output = (total * valid_col).astype(jnp.bfloat16).reshape(image_count, patch_rows, model_width)
    stat_terms = jnp.stack(
        [
            jnp.sum(valid_col * attn_out * attn_out),
            jnp.sum(valid_col * moe_out * moe_out),
            jnp.sum(valid_col * total * total),
            jnp.sum(row_valid.astype(jnp.float32)) * model_width,
        ]
    )
    grad_total = cotangent.reshape(row_count, model_width).astype(jnp.float32) * valid_col
    grad_gate = jnp.sum(grad_total[:, None, :] * pair_values, axis=2)
    grad_value = (
        (grad_total[:, None, :] * chosen[:, :, None])
        .astype(jnp.bfloat16)
        .reshape(row_count * TOP, model_width)
    )
    padded_grad = jnp.concatenate([grad_value, jnp.zeros((1, model_width), jnp.bfloat16)], axis=0)
    grad_sent = send_slots(padded_grad[pair_src])
    grad_hidden = jnp.einsum(
        "secd,efd->secf", grad_sent, w_second, preferred_element_type=jnp.float32
    )
    grad_pre = (grad_hidden * gelu_slope(pre_act)).astype(jnp.bfloat16)
    rows_all = lax.all_gather(arrived, "seq", axis=0, tiled=True)
    sent_all = lax.all_gather(grad_sent, "seq", axis=0, tiled=True)
    pre_all = jnp.einsum("secd,efd->secf", rows_all, w_first, preferred_element_type=jnp.float32)
    hidden_all = jax.nn.gelu(pre_all, approximate=False).astype(jnp.bfloat16)
    grad_hidden_all = jnp.einsum(
        "secd,efd->secf", sent_all, w_second, preferred_element_type=jnp.float32
    )
    grad_pre_all = (grad_hidden_all * gelu_slope(pre_all)).astype(jnp.bfloat16)
    grad_second = jnp.einsum(
        "secf,secd->efd", hidden_all, sent_all, preferred_element_type=jnp.float32
    ).reshape(-1, model_width)
    grad_first = jnp.einsum(
        "secf,secd->efd", grad_pre_all, rows_all, preferred_element_type=jnp.float32
    ).reshape(-1, model_width)
    grad_part_in = jnp.einsum(
        "secf,efd->secd", grad_pre, w_first, preferred_element_type=jnp.float32
    ).astype(jnp.bfloat16)
    grad_in_table = return_slots(grad_part_in)
    padded_back = jnp.concatenate([grad_in_table, jnp.zeros((1, model_width), jnp.float32)], axis=0)
    grad_dispatch = jnp.sum(
        padded_back[slot_dest.reshape(-1)].reshape(row_count, TOP, model_width), axis=1
    )
    expert_ids = jnp.arange(EXPERTS, dtype=jnp.int32)
    grad_probs = jnp.sum(
        jnp.where(route_rows[:, :, None] == expert_ids[None, None, :], grad_gate[:, :, None], 0.0),
        axis=1,
    )
    grad_logits = (
        gate_probs * (grad_probs - jnp.sum(grad_probs * gate_probs, axis=-1, keepdims=True))
    ).astype(jnp.bfloat16)
    grad_router = jnp.einsum("rd,re->de", moe_in, grad_logits, preferred_element_type=jnp.float32)
    grad_moe_in = grad_dispatch + jnp.einsum(
        "re,de->rd", grad_logits, w_router, preferred_element_type=jnp.float32
    )
    grad_mid_norm, grad_gain_two, grad_shift_two = norm_backward(
        grad_moe_in, normed_two, inv_two, gain_two
    )
    grad_middle = grad_total + grad_mid_norm
    grad_attn = grad_middle.astype(jnp.bfloat16)
    grad_proj = jnp.einsum("rd,re->de", attended, grad_attn, preferred_element_type=jnp.float32)
    grad_attended = jnp.einsum(
        "re,de->rd", grad_attn, w_proj, preferred_element_type=jnp.float32
    ).astype(jnp.bfloat16)
    grad_heads = grad_attended.reshape(head_shape)
    keys_again, values_again = (
        lax.all_gather(key_rows, "seq", axis=1, tiled=True),
        lax.all_gather(value_rows, "seq", axis=1, tiled=True),
    )
    key_heads = keys_again.reshape(head_shape)
    value_heads = values_again.reshape(head_shape)
    probs_again = jnp.exp(score_block(query_heads, key_heads, key_mask, score_scale) - log_total)
    grad_probs_att = jnp.einsum(
        "ishd,ithd->ihst", grad_heads, value_heads, preferred_element_type=jnp.float32
    )
    delta = jnp.sum(grad_probs_att * probs_again, axis=-1, keepdims=True)
    grad_scores = (probs_again * (grad_probs_att - delta)).astype(jnp.bfloat16)
    grad_queries = (
        jnp.einsum("ihst,ithd->ishd", grad_scores, key_heads, preferred_element_type=jnp.float32)
        * score_scale
    )
    grad_keys_full = (
        jnp.einsum("ihst,ishd->ithd", grad_scores, query_heads, preferred_element_type=jnp.float32)
        * score_scale
    )
    grad_values_full = jnp.einsum(
        "ihst,ishd->ithd",
        probs_again.astype(jnp.bfloat16),
        grad_heads,
        preferred_element_type=jnp.float32,
    )
    grad_keys, grad_values = (
        lax.psum_scatter(
            grad_keys_full.reshape(image_count, full_patches, model_width),
            "seq",
            scatter_dimension=1,
            tiled=True,
        ),
        lax.psum_scatter(
            grad_values_full.reshape(image_count, full_patches, model_width),
            "seq",
            scatter_dimension=1,
            tiled=True,
        ),
    )
    grad_packed = jnp.concatenate(
        [
            grad_queries.reshape(row_count, model_width),
            grad_keys.reshape(row_count, model_width),
            grad_values.reshape(row_count, model_width),
        ],
        axis=1,
    ).astype(jnp.bfloat16)
    grad_qkv = jnp.einsum("rd,re->de", attn_in, grad_packed, preferred_element_type=jnp.float32)
    grad_attn_in = jnp.einsum("re,de->rd", grad_packed, w_qkv, preferred_element_type=jnp.float32)
    grad_in_norm, grad_gain_one, grad_shift_one = norm_backward(
        grad_attn_in, normed_one, inv_one, gain_one
    )
    input_grad = (
        (grad_middle + grad_in_norm)
        .astype(jnp.bfloat16)
        .reshape(image_count, patch_rows, model_width)
    )
    small = lax.psum(
        (
            grad_gain_one,
            grad_shift_one,
            grad_gain_two,
            grad_shift_two,
            stat_terms,
        ),
        ("seq", "ep"),
    )
    big = lax.psum(
        tuple(g.astype(jnp.bfloat16) for g in (grad_qkv, grad_proj, grad_router)),
        ("seq", "ep"),
    )
    summed = tuple(g.astype(jnp.float32) for g in big) + small
    expert_grads = (grad_first, grad_second)
    rms_stats = jnp.sqrt(summed[7][:3] / summed[7][3])
    return (
        output,
        input_grad,
        summed[3],
        summed[4],
        summed[0],
        summed[1],
        summed[5],
        summed[6],
        summed[2],
        expert_grads[0],
        expert_grads[1],
        rms_stats,
    )


def solution(mesh):
    in_specs = (
        P("ep", "seq", None),
        P("ep", "seq", None),
        P("ep", "seq"),
        P("ep"),
        P(),
        P(),
        P(),
        P(),
        P(),
        P(),
        P(),
        P("ep", None),
        P("ep", None),
        P("ep", "seq", None),
    )
    out_specs = (
        P("ep", "seq", None),
        P("ep", "seq", None),
        P(),
        P(),
        P(),
        P(),
        P(),
        P(),
        P(),
        P("ep", None),
        P("ep", None),
        P(),
    )
    return jax.shard_map(
        per_device, mesh=mesh, in_specs=in_specs, out_specs=out_specs, check_vma=False
    )
```

```python
import itertools

import jax
import jax.numpy as jnp
from jax import lax
from jax.experimental import pallas as pl
from jax.experimental.pallas import tpu as pltpu
from jax.sharding import PartitionSpec as P

HEADS = 12
EXPERTS = 32
TOP = 2
PATCHES = 576
SHORT = 196

norm_eps = 1e-06
neg_big = -1e30
f32 = jnp.float32
bf16 = jnp.bfloat16

tail_slope = 0.33
tail_terms = (
    0.18635779800457905,
    0.18295602991113566,
    0.2012232872944192,
    0.04722279904104141,
    0.40849559831839843,
    -0.3511445702318978,
    0.46023391759858995,
    -0.13534486747679436,
)


def mm(a, b):
    return lax.dot_general(a, b, (((1,), (0,)), ((), ())), preferred_element_type=f32)


def mm_nt(a, b):
    return lax.dot_general(a, b, (((1,), (1,)), ((), ())), preferred_element_type=f32)


def mm_tn(a, b):
    return lax.dot_general(a, b, (((0,), (0,)), ((), ())), preferred_element_type=f32)


def gelu_pair(v):
    size = jnp.abs(v)
    bell = jnp.exp(v * v * -0.5)
    t = 1.0 / (1.0 + size * (tail_slope * 0.7071067811865476))
    poly = tail_terms[-1] * 0.5
    for term in tail_terms[-2::-1]:
        poly = poly * t + term * 0.5
    tail = poly * t * bell
    cdf = jnp.where(v >= 0.0, 1.0 - tail, tail)
    return v * cdf, cdf + v * bell * 0.3989422804014327


def normalize(values):
    centred = values - jnp.mean(values, axis=-1, keepdims=True)
    inv_root = lax.rsqrt(jnp.mean(centred * centred, axis=-1, keepdims=True) + norm_eps)
    return centred * inv_root, inv_root


def norm_row_grad(upstream, normed, inv_root, gain):
    scaled = upstream * gain
    return inv_root * (
        scaled
        - jnp.mean(scaled, axis=-1, keepdims=True)
        - normed * jnp.mean(scaled * normed, axis=-1, keepdims=True)
    )


def valid_rows(places_ref, image_count, patch_rows, shape, axis):
    row = lax.broadcasted_iota(jnp.int32, shape, axis)
    first_patch = places_ref[1] * patch_rows
    valid = row < 0
    for image in range(image_count):
        length = jnp.where(image < places_ref[0], PATCHES, SHORT)
        start = image * patch_rows
        stop = start + jnp.clip(length - first_patch, 0, patch_rows)
        valid = valid | ((row >= start) & (row < stop))
    return valid


def routing_kernel(
    places_ref, pairs_ref, route_col_ref, dest_col_ref, dest_row_ref,
    *, image_count, patch_rows, capacity, stride,
):
    rows = pairs_ref.shape[1]
    eye = lax.broadcasted_iota(jnp.int32, (rows, rows), 0) == lax.broadcasted_iota(
        jnp.int32, (rows, rows), 1
    )

    def as_column(line):
        return jnp.sum(jnp.where(eye, line.astype(f32), 0.0), axis=1, keepdims=True).astype(
            jnp.int32
        )

    e_row = [pairs_ref[k : k + 1, :] for k in range(TOP)]
    e_col = [as_column(line) for line in e_row]
    prio_row = pairs_ref[TOP : TOP + 1, :]
    prio_col = as_column(prio_row)
    for k in range(TOP):
        route_col_ref[:, k : k + 1] = e_col[k]
    valid_col = valid_rows(places_ref, image_count, patch_rows, (rows, 1), 0)
    valid_row = valid_rows(places_ref, image_count, patch_rows, (1, rows), 1)
    weight_col = valid_col.astype(f32)
    weight_row = valid_row.astype(f32)
    row_first = (prio_row < prio_col).astype(f32) * weight_row
    col_first = (prio_col < prio_row).astype(f32) * weight_col
    for k in range(TOP):
        count = jnp.where(e_col[k] == e_row[k], row_first, 0.0)
        for earlier in range(k):
            count = count + jnp.where(e_col[k] == e_row[earlier], weight_row, 0.0)
        slot = jnp.sum(count, axis=1, keepdims=True).astype(jnp.int32)
        keep = valid_col & (slot < capacity)
        dest_col_ref[:, k : k + 1] = jnp.where(keep, e_col[k] * stride + slot, -1)
        count = jnp.where(e_col[k] == e_row[k], col_first, 0.0)
        for earlier in range(k):
            count = count + jnp.where(e_col[earlier] == e_row[k], weight_col, 0.0)
        slot = jnp.sum(count, axis=0, keepdims=True).astype(jnp.int32)
        keep = valid_row & (slot < capacity)
        dest_row_ref[k : k + 1, :] = jnp.where(keep, e_row[k] * stride + slot, -1)


def neighbour(places_ref, shift, seq_count):
    return (places_ref[1] + (shift + seq_count)) % seq_count


def attention_kernel(
    places_ref, tokens_ref, gain_ref, shift_ref, weight_ref, *refs,
    group_heads, head_width,
):
    seq_count, _, patch_rows, width = tokens_ref.shape
    attended_refs = refs[:seq_count]
    q_ref, k_ref, v_ref, probs_ref, normed_ref, spread_ref = refs[seq_count:]
    total_rows = seq_count * patch_rows
    group_width = group_heads * head_width
    values = tokens_ref[...].reshape(total_rows, width).astype(f32)
    normed, _ = normalize(values)
    attn_in = (normed * gain_ref[...] + shift_ref[...]).astype(bf16)
    normed_ref[0] = attn_in
    q, k, v = (
        mm_nt(attn_in, weight_ref[0, part * group_width : (part + 1) * group_width, :]).astype(bf16)
        for part in range(3)
    )
    q_ref[0] = q
    k_ref[0] = k
    v_ref[0] = v
    length = jnp.where(pl.program_id(0) < places_ref[0], PATCHES, SHORT)
    key_valid = lax.broadcasted_iota(jnp.int32, (1, total_rows), 1) < length
    lane = lax.broadcasted_iota(jnp.int32, (1, group_width), 1)
    scaled_q = (q.astype(f32) * head_width ** (-0.5)).astype(bf16)
    attended = jnp.zeros((total_rows, group_width), f32)
    for head in range(group_heads):
        in_head = (lane >= head * head_width) & (lane < (head + 1) * head_width)
        scores = mm_nt(jnp.where(in_head, scaled_q, jnp.zeros_like(scaled_q)), k)
        scores = jnp.where(key_valid, scores, neg_big)
        exp_scores = jnp.exp(scores - jnp.max(scores, axis=-1, keepdims=True))
        inverse = 1.0 / jnp.sum(exp_scores, axis=-1, keepdims=True)
        probs = (exp_scores * inverse).astype(bf16)
        probs_ref[0, head] = probs
        attended = jnp.where(in_head, mm(probs, v), attended)
    spread_ref[...] = attended.astype(bf16).reshape(spread_ref.shape)
    for shift, attended_ref in enumerate(attended_refs):
        attended_ref[0] = spread_ref[neighbour(places_ref, shift, seq_count)]


def slot_picks(dest_row_ref, stride, k):
    slot = lax.broadcasted_iota(jnp.int32, (EXPERTS * stride, 1), 0)
    return (slot == dest_row_ref[k : k + 1, :]).astype(f32).astype(bf16)


def send_grads_kernel(cotangent_ref, dest_row_ref, *sent_refs, stride):
    width = cotangent_ref.shape[-1]
    cotangent = cotangent_ref[...].reshape(-1, width)
    pick = slot_picks(dest_row_ref, stride, 0)
    for k in range(1, TOP):
        pick = pick + slot_picks(dest_row_ref, stride, k)
    sent = mm(pick, cotangent).astype(bf16)
    store_chunks(sent_refs, sent, stride)


def store_chunks(chunk_refs, table, stride):
    width = table.shape[-1]
    targets, each = chunk_refs[0].shape[:2]
    grouped = table.reshape(targets, len(chunk_refs) * each, stride, width)
    for at, chunk_ref in enumerate(chunk_refs):
        chunk_ref[...] = grouped[:, at * each : (at + 1) * each]


def three_terms(values):
    high = values.astype(bf16)
    rest = values - high.astype(f32)
    middle = rest.astype(bf16)
    return high, middle, (rest - middle.astype(f32)).astype(bf16)


def diagonal(stride):
    row = lax.broadcasted_iota(jnp.int32, (1, stride, stride), 1)
    return row == lax.broadcasted_iota(jnp.int32, (1, stride, stride), 2)


def row_scalars(block, stride):
    spare = block[:, stride - 3 : stride, :stride].astype(f32)
    line = spare[:, 0:1] + spare[:, 1:2] + spare[:, 2:3]
    return jnp.sum(jnp.where(diagonal(stride), line, 0.0), axis=2, keepdims=True)


def with_scalars(block, column, stride):
    width = block.shape[-1]
    line = jnp.sum(jnp.where(diagonal(stride), column, 0.0), axis=1, keepdims=True)
    line = jnp.concatenate(
        [line, jnp.zeros((line.shape[0], 1, width - stride), f32)], axis=2
    )
    row = lax.broadcasted_iota(jnp.int32, (1, stride, 1), 1)
    for at, term in enumerate(three_terms(line)):
        block = jnp.where(row == stride - 3 + at, term.astype(f32), block)
    return block


def group_rows(places_ref, shift, seq_count, group_width):
    start = neighbour(places_ref, shift, seq_count) * group_width
    return pl.ds(pl.multiple_of(start, 16), group_width)


def dispatch_kernel(
    places_ref, tokens_ref, proj_ref, gain_ref, shift_ref,
    router_ref, route_col_ref, dest_row_ref, *refs, image_count, patch_rows, stride, seq_count,
):
    attended_refs = refs[:seq_count]
    middle_ref, gate_ref, stats_ref, *sent_refs = refs[seq_count:]
    rows, width = middle_ref.shape
    group_width = attended_refs[0].shape[-1]
    attn_out = jnp.zeros((rows, width), f32)
    for shift, attended_ref in enumerate(attended_refs):
        attn_out = attn_out + mm(
            attended_ref[...].reshape(rows, group_width),
            proj_ref[group_rows(places_ref, -shift, seq_count, group_width), :],
        )
    valid = valid_rows(places_ref, image_count, patch_rows, (rows, 1), 0).astype(f32)
    stats_ref[...] = total_at(attn_out * attn_out * valid, 0)
    middle = tokens_ref[...].reshape(rows, width).astype(f32) + attn_out
    middle_ref[...] = middle
    normed, _ = normalize(middle)
    moe_in = (normed * gain_ref[...] + shift_ref[...]).astype(bf16)
    logits = mm(moe_in, router_ref[...])
    exp_logits = jnp.exp(logits - jnp.max(logits, axis=-1, keepdims=True))
    gate = exp_logits / jnp.sum(exp_logits, axis=-1, keepdims=True)
    gate_ref[...] = gate
    expert_lane = lax.broadcasted_iota(jnp.int32, (1, EXPERTS), 1)
    pick_any = jnp.zeros((EXPERTS * stride, rows), bf16)
    slot_gate = jnp.zeros((EXPERTS * stride, 128), f32)
    for k in range(TOP):
        chosen = jnp.sum(
            jnp.where(expert_lane == route_col_ref[:, k : k + 1], gate, 0.0),
            axis=-1,
            keepdims=True,
        )
        pick = slot_picks(dest_row_ref, stride, k)
        pick_any = pick_any + pick
        for term in three_terms(jnp.broadcast_to(chosen, (rows, 128))):
            slot_gate = slot_gate + mm(pick, term)
    sent = mm(pick_any, moe_in).reshape(EXPERTS, stride, width)
    slot_gate = slot_gate[:, 0:1].reshape(EXPERTS, stride, 1)
    sent = with_scalars(sent, slot_gate, stride).astype(bf16)
    store_chunks(sent_refs, sent.reshape(EXPERTS * stride, width), stride)


def scaled_rows(rows_block, grads_block):
    groups, stride, width = rows_block.shape
    scale = row_scalars(rows_block, stride)
    return (grads_block.astype(f32) * scale).astype(bf16).reshape(groups * stride, width)


def expert_kernel(
    rows_ref, cotangent_ref, first_ref, second_ref, *refs, pieces,
):
    value_ref, back_ref, value_acc, grad_acc, scaled_ref = refs[-5:]
    count, _, stride, width = rows_ref.shape
    rows = count * stride
    piece = first_ref.shape[0] // pieces
    step = pl.program_id(1)

    @pl.when(step == 0)
    def _():
        scaled_ref[...] = scaled_rows(rows_ref[:, 0], cotangent_ref[:, 0])

    moe_rows = rows_ref[:, 0].reshape(rows, width)
    grad_rows = scaled_ref[...]
    value = jnp.zeros((rows, width), f32)
    grad = jnp.zeros((rows, width), f32)
    for at in range(pieces):
        first = first_ref[at * piece : (at + 1) * piece, :]
        second = second_ref[at * piece : (at + 1) * piece, :]
        hidden, slope = gelu_pair(mm_nt(moe_rows, first))
        grad_pre = (mm_nt(grad_rows, second) * slope).astype(bf16)
        value = value + mm(hidden.astype(bf16), second)
        grad = grad + mm(grad_pre, first)

    @pl.when(step == 0)
    def _():
        value_acc[...] = value
        grad_acc[...] = grad

    @pl.when(step > 0)
    def _():
        value_acc[...] += value
        grad_acc[...] += grad

    @pl.when(step == pl.num_programs(1) - 1)
    def _():
        value_low = value_acc[...].astype(bf16).reshape(count, stride, width)
        value_ref[:, 0] = value_low
        gate_grad = jnp.sum(
            cotangent_ref[:, 0].astype(f32) * value_low.astype(f32), axis=-1, keepdims=True
        )
        grad_low = grad_acc[...].reshape(count, stride, width)
        back_ref[:, 0] = with_scalars(grad_low, gate_grad, stride).astype(bf16)


def table_part(chunk_refs, part):
    split = chunk_refs[0].shape[0] * chunk_refs[0].shape[1] * len(chunk_refs) // EXPERTS
    pieces = []
    for chunk_ref in chunk_refs:
        sources, each, stride, width = chunk_ref.shape
        block = chunk_ref[...].reshape(sources // split, split, each, stride, width)
        pieces.append(block[:, part])
    table = pieces[0] if len(pieces) == 1 else jnp.concatenate(pieces, axis=1)
    return table.reshape(EXPERTS, table.shape[2], table.shape[3])


def combine_kernel(
    places_ref, middle_ref, gate_ref, cotangent_ref, proj_ref, gain_ref,
    shift_ref, router_ref, route_col_ref, dest_col_ref, stats_ref, *refs,
    image_count, patch_rows, stride, split, seq_count, chunks,
):
    attended_refs = refs[:seq_count]
    back_refs = refs[seq_count : seq_count + chunks]
    grad_middle_ref, router_grad_ref, small_ref = refs[seq_count + chunks :][:3]
    leaving_refs = refs[seq_count + chunks + 3 :]
    rows, width = middle_ref.shape
    group_width = attended_refs[0].shape[-1]
    slots = EXPERTS * stride
    middle = middle_ref[...]
    gate = gate_ref[...]
    valid = valid_rows(places_ref, image_count, patch_rows, (rows, 1), 0).astype(f32)
    grad_total = cotangent_ref[...].reshape(rows, width).astype(f32) * valid
    expert_lane = lax.broadcasted_iota(jnp.int32, (1, EXPERTS), 1)
    slot_lane = lax.broadcasted_iota(jnp.int32, (1, stride), 1)
    slot = lax.broadcasted_iota(jnp.int32, (1, slots), 1)
    pick_any = jnp.zeros((rows, slots), bf16)
    for k in range(TOP):
        pick_any = pick_any + (slot == dest_col_ref[:, k : k + 1]).astype(f32).astype(bf16)
    grad_dispatch = jnp.zeros((rows, width), f32)
    scalar_rows = [jnp.zeros((rows, stride), f32) for _ in range(TOP)]
    own = [
        (expert_lane == route_col_ref[:, k : k + 1]).astype(f32).astype(bf16) for k in range(TOP)
    ]
    for part in range(split):
        table = table_part(back_refs, part)
        grad_dispatch = grad_dispatch + mm(pick_any, table.reshape(slots, width))
        for at in range(stride - 3, stride):
            line = table[:, at, :stride]
            for k in range(TOP):
                scalar_rows[k] = scalar_rows[k] + mm(own[k], line)
    grad_probs = jnp.zeros((rows, EXPERTS), f32)
    for k in range(TOP):
        place = dest_col_ref[:, k : k + 1] - route_col_ref[:, k : k + 1] * stride
        grad_gate = jnp.sum(
            jnp.where(slot_lane == place, scalar_rows[k], 0.0), axis=-1, keepdims=True
        )
        grad_probs = grad_probs + own[k].astype(f32) * grad_gate
    grad_logits = (
        gate * (grad_probs - jnp.sum(grad_probs * gate, axis=-1, keepdims=True))
    ).astype(bf16)
    grad_moe_in = grad_dispatch + mm_nt(grad_logits, router_ref[...])
    normed, inv_root = normalize(middle)
    moe_in = (normed * gain_ref[...] + shift_ref[...]).astype(bf16)
    grad_middle = grad_total + norm_row_grad(grad_moe_in, normed, inv_root, gain_ref[...])
    grad_middle_ref[...] = grad_middle
    grad_attn = grad_middle.astype(bf16)
    for shift in range(seq_count):
        attended = attended_refs[shift][...].reshape(rows, group_width)
        own_rows = group_rows(places_ref, -shift, seq_count, group_width)
        _, strip, _ = leaving_refs[shift].shape
        grads = mm_nt(grad_attn, proj_ref[own_rows, :]).astype(bf16)
        leaving_refs[shift][: rows // strip] = grads.reshape(-1, strip, group_width)
        grads = mm_tn(grad_attn, attended).astype(bf16)
        leaving_refs[shift][rows // strip :] = grads.reshape(-1, strip, group_width)
    router_grad_ref[...] = mm_tn(grad_logits, moe_in)
    small_ref[0:1, :] = jnp.sum(grad_moe_in * normed, axis=0, keepdims=True)
    small_ref[1:2, :] = jnp.sum(grad_moe_in, axis=0, keepdims=True)
    lane = lax.broadcasted_iota(jnp.int32, (1, width), 1)
    count = jnp.sum(valid, axis=0, keepdims=True) * width
    small_ref[2:3, :] = stats_ref[...] + jnp.where(lane == 3, count, 0.0)


def total_at(values, place):
    lane = lax.broadcasted_iota(jnp.int32, (1, values.shape[-1]), 1)
    by_lane = jnp.sum(values, axis=0, keepdims=True)
    return jnp.where(lane == place, jnp.sum(by_lane, axis=1, keepdims=True), 0.0)


def output_kernel(
    places_ref, middle_ref, gate_ref, route_col_ref, dest_col_ref, *refs,
    image_count, patch_rows, stride, split,
):
    value_refs = refs[:-2]
    output_ref, stats_ref = refs[-2:]
    rows, width = middle_ref.shape
    slots = EXPERTS * stride
    gate = gate_ref[...]
    expert_lane = lax.broadcasted_iota(jnp.int32, (1, EXPERTS), 1)
    slot = lax.broadcasted_iota(jnp.int32, (1, slots), 1)
    moe_out = jnp.zeros((rows, width), f32)
    tables = [table_part(value_refs, part).reshape(slots, width) for part in range(split)]
    for k in range(TOP):
        pick = (slot == dest_col_ref[:, k : k + 1]).astype(f32).astype(bf16)
        pair_value = mm(pick, tables[0])
        for table in tables[1:]:
            pair_value = pair_value + mm(pick, table)
        own = expert_lane == route_col_ref[:, k : k + 1]
        moe_out = moe_out + jnp.sum(jnp.where(own, gate, 0.0), axis=-1, keepdims=True) * pair_value
    valid = valid_rows(places_ref, image_count, patch_rows, (rows, 1), 0).astype(f32)
    total = middle_ref[...] + moe_out
    output_ref[...] = (total * valid).astype(bf16).reshape(output_ref.shape)
    stats_ref[...] = total_at(moe_out * moe_out * valid, 1) + total_at(total * total * valid, 2)


def attention_grad_kernel(
    places_ref, q_ref, k_ref, v_ref, probs_ref, normed_ref, *refs,
    group_heads, head_width, seq_count,
):
    grad_refs = refs[:seq_count]
    packed_refs = refs[seq_count : 2 * seq_count]
    keep_ref, give_ref, weight_acc, grad_spread, packed_spread, halves = refs[2 * seq_count :]
    patch_rows = grad_spread.shape[1]
    strips = patch_rows // grad_refs[0].shape[1]
    image_strips = pl.ds(pl.program_id(0) * strips, strips)
    total_rows = q_ref.shape[1]
    group_width = group_heads * head_width
    scale = head_width ** (-0.5)
    for shift, grad_ref in enumerate(grad_refs):
        grad_spread[neighbour(places_ref, shift, seq_count)] = grad_ref[image_strips].reshape(
            patch_rows, group_width
        )
    grad_heads = grad_spread[...].reshape(total_rows, group_width)
    q, k, v = q_ref[0], k_ref[0], v_ref[0]
    lane = lax.broadcasted_iota(jnp.int32, (1, group_width), 1)
    nothing = jnp.zeros_like(q)
    grad_q = jnp.zeros((total_rows, group_width), f32)
    grad_k = jnp.zeros((total_rows, group_width), f32)
    grad_v = jnp.zeros((total_rows, group_width), f32)
    for head in range(group_heads):
        in_head = (lane >= head * head_width) & (lane < (head + 1) * head_width)
        own_grad = jnp.where(in_head, grad_heads, nothing)
        probs_low = probs_ref[0, head]
        probs = probs_low.astype(f32)
        grad_probs = mm_nt(own_grad, v)
        delta = jnp.sum(probs * grad_probs, axis=-1, keepdims=True)
        grad_scores = (probs * (grad_probs - delta)).astype(bf16)
        grad_q = jnp.where(in_head, mm(grad_scores, k), grad_q)
        grad_k = jnp.where(in_head, mm_tn(grad_scores, q), grad_k)
        grad_v = jnp.where(in_head, mm_tn(probs_low, grad_heads), grad_v)
    packed = jnp.concatenate([grad_q * scale, grad_k * scale, grad_v], axis=1).astype(bf16)
    packed_spread[...] = packed.reshape(packed_spread.shape)
    for shift, packed_ref in enumerate(packed_refs):
        packed_ref[0] = packed_spread[neighbour(places_ref, shift, seq_count)]
    weight_grad = mm_tn(packed, normed_ref[0])

    @pl.when(pl.program_id(0) == 0)
    def _():
        weight_acc[...] = weight_grad

    @pl.when(pl.program_id(0) > 0)
    def _():
        weight_acc[...] += weight_grad

    @pl.when(pl.program_id(0) == pl.num_programs(0) - 1)
    def _():
        width = weight_acc.shape[1]
        count, strip, _ = grad_refs[0].shape
        proj_strips = slice(count - width // strip, count)
        proj_grad = grad_refs[0][proj_strips].astype(f32)
        for grad_ref in grad_refs[1:]:
            proj_grad = proj_grad + grad_ref[proj_strips].astype(f32)
        proj_grad = proj_grad.reshape(width, group_width)
        half = halves.shape[1]
        slab = jnp.concatenate([weight_acc[...], proj_grad.T], axis=0).astype(bf16)
        halves[0] = slab[:half]
        halves[1] = slab[half:]
        keep_ref[...] = halves[places_ref[2]]
        give_ref[...] = halves[1 - places_ref[2]]


def reduce_kernel(parts_ref, copies_ref):
    total = parts_ref[0].astype(f32)
    for at in range(1, parts_ref.shape[0]):
        total = total + parts_ref[at].astype(f32)
    copies_ref[...] = jnp.broadcast_to(total.astype(bf16)[None], copies_ref.shape)


def assemble_kernel(places_ref, *refs, seq_count):
    own_refs = refs[:seq_count]
    other_refs = refs[seq_count : 2 * seq_count]
    qkv_ref, proj_ref, slabs = refs[2 * seq_count :]
    width = proj_ref.shape[0]
    group_width = width // seq_count
    half = own_refs[0].shape[0]
    for shift in range(seq_count):
        group = neighbour(places_ref, -shift, seq_count)
        for places, source_ref in (
            (places_ref[2], own_refs[shift]), (1 - places_ref[2], other_refs[shift]),
        ):
            start = pl.multiple_of(places * half, 16)
            slabs[group, pl.ds(start, half), :] = source_ref[...]
    for part in range(4):
        values = slabs[:, part * group_width : (part + 1) * group_width, :]
        values = values.reshape(width, width).astype(f32)
        if part < 3:
            qkv_ref[:, part * width : (part + 1) * width] = values.T
        else:
            proj_ref[...] = values


def input_grad_kernel(
    places_ref, weight_ref, tokens_ref, grad_middle_ref, gain_ref, before_ref, stats_ref,
    router_ref, *refs,
):
    *packed_refs, input_grad_ref, small_ref = refs
    _, patch_rows, width = tokens_ref.shape
    grad = jnp.zeros((patch_rows, width), f32)
    for shift, packed_ref in enumerate(packed_refs):
        group = neighbour(places_ref, -shift, len(packed_refs))
        grad = grad + mm(packed_ref[0], weight_ref[group])
    normed, inv_root = normalize(tokens_ref[0].astype(f32))
    row_grad = norm_row_grad(grad, normed, inv_root, gain_ref[...])
    input_grad_ref[0] = (grad_middle_ref[0] + row_grad).astype(bf16)

    @pl.when(pl.program_id(0) == 0)
    def _():
        small_ref[0:2, :] = before_ref[0:2, :]
        small_ref[2:3, :] = before_ref[2:3, :] + stats_ref[...]
        small_ref[3:5, :] = jnp.zeros((2, width), f32)
        small_ref[5:8, :] = jnp.zeros((3, width), f32)
        small_ref[5:6, : router_ref.shape[-1]] = jnp.sum(router_ref[...], axis=0)

    small_ref[3:4, :] += jnp.sum(grad * normed, axis=0, keepdims=True)
    small_ref[4:5, :] += jnp.sum(grad, axis=0, keepdims=True)


def expert_grad_kernel(*refs, row_pieces, row_blocks):
    rows_ref, cotangent_ref, first_ref, second_ref = refs[:4]
    first_grad_ref, second_grad_ref, done_ref, grad_pre_ref, hidden_ref, scaled_ref = refs[-6:]
    stride, width = rows_ref.shape[-2:]
    rows = grad_pre_ref.shape[1]

    def scale():
        share = rows // rows_ref.shape[0]
        for place in range(rows_ref.shape[0]):
            own = slice(place * share, (place + 1) * share)
            scaled_ref[own, :] = scaled_rows(rows_ref[place, :, 0], cotangent_ref[place, :, 0])

    if row_blocks == 1:
        pl.when(pl.program_id(0) == 0)(scale)
    else:
        scale()
    moe_rows = rows_ref[...].reshape(rows, width)
    piece = rows // row_pieces
    first = first_ref[...]
    second = second_ref[...]
    for at in range(row_pieces):
        own = slice(at * piece, (at + 1) * piece)
        hidden, slope = gelu_pair(mm_nt(first, moe_rows[own]))
        hidden_ref[:, own] = hidden.astype(bf16)
        grad_pre_ref[:, own] = (mm_nt(second, scaled_ref[own, :]) * slope).astype(bf16)
    if row_blocks > 1:

        @pl.when(pl.program_id(1) == 0)
        def _():
            second_grad_ref[...] = jnp.zeros(second_grad_ref.shape, f32)
            first_grad_ref[...] = jnp.zeros(first_grad_ref.shape, f32)

        second_grad_ref[...] += mm(hidden_ref[...], scaled_ref[...])
        first_grad_ref[...] += mm(grad_pre_ref[...], moe_rows)
    else:
        second_grad_ref[...] = mm(hidden_ref[...], scaled_ref[...])
        first_grad_ref[...] = mm(grad_pre_ref[...], moe_rows)
    done_ref[...] = jnp.zeros(done_ref.shape, f32)


smem = pl.BlockSpec(memory_space=pltpu.SMEM)
vmem = pl.BlockSpec(memory_space=pltpu.VMEM)
params = pltpu.CompilerParams(vmem_limit_bytes=60 * 1024 * 1024)


def cost(microseconds):
    return pl.CostEstimate(
        flops=int(microseconds * 6e8), transcendentals=0, bytes_accessed=int(microseconds * 1e5)
    )


def struct(shape, dtype):
    return jax.ShapeDtypeStruct(shape, dtype)


def per_device(
    tokens, routes, priority, hires, gain_one, shift_one, w_qkv, w_proj, gain_two, shift_two,
    w_router, expert_in, expert_out, cotangent,
):
    image_count, patch_rows, width = tokens.shape
    rows = image_count * patch_rows
    seq_count = lax.axis_size("seq")
    ep_count = lax.axis_size("ep")
    full_rows = patch_rows * seq_count
    head_width = width // HEADS
    group_heads = HEADS // seq_count
    group_width = group_heads * head_width
    local_experts = max(1, EXPERTS // ep_count)
    split = max(1, ep_count // EXPERTS)
    local_hidden = expert_in.shape[0] // local_experts
    capacity = max(2, (105 * TOP * rows + 100 * EXPERTS - 1) // (100 * EXPERTS))
    stride = (capacity + 3 + 15) // 16 * 16
    chunks = 2 if local_experts % 2 == 0 else 1
    each = local_experts // chunks
    seq_place = lax.axis_index("seq")
    ep_place = lax.axis_index("ep")
    places = jnp.stack([hires[0], seq_place.astype(jnp.int32), (ep_place % 2).astype(jnp.int32)])
    gain_one, shift_one, gain_two, shift_two = (
        vector.reshape(1, width) for vector in (gain_one, shift_one, gain_two, shift_two)
    )
    common = dict(image_count=image_count, patch_rows=patch_rows, stride=stride)

    def exchange(values, axis):
        return lax.all_to_all(values, axis, split_axis=0, concat_axis=0, tiled=True)

    def send_slots(chunk):
        if split > 1:
            chunk = jnp.broadcast_to(chunk[:, None], (EXPERTS, split) + chunk.shape[1:])
            chunk = chunk.reshape((ep_count,) + chunk.shape[2:])
        return exchange(chunk, "ep")

    def move(values, axis, shift):
        count = lax.axis_size(axis)
        if shift % count == 0:
            return values
        return lax.ppermute(values, axis, [(at, (at + shift) % count) for at in range(count)])

    def other_core(values):
        return lax.ppermute(values, "ep", [(at, at ^ 1) for at in range(ep_count)])

    def hold(values, *others):
        values = tuple(values)
        anywhere = pl.BlockSpec(memory_space=pl.ANY)
        return call(
            lambda *refs: None,
            "hold",
            waits=others,
            in_specs=[anywhere] * len(values),
            out_specs=[anywhere] * len(values),
            out_shape=[struct(value.shape, value.dtype) for value in values],
            input_output_aliases={at: at for at in range(len(values))},
            cost_estimate=cost(1),
        )(*values)

    def over_seq(values):
        return lax.all_gather(values, "seq", axis=0, tiled=False)

    def call(kernel, name, waits=(), **spec):
        waits = tuple(waits)

        def run(*operands):
            count = len(operands)

            def body(*refs):
                kernel(*refs[:count], *refs[count + len(waits) :])

            unread = [pl.BlockSpec(memory_space=pl.ANY)] * len(waits)
            if "grid_spec" in spec:
                grid_spec = dict(spec["grid_spec"])
                grid_spec["in_specs"] = grid_spec["in_specs"] + unread
                own = dict(spec, grid_spec=pltpu.PrefetchScalarGridSpec(**grid_spec))
            else:
                own = dict(spec, in_specs=spec["in_specs"] + unread)
            return pl.pallas_call(body, name=name, compiler_params=params, **own)(
                *operands, *waits
            )

        return run

    def slot_struct(experts):
        return struct((min(ep_count, EXPERTS), experts, stride, width), bf16)

    chunk_struct = slot_struct(each)
    moved_struct = struct((ep_count, each, stride, width), bf16)

    tokens_all = over_seq(tokens)
    pairs = jnp.concatenate([routes.reshape(rows, TOP).T, priority.reshape(1, rows)], axis=0)
    route_col, dest_col, dest_row = call(
        lambda *refs: routing_kernel(*refs, capacity=capacity, **common),
        "routing",
        in_specs=[smem, vmem],
        out_specs=[vmem] * 3,
        out_shape=[
            struct((rows, TOP), jnp.int32),
            struct((rows, TOP), jnp.int32),
            struct((TOP, rows), jnp.int32),
        ],
        cost_estimate=cost(3),
    )(places, pairs)
    (cotangent_sent,) = call(
        lambda *refs: send_grads_kernel(*refs, stride=stride),
        "send_grads",
        in_specs=[vmem] * 2,
        out_specs=[vmem],
        out_shape=[slot_struct(local_experts)],
        cost_estimate=cost(3),
    )(cotangent, dest_row)
    cotangent_slots = send_slots(cotangent_sent)
    weight_groups = (
        w_qkv.reshape(width, 3, seq_count, group_width)
        .transpose(2, 1, 3, 0)
        .reshape(seq_count, 3 * group_width, width)
    )

    row_block = pl.BlockSpec((1, full_rows, group_width), lambda i, *_: (i, 0, 0))
    probs_block = pl.BlockSpec((1, group_heads, full_rows, full_rows), lambda i, *_: (i, 0, 0, 0))
    normed_block = pl.BlockSpec((1, full_rows, width), lambda i, *_: (i, 0, 0))
    spread_block = pl.BlockSpec((1, patch_rows, group_width), lambda i, *_: (i, 0, 0))
    packed_block = pl.BlockSpec((1, patch_rows, 3 * group_width), lambda i, *_: (i, 0, 0))
    vector_block = pl.BlockSpec((1, width), lambda i, *_: (0, 0))
    image_block = pl.BlockSpec((1, patch_rows, width), lambda i, *_: (i, 0, 0))
    spread_struct = struct((image_count, patch_rows, group_width), bf16)
    row_struct = struct((image_count, full_rows, group_width), bf16)
    *attended, q, k, v, probs, attn_in = call(
        lambda *refs: attention_kernel(*refs, group_heads=group_heads, head_width=head_width),
        "attention",
        waits=[cotangent_sent],
        grid_spec=dict(
            num_scalar_prefetch=1,
            grid=(image_count,),
            in_specs=[
                pl.BlockSpec((seq_count, 1, patch_rows, width), lambda i, *_: (0, i, 0, 0)),
                vector_block,
                vector_block,
                pl.BlockSpec((1, 3 * group_width, width), lambda i, at: (at[1], 0, 0)),
            ],
            out_specs=[spread_block] * seq_count
            + [row_block, row_block, row_block, probs_block, normed_block],
            scratch_shapes=[pltpu.VMEM((seq_count, patch_rows, group_width), bf16)],
        ),
        out_shape=[spread_struct] * seq_count
        + [
            row_struct,
            row_struct,
            row_struct,
            struct((image_count, group_heads, full_rows, full_rows), bf16),
            struct((image_count, full_rows, width), bf16),
        ],
        cost_estimate=cost(16),
    )(places, tokens_all, gain_one, shift_one, weight_groups)
    (cotangent_slots,) = hold([cotangent_slots], attended[0])
    attended = [move(block, "seq", shift) for shift, block in enumerate(attended)]

    middle, gate, stats, *rows_sent = call(
        lambda *refs: dispatch_kernel(*refs, seq_count=seq_count, **common),
        "dispatch",
        waits=[cotangent_slots],
        in_specs=[smem] + [vmem] * (7 + seq_count),
        out_specs=[vmem] * (3 + chunks),
        out_shape=[
            struct((rows, width), f32),
            struct((rows, EXPERTS), f32),
            struct((1, width), f32),
        ]
        + [chunk_struct] * chunks,
        cost_estimate=cost(9),
    )(
        places, tokens, w_proj, gain_two, shift_two, w_router, route_col, dest_row, *attended,
    )
    row_slots = [send_slots(chunk) for chunk in rows_sent]

    hidden_tile = local_hidden // 2
    tiles = local_hidden // hidden_tile
    moved_block = pl.BlockSpec((ep_count, 1, stride, width), lambda e, f: (0, e, 0, 0))
    cotangent_all = over_seq(cotangent_slots)
    grads_back, values_back = [], ()
    for at in range(chunks):
        weight_block = pl.BlockSpec(
            (hidden_tile, width), lambda e, f, at=at: ((e + at * each) * tiles + f, 0)
        )
        all_block = pl.BlockSpec(
            (ep_count, 1, stride, width), lambda e, f, at=at: (0, e + at * each, 0, 0)
        )
        value, back = call(
            lambda *refs: expert_kernel(*refs, pieces=max(1, hidden_tile // 512)),
            "experts",
            waits=[cotangent_all] * (at > 0),
            grid=(each, tiles),
            in_specs=[moved_block, all_block, weight_block, weight_block]
            + [pl.BlockSpec(memory_space=pl.ANY)] * len(values_back),
            out_specs=[all_block, moved_block],
            out_shape=[struct((ep_count, local_experts, stride, width), bf16), moved_struct],
            scratch_shapes=[pltpu.VMEM((ep_count * stride, width), f32)] * 2
            + [pltpu.VMEM((ep_count * stride, width), bf16)],
            input_output_aliases={4: 0} if values_back else {},
            cost_estimate=cost(16),
        )(row_slots[at], cotangent_slots, expert_in, expert_out, *values_back)
        grads_back.append(exchange(back, "ep"))
        values_back = (value,)

    all_rows = seq_count * ep_count * stride
    grad_tile = min(768, local_hidden)
    grad_tiles = local_hidden // grad_tile
    anywhere = pl.BlockSpec(memory_space=pl.ANY)
    rows_all = [over_seq(slots) for slots in row_slots]
    grads = []

    row_blocks = max(1, all_rows // 1024)
    sources = ep_count // row_blocks
    block_rows = all_rows // row_blocks

    def expert_grads(expert, begin, count, *others):
        place = expert * grad_tiles + begin
        tile_block = pl.BlockSpec((grad_tile, width), lambda f, r: (place + f, 0))

        def source_block(own):
            return pl.BlockSpec(
                (seq_count, sources, 1, stride, width),
                lambda f, r: (0, r, own, 0, 0),
                pipeline_mode=pl.Buffered(1 if row_blocks == 1 else 2),
            )

        *grads[:], done = call(
            lambda *refs: expert_grad_kernel(
                *refs, row_pieces=max(1, block_rows // 512), row_blocks=row_blocks
            ),
            "expert_grads",
            waits=others,
            grid=(count, row_blocks),
            in_specs=[source_block(expert % each), source_block(expert), tile_block, tile_block]
            + [anywhere] * len(grads),
            out_specs=[tile_block, tile_block, pl.BlockSpec((8, 128), lambda f, r: (0, 0))],
            out_shape=[
                struct(expert_in.shape, f32),
                struct(expert_out.shape, f32),
                struct((8, 128), f32),
            ],
            scratch_shapes=[pltpu.VMEM((grad_tile, block_rows), bf16)] * 2
            + [pltpu.VMEM((block_rows, width), bf16)],
            input_output_aliases={4: 0, 5: 1} if grads else {},
            cost_estimate=cost(7 * count),
        )(rows_all[expert // each], cotangent_all, expert_in, expert_out, *grads)
        return done

    work = [(expert, 0, grad_tiles) for expert in range(local_experts - 1)]
    last = local_experts - 1
    work += [(last, 0, grad_tiles // 2), (last, grad_tiles // 2, grad_tiles - grad_tiles // 2)]
    work = iter(work)

    def next_grads(*others):
        return [expert_grads(*part, *others) for part in itertools.islice(work, 1)]

    early = next_grads(values_back[0], grads_back[0]) if local_experts > 3 else []
    leaving_shape = ((rows + width) // 48, 48, group_width)
    grad_middle, router_grad, small, *leaving = call(
        lambda *refs: combine_kernel(
            *refs, split=split, seq_count=seq_count, chunks=chunks, **common
        ),
        "combine",
        waits=early,
        in_specs=[smem] + [vmem] * (10 + seq_count + chunks),
        out_specs=[vmem] * (3 + seq_count),
        out_shape=[
            struct((rows, width), f32),
            struct((EXPERTS, width), f32),
            struct((3, width), f32),
        ]
        + [struct(leaving_shape, bf16)] * seq_count,
        cost_estimate=cost(10),
    )(
        places, middle, gate, cotangent, w_proj, gain_two, shift_two, w_router,
        route_col, dest_col, stats, *attended, *grads_back,
    )
    devices = seq_count * ep_count
    leaving = [move(block, "seq", -at) for at, block in enumerate(leaving)]
    piece = EXPERTS * width // devices
    router_grad = exchange(router_grad.reshape(devices, 1, piece), ("seq", "ep"))
    values_moved = exchange(values_back[0], "ep")
    middle_done = next_grads(grad_middle) if local_experts > 2 else []
    half = 2 * group_width
    *packed_sent, keep, give = call(
        lambda *refs: attention_grad_kernel(
            *refs, group_heads=group_heads, head_width=head_width, seq_count=seq_count
        ),
        "attention_grad",
        waits=middle_done,
        grid=(image_count,),
        in_specs=[smem, row_block, row_block, row_block, probs_block, normed_block]
        + [pl.BlockSpec(leaving_shape, lambda i: (0, 0, 0))] * seq_count,
        out_specs=[packed_block] * seq_count
        + [pl.BlockSpec((half, width), lambda i: (0, 0))] * 2,
        out_shape=[struct((image_count, patch_rows, 3 * group_width), bf16)] * seq_count
        + [struct((half, width), bf16)] * 2,
        scratch_shapes=[
            pltpu.VMEM((3 * group_width, width), f32),
            pltpu.VMEM((seq_count, patch_rows, group_width), bf16),
            pltpu.VMEM((seq_count, patch_rows, 3 * group_width), bf16),
            pltpu.VMEM((2, half, width), bf16),
        ],
        cost_estimate=cost(18),
    )(places, q, k, v, probs, attn_in, *leaving)
    packed = [move(block, "seq", shift) for shift, block in enumerate(packed_sent)]

    pairs_along = ep_count // 2
    same_core = [[2 * at + core for at in range(pairs_along)] for core in range(2)]

    def along_core(values):
        return lax.all_to_all(
            values, "ep", split_axis=0, concat_axis=0, tiled=True, axis_index_groups=same_core
        )

    slab = (keep.astype(f32) + other_core(give).astype(f32)).astype(bf16)
    slab_struct = struct((pairs_along, half // pairs_along, width), bf16)
    slab = along_core(slab.reshape(slab_struct.shape))
    late = next_grads(packed_sent[0]) if local_experts > 1 else []
    slab = call(
        reduce_kernel,
        "reduce_slab",
        waits=late + [values_moved] + packed[1:],
        in_specs=[vmem],
        out_specs=vmem,
        out_shape=slab_struct,
        cost_estimate=cost(1),
    )(slab)
    slab_moved = along_core(slab).reshape(half, width)
    output, value_stats = call(
        lambda *refs: output_kernel(*refs, split=split, **common),
        "output",
        waits=next_grads(slab) + [slab_moved],
        in_specs=[smem] + [vmem] * 5,
        out_specs=[vmem] * 2,
        out_shape=[struct((image_count, patch_rows, width), bf16), struct((1, width), f32)],
        cost_estimate=cost(5),
    )(places, middle, gate, route_col, dest_col, values_moved)
    own_slabs = [move(slab_moved, "seq", shift) for shift in range(seq_count)]
    input_grad, small = call(
        input_grad_kernel,
        "input_grad",
        grid=(image_count,),
        in_specs=[
            smem,
            pl.BlockSpec((seq_count, 3 * group_width, width), lambda i: (0, 0, 0)),
            image_block,
            image_block,
            vector_block,
            pl.BlockSpec((3, width), lambda i: (0, 0)),
            pl.BlockSpec((1, width), lambda i: (0, 0)),
            pl.BlockSpec((devices, 1, piece), lambda i: (0, 0, 0)),
        ]
        + [packed_block] * seq_count,
        out_specs=[image_block, pl.BlockSpec((8, width), lambda i: (0, 0))],
        out_shape=[struct((image_count, patch_rows, width), bf16), struct((8, width), f32)],
        cost_estimate=cost(7),
    )(
        places, weight_groups, tokens, grad_middle.reshape(image_count, patch_rows, width),
        gain_one, small, value_stats, router_grad, *packed,
    )
    own_slabs = hold(own_slabs, *next_grads(input_grad))
    other_slabs = [other_core(each_slab) for each_slab in own_slabs]
    qkv_grad, proj_grad = call(
        lambda *refs: assemble_kernel(*refs, seq_count=seq_count),
        "assemble",
        in_specs=[smem] + [vmem] * (2 * seq_count),
        out_specs=[vmem] * 2,
        out_shape=[struct((width, 3 * width), f32), struct((width, width), f32)],
        scratch_shapes=[pltpu.VMEM((seq_count, 2 * half, width), bf16)],
        cost_estimate=cost(8),
    )(places, *own_slabs, *other_slabs)

    copies = jnp.broadcast_to(small[None], (devices, 8, width))
    copies = exchange(copies, ("seq", "ep"))
    sums = jnp.sum(copies[:, :5], axis=0)
    router_grad = copies[:, 5, :piece].reshape(EXPERTS, width).T
    return (
        output,
        input_grad,
        sums[3],
        sums[4],
        qkv_grad,
        proj_grad,
        sums[0],
        sums[1],
        router_grad,
        grads[0],
        grads[1],
        jnp.sqrt(sums[2, :3] / sums[2, 3]),
    )


def solution(mesh):
    in_specs = (
        P("ep", "seq", None),
        P("ep", "seq", None),
        P("ep", "seq"),
        P("ep"),
        P(),
        P(),
        P(),
        P(),
        P(),
        P(),
        P(),
        P("ep", None),
        P("ep", None),
        P("ep", "seq", None),
    )
    out_specs = (
        P("ep", "seq", None),
        P("ep", "seq", None),
        P(),
        P(),
        P(),
        P(),
        P(),
        P(),
        P(),
        P("ep", None),
        P("ep", None),
        P(),
    )
    return jax.shard_map(
        per_device, mesh=mesh, in_specs=in_specs, out_specs=out_specs, check_vma=False
    )
```

```python
import itertools

import jax
import jax.numpy as jnp
from jax import lax
from jax.experimental import pallas as pl
from jax.experimental.pallas import tpu as pltpu
from jax.sharding import PartitionSpec as P

HEADS = 12
EXPERTS = 32
TOP = 2
PATCHES = 576
SHORT = 196

norm_eps = 1e-06
neg_big = -1e30
f32 = jnp.float32
bf16 = jnp.bfloat16

tail_slope = 0.33
tail_terms = (
    0.18635779800457905,
    0.18295602991113566,
    0.2012232872944192,
    0.04722279904104141,
    0.40849559831839843,
    -0.3511445702318978,
    0.46023391759858995,
    -0.13534486747679436,
)


def mm(a, b):
    return lax.dot_general(a, b, (((1,), (0,)), ((), ())), preferred_element_type=f32)


def mm_nt(a, b):
    return lax.dot_general(a, b, (((1,), (1,)), ((), ())), preferred_element_type=f32)


def mm_tn(a, b):
    return lax.dot_general(a, b, (((0,), (0,)), ((), ())), preferred_element_type=f32)


def gelu_pair(v):
    size = jnp.abs(v)
    bell = jnp.exp(v * v * -0.5)
    t = 1.0 / (1.0 + size * (tail_slope * 0.7071067811865476))
    poly = tail_terms[-1] * 0.5
    for term in tail_terms[-2::-1]:
        poly = poly * t + term * 0.5
    tail = poly * t * bell
    cdf = jnp.where(v >= 0.0, 1.0 - tail, tail)
    return v * cdf, cdf + v * bell * 0.3989422804014327


def normalize(values):
    centred = values - jnp.mean(values, axis=-1, keepdims=True)
    inv_root = lax.rsqrt(jnp.mean(centred * centred, axis=-1, keepdims=True) + norm_eps)
    return centred * inv_root, inv_root


def norm_row_grad(upstream, normed, inv_root, gain):
    scaled = upstream * gain
    return inv_root * (
        scaled
        - jnp.mean(scaled, axis=-1, keepdims=True)
        - normed * jnp.mean(scaled * normed, axis=-1, keepdims=True)
    )


def valid_rows(places_ref, image_count, patch_rows, shape, axis):
    row = lax.broadcasted_iota(jnp.int32, shape, axis)
    first_patch = places_ref[1] * patch_rows
    valid = row < 0
    for image in range(image_count):
        length = jnp.where(image < places_ref[0], PATCHES, SHORT)
        start = image * patch_rows
        stop = start + jnp.clip(length - first_patch, 0, patch_rows)
        valid = valid | ((row >= start) & (row < stop))
    return valid


def routing_kernel(
    places_ref, pairs_ref, route_col_ref, dest_col_ref, dest_row_ref,
    *, image_count, patch_rows, capacity, stride,
):
    rows = pairs_ref.shape[1]
    eye = lax.broadcasted_iota(jnp.int32, (rows, rows), 0) == lax.broadcasted_iota(
        jnp.int32, (rows, rows), 1
    )

    def as_column(line):
        return jnp.sum(jnp.where(eye, line.astype(f32), 0.0), axis=1, keepdims=True).astype(
            jnp.int32
        )

    e_row = [pairs_ref[k : k + 1, :] for k in range(TOP)]
    e_col = [as_column(line) for line in e_row]
    prio_row = pairs_ref[TOP : TOP + 1, :]
    prio_col = as_column(prio_row)
    for k in range(TOP):
        route_col_ref[:, k : k + 1] = e_col[k]
    valid_col = valid_rows(places_ref, image_count, patch_rows, (rows, 1), 0)
    valid_row = valid_rows(places_ref, image_count, patch_rows, (1, rows), 1)
    weight_col = valid_col.astype(f32)
    weight_row = valid_row.astype(f32)
    row_first = (prio_row < prio_col).astype(f32) * weight_row
    col_first = (prio_col < prio_row).astype(f32) * weight_col
    for k in range(TOP):
        count = jnp.where(e_col[k] == e_row[k], row_first, 0.0)
        for earlier in range(k):
            count = count + jnp.where(e_col[k] == e_row[earlier], weight_row, 0.0)
        slot = jnp.sum(count, axis=1, keepdims=True).astype(jnp.int32)
        keep = valid_col & (slot < capacity)
        dest_col_ref[:, k : k + 1] = jnp.where(keep, e_col[k] * stride + slot, -1)
        count = jnp.where(e_col[k] == e_row[k], col_first, 0.0)
        for earlier in range(k):
            count = count + jnp.where(e_col[earlier] == e_row[k], weight_col, 0.0)
        slot = jnp.sum(count, axis=0, keepdims=True).astype(jnp.int32)
        keep = valid_row & (slot < capacity)
        dest_row_ref[k : k + 1, :] = jnp.where(keep, e_row[k] * stride + slot, -1)


def side_by_side(values):
    half = values.shape[0] // 2
    return jnp.concatenate([values[:half], values[half:]], axis=1)


def stacked(values):
    width = values.shape[1] // 2
    return jnp.concatenate([values[:, :width], values[:, width:]], axis=0)


def neighbour(places_ref, shift, seq_count):
    return (places_ref[1] + (shift + seq_count)) % seq_count


def attention_kernel(
    places_ref, gain_ref, shift_ref, weight_ref, *refs,
    seq_count, group_heads, head_width,
):
    tokens_refs = refs[:seq_count]
    attended_refs = refs[seq_count : 2 * seq_count]
    q_ref, k_ref, v_ref, probs_ref, normed_ref, spread_ref, tokens_ref = refs[2 * seq_count :]
    _, patch_rows, width = tokens_refs[0].shape
    for shift, source_ref in enumerate(tokens_refs):
        tokens_ref[neighbour(places_ref, -shift, seq_count)] = source_ref[0]
    total_rows = seq_count * patch_rows
    group_width = group_heads * head_width
    values = tokens_ref[...].reshape(total_rows, width).astype(f32)
    normed, _ = normalize(values)
    attn_in = (normed * gain_ref[...] + shift_ref[...]).astype(bf16)
    normed_ref[0] = attn_in
    q, k, v = (
        mm_nt(attn_in, weight_ref[0, part * group_width : (part + 1) * group_width, :]).astype(bf16)
        for part in range(3)
    )
    q_ref[0] = q
    k_ref[0] = k
    v_ref[0] = v
    length = jnp.where(pl.program_id(0) < places_ref[0], PATCHES, SHORT)
    key_valid = lax.broadcasted_iota(jnp.int32, (1, total_rows), 1) < length
    lane = lax.broadcasted_iota(jnp.int32, (1, group_width), 1)
    scaled_q = (q.astype(f32) * head_width ** (-0.5)).astype(bf16)
    attended = jnp.zeros((total_rows, group_width), f32)
    for head in range(group_heads):
        in_head = (lane >= head * head_width) & (lane < (head + 1) * head_width)
        scores = mm_nt(jnp.where(in_head, scaled_q, jnp.zeros_like(scaled_q)), k)
        scores = jnp.where(key_valid, scores, neg_big)
        exp_scores = jnp.exp(scores - jnp.max(scores, axis=-1, keepdims=True))
        inverse = 1.0 / jnp.sum(exp_scores, axis=-1, keepdims=True)
        probs = (exp_scores * inverse).astype(bf16)
        probs_ref[0, head] = probs
        attended = jnp.where(in_head, mm(probs, v), attended)
    spread_ref[...] = attended.astype(bf16).reshape(spread_ref.shape)
    for shift, attended_ref in enumerate(attended_refs):
        attended_ref[0] = side_by_side(spread_ref[neighbour(places_ref, shift, seq_count)])


def slot_picks(dest_row_ref, stride, k):
    slot = lax.broadcasted_iota(jnp.int32, (EXPERTS * stride, 1), 0)
    return (slot == dest_row_ref[k : k + 1, :]).astype(f32).astype(bf16)


def send_grads_kernel(cotangent_ref, dest_row_ref, *sent_refs, stride):
    width = cotangent_ref.shape[-1]
    cotangent = cotangent_ref[...].reshape(-1, width)
    pick = slot_picks(dest_row_ref, stride, 0)
    for k in range(1, TOP):
        pick = pick + slot_picks(dest_row_ref, stride, k)
    sent = mm(pick, cotangent).astype(bf16)
    store_chunks(sent_refs, sent, stride)


def store_chunks(chunk_refs, table, stride):
    width = table.shape[-1]
    targets, each = chunk_refs[0].shape[:2]
    grouped = table.reshape(targets, len(chunk_refs) * each, stride, width)
    for at, chunk_ref in enumerate(chunk_refs):
        chunk_ref[...] = grouped[:, at * each : (at + 1) * each]


def three_terms(values):
    high = values.astype(bf16)
    rest = values - high.astype(f32)
    middle = rest.astype(bf16)
    return high, middle, (rest - middle.astype(f32)).astype(bf16)


def diagonal(stride):
    row = lax.broadcasted_iota(jnp.int32, (1, stride, stride), 1)
    return row == lax.broadcasted_iota(jnp.int32, (1, stride, stride), 2)


def row_scalars(block, stride):
    spare = block[:, stride - 3 : stride, :stride].astype(f32)
    line = spare[:, 0:1] + spare[:, 1:2] + spare[:, 2:3]
    return jnp.sum(jnp.where(diagonal(stride), line, 0.0), axis=2, keepdims=True)


def with_scalars(block, column, stride):
    width = block.shape[-1]
    line = jnp.sum(jnp.where(diagonal(stride), column, 0.0), axis=1, keepdims=True)
    line = jnp.concatenate(
        [line, jnp.zeros((line.shape[0], 1, width - stride), f32)], axis=2
    )
    row = lax.broadcasted_iota(jnp.int32, (1, stride, 1), 1)
    for at, term in enumerate(three_terms(line)):
        block = jnp.where(row == stride - 3 + at, term.astype(f32), block)
    return block


def unpacked(blocks_ref):
    return jnp.concatenate([stacked(blocks_ref[at]) for at in range(blocks_ref.shape[0])], axis=0)


def group_rows(places_ref, shift, seq_count, group_width):
    start = neighbour(places_ref, shift, seq_count) * group_width
    return pl.ds(pl.multiple_of(start, 16), group_width)


def dispatch_kernel(
    places_ref, tokens_ref, proj_ref, gain_ref, shift_ref,
    router_ref, route_col_ref, dest_row_ref, *refs, image_count, patch_rows, stride, seq_count,
):
    attended_refs = refs[:seq_count]
    middle_ref, gate_ref, stats_ref, *sent_refs = refs[seq_count:]
    rows, width = middle_ref.shape
    group_width = attended_refs[0].shape[-1] // 2
    attn_out = jnp.zeros((rows, width), f32)
    for shift, attended_ref in enumerate(attended_refs):
        attn_out = attn_out + mm(
            unpacked(attended_ref),
            proj_ref[group_rows(places_ref, -shift, seq_count, group_width), :],
        )
    valid = valid_rows(places_ref, image_count, patch_rows, (rows, 1), 0).astype(f32)
    stats_ref[...] = total_at(attn_out * attn_out * valid, 0)
    middle = tokens_ref[...].reshape(rows, width).astype(f32) + attn_out
    middle_ref[...] = middle
    normed, _ = normalize(middle)
    moe_in = (normed * gain_ref[...] + shift_ref[...]).astype(bf16)
    logits = mm(moe_in, router_ref[...])
    exp_logits = jnp.exp(logits - jnp.max(logits, axis=-1, keepdims=True))
    gate = exp_logits / jnp.sum(exp_logits, axis=-1, keepdims=True)
    gate_ref[...] = gate
    expert_lane = lax.broadcasted_iota(jnp.int32, (1, EXPERTS), 1)
    pick_any = jnp.zeros((EXPERTS * stride, rows), bf16)
    slot_gate = jnp.zeros((EXPERTS * stride, 128), f32)
    for k in range(TOP):
        chosen = jnp.sum(
            jnp.where(expert_lane == route_col_ref[:, k : k + 1], gate, 0.0),
            axis=-1,
            keepdims=True,
        )
        pick = slot_picks(dest_row_ref, stride, k)
        pick_any = pick_any + pick
        for term in three_terms(jnp.broadcast_to(chosen, (rows, 128))):
            slot_gate = slot_gate + mm(pick, term)
    sent = mm(pick_any, moe_in).reshape(EXPERTS, stride, width)
    slot_gate = slot_gate[:, 0:1].reshape(EXPERTS, stride, 1)
    sent = with_scalars(sent, slot_gate, stride).astype(bf16)
    store_chunks(sent_refs, sent.reshape(EXPERTS * stride, width), stride)


def scaled_rows(rows_block, grads_block):
    groups, stride, width = rows_block.shape
    scale = row_scalars(rows_block, stride)
    return (grads_block.astype(f32) * scale).astype(bf16).reshape(groups * stride, width)


def expert_kernel(
    rows_ref, cotangent_ref, first_ref, second_ref, *refs, pieces,
):
    value_ref, back_ref, value_acc, grad_acc, scaled_ref = refs[-5:]
    count, _, stride, width = rows_ref.shape
    rows = count * stride
    piece = first_ref.shape[0] // pieces
    step = pl.program_id(1)

    @pl.when(step == 0)
    def _():
        scaled_ref[...] = scaled_rows(rows_ref[:, 0], cotangent_ref[:, 0])

    moe_rows = rows_ref[:, 0].reshape(rows, width)
    grad_rows = scaled_ref[...]
    value = jnp.zeros((rows, width), f32)
    grad = jnp.zeros((rows, width), f32)
    for at in range(pieces):
        first = first_ref[at * piece : (at + 1) * piece, :]
        second = second_ref[at * piece : (at + 1) * piece, :]
        hidden, slope = gelu_pair(mm_nt(moe_rows, first))
        grad_pre = (mm_nt(grad_rows, second) * slope).astype(bf16)
        value = value + mm(hidden.astype(bf16), second)
        grad = grad + mm(grad_pre, first)

    @pl.when(step == 0)
    def _():
        value_acc[...] = value
        grad_acc[...] = grad

    @pl.when(step > 0)
    def _():
        value_acc[...] += value
        grad_acc[...] += grad

    @pl.when(step == pl.num_programs(1) - 1)
    def _():
        value_low = value_acc[...].astype(bf16).reshape(count, stride, width)
        value_ref[:, 0] = value_low
        gate_grad = jnp.sum(
            cotangent_ref[:, 0].astype(f32) * value_low.astype(f32), axis=-1, keepdims=True
        )
        grad_low = grad_acc[...].reshape(count, stride, width)
        back_ref[:, 0] = with_scalars(grad_low, gate_grad, stride).astype(bf16)


def table_part(chunk_refs, part):
    split = chunk_refs[0].shape[0] * chunk_refs[0].shape[1] * len(chunk_refs) // EXPERTS
    pieces = []
    for chunk_ref in chunk_refs:
        sources, each, stride, width = chunk_ref.shape
        block = chunk_ref[...].reshape(sources // split, split, each, stride, width)
        pieces.append(block[:, part])
    table = pieces[0] if len(pieces) == 1 else jnp.concatenate(pieces, axis=1)
    return table.reshape(EXPERTS, table.shape[2], table.shape[3])


def combine_kernel(
    places_ref, middle_ref, gate_ref, cotangent_ref, proj_ref, gain_ref,
    shift_ref, router_ref, route_col_ref, dest_col_ref, stats_ref, *refs,
    image_count, patch_rows, stride, split, seq_count, chunks,
):
    attended_refs = refs[:seq_count]
    back_refs = refs[seq_count : seq_count + chunks]
    grad_middle_ref, router_grad_ref, small_ref = refs[seq_count + chunks :][:3]
    leaving_refs = refs[seq_count + chunks + 3 :]
    rows, width = middle_ref.shape
    group_width = attended_refs[0].shape[-1] // 2
    slots = EXPERTS * stride
    middle = middle_ref[...]
    gate = gate_ref[...]
    valid = valid_rows(places_ref, image_count, patch_rows, (rows, 1), 0).astype(f32)
    grad_total = cotangent_ref[...].reshape(rows, width).astype(f32) * valid
    expert_lane = lax.broadcasted_iota(jnp.int32, (1, EXPERTS), 1)
    slot_lane = lax.broadcasted_iota(jnp.int32, (1, stride), 1)
    slot = lax.broadcasted_iota(jnp.int32, (1, slots), 1)
    pick_any = jnp.zeros((rows, slots), bf16)
    for k in range(TOP):
        pick_any = pick_any + (slot == dest_col_ref[:, k : k + 1]).astype(f32).astype(bf16)
    grad_dispatch = jnp.zeros((rows, width), f32)
    scalar_rows = [jnp.zeros((rows, stride), f32) for _ in range(TOP)]
    own = [
        (expert_lane == route_col_ref[:, k : k + 1]).astype(f32).astype(bf16) for k in range(TOP)
    ]
    for part in range(split):
        table = table_part(back_refs, part)
        grad_dispatch = grad_dispatch + mm(pick_any, table.reshape(slots, width))
        for at in range(stride - 3, stride):
            line = table[:, at, :stride]
            for k in range(TOP):
                scalar_rows[k] = scalar_rows[k] + mm(own[k], line)
    grad_probs = jnp.zeros((rows, EXPERTS), f32)
    for k in range(TOP):
        place = dest_col_ref[:, k : k + 1] - route_col_ref[:, k : k + 1] * stride
        grad_gate = jnp.sum(
            jnp.where(slot_lane == place, scalar_rows[k], 0.0), axis=-1, keepdims=True
        )
        grad_probs = grad_probs + own[k].astype(f32) * grad_gate
    grad_logits = (
        gate * (grad_probs - jnp.sum(grad_probs * gate, axis=-1, keepdims=True))
    ).astype(bf16)
    grad_moe_in = grad_dispatch + mm_nt(grad_logits, router_ref[...])
    normed, inv_root = normalize(middle)
    moe_in = (normed * gain_ref[...] + shift_ref[...]).astype(bf16)
    grad_middle = grad_total + norm_row_grad(grad_moe_in, normed, inv_root, gain_ref[...])
    grad_middle_ref[...] = grad_middle
    grad_attn = grad_middle.astype(bf16)
    for shift in range(seq_count):
        attended = unpacked(attended_refs[shift])
        own_rows = group_rows(places_ref, -shift, seq_count, group_width)
        grads = mm_nt(grad_attn, proj_ref[own_rows, :]).astype(bf16)
        leaving_refs[shift][: rows // 2, :] = side_by_side(grads)
        grads = mm_tn(grad_attn, attended).astype(bf16)
        leaving_refs[shift][rows // 2 :, :] = side_by_side(grads)
    router_grad_ref[...] = mm_tn(grad_logits, moe_in)
    small_ref[0:1, :] = jnp.sum(grad_moe_in * normed, axis=0, keepdims=True)
    small_ref[1:2, :] = jnp.sum(grad_moe_in, axis=0, keepdims=True)
    lane = lax.broadcasted_iota(jnp.int32, (1, width), 1)
    count = jnp.sum(valid, axis=0, keepdims=True) * width
    small_ref[2:3, :] = stats_ref[...] + jnp.where(lane == 3, count, 0.0)


def total_at(values, place):
    lane = lax.broadcasted_iota(jnp.int32, (1, values.shape[-1]), 1)
    by_lane = jnp.sum(values, axis=0, keepdims=True)
    return jnp.where(lane == place, jnp.sum(by_lane, axis=1, keepdims=True), 0.0)


def output_kernel(
    places_ref, middle_ref, gate_ref, route_col_ref, dest_col_ref, *refs,
    image_count, patch_rows, stride, split,
):
    value_refs = refs[:-2]
    output_ref, stats_ref = refs[-2:]
    rows, width = middle_ref.shape
    slots = EXPERTS * stride
    gate = gate_ref[...]
    expert_lane = lax.broadcasted_iota(jnp.int32, (1, EXPERTS), 1)
    slot = lax.broadcasted_iota(jnp.int32, (1, slots), 1)
    moe_out = jnp.zeros((rows, width), f32)
    tables = [table_part(value_refs, part).reshape(slots, width) for part in range(split)]
    for k in range(TOP):
        pick = (slot == dest_col_ref[:, k : k + 1]).astype(f32).astype(bf16)
        pair_value = mm(pick, tables[0])
        for table in tables[1:]:
            pair_value = pair_value + mm(pick, table)
        own = expert_lane == route_col_ref[:, k : k + 1]
        moe_out = moe_out + jnp.sum(jnp.where(own, gate, 0.0), axis=-1, keepdims=True) * pair_value
    valid = valid_rows(places_ref, image_count, patch_rows, (rows, 1), 0).astype(f32)
    total = middle_ref[...] + moe_out
    output_ref[...] = (total * valid).astype(bf16).reshape(output_ref.shape)
    stats_ref[...] = total_at(moe_out * moe_out * valid, 1) + total_at(total * total * valid, 2)


def attention_grad_kernel(
    places_ref, q_ref, k_ref, v_ref, probs_ref, normed_ref, *refs,
    group_heads, head_width, seq_count,
):
    grad_refs = refs[:seq_count]
    packed_refs = refs[seq_count : 2 * seq_count]
    slab_ref, weight_acc, grad_spread, packed_spread = refs[2 * seq_count :]
    patch_rows = grad_spread.shape[2]
    rows = grad_spread.shape[0] * patch_rows
    total_rows = q_ref.shape[1]
    group_width = group_heads * head_width
    scale = head_width ** (-0.5)

    @pl.when(pl.program_id(0) == 0)
    def _():
        for shift, grad_ref in enumerate(grad_refs):
            place = neighbour(places_ref, shift, seq_count)
            grads = stacked(grad_ref[: rows // 2, :])
            for image in range(grad_spread.shape[0]):
                grad_spread[image, place] = grads[image * patch_rows : (image + 1) * patch_rows]

    grad_heads = grad_spread[pl.program_id(0)].reshape(total_rows, group_width)
    q, k, v = q_ref[0], k_ref[0], v_ref[0]
    lane = lax.broadcasted_iota(jnp.int32, (1, group_width), 1)
    nothing = jnp.zeros_like(q)
    grad_q = jnp.zeros((total_rows, group_width), f32)
    grad_k = jnp.zeros((total_rows, group_width), f32)
    grad_v = jnp.zeros((total_rows, group_width), f32)
    for head in range(group_heads):
        in_head = (lane >= head * head_width) & (lane < (head + 1) * head_width)
        own_grad = jnp.where(in_head, grad_heads, nothing)
        probs_low = probs_ref[0, head]
        probs = probs_low.astype(f32)
        grad_probs = mm_nt(own_grad, v)
        delta = jnp.sum(probs * grad_probs, axis=-1, keepdims=True)
        grad_scores = (probs * (grad_probs - delta)).astype(bf16)
        grad_q = jnp.where(in_head, mm(grad_scores, k), grad_q)
        grad_k = jnp.where(in_head, mm_tn(grad_scores, q), grad_k)
        grad_v = jnp.where(in_head, mm_tn(probs_low, grad_heads), grad_v)
    packed = jnp.concatenate([grad_q * scale, grad_k * scale, grad_v], axis=1).astype(bf16)
    packed_spread[...] = packed.reshape(packed_spread.shape)
    for shift, packed_ref in enumerate(packed_refs):
        packed_ref[0] = packed_spread[neighbour(places_ref, shift, seq_count)]
    weight_grad = mm_tn(packed, normed_ref[0])

    @pl.when(pl.program_id(0) == 0)
    def _():
        weight_acc[...] = weight_grad

    @pl.when(pl.program_id(0) > 0)
    def _():
        weight_acc[...] += weight_grad

    @pl.when(pl.program_id(0) == pl.num_programs(0) - 1)
    def _():
        width = weight_acc.shape[1]
        proj_grad = grad_refs[0][rows // 2 :, :].astype(f32)
        for grad_ref in grad_refs[1:]:
            proj_grad = proj_grad + grad_ref[rows // 2 :, :].astype(f32)
        proj_grad = stacked(proj_grad)
        slab = jnp.concatenate([weight_acc[...], proj_grad.T], axis=0).astype(bf16)
        along, cores, chunk, _ = slab_ref.shape
        for core in range(cores):
            for at in range(along):
                start = (core * along + at) * chunk
                slab_ref[at, core] = slab[start : start + chunk]


def assemble_kernel(places_ref, *refs, seq_count):
    own_refs = refs[:seq_count]
    other_refs = refs[seq_count : 2 * seq_count]
    qkv_ref, proj_ref, slabs = refs[2 * seq_count :]
    width = proj_ref.shape[0]
    group_width = width // seq_count
    half = own_refs[0].shape[0]
    @pl.when(pl.program_id(0) == 0)
    def _():
        for shift in range(seq_count):
            group = neighbour(places_ref, -shift, seq_count)
            for places, source_ref in (
                (places_ref[2], own_refs[shift]), (1 - places_ref[2], other_refs[shift]),
            ):
                start = pl.multiple_of(places * half, 16)
                slabs[group, pl.ds(start, half), :] = source_ref[...]

    part = pl.program_id(0)
    values = slabs[:, pl.ds(pl.multiple_of(part * group_width, 16), group_width), :]
    values = values.reshape(width, width).astype(f32)

    @pl.when(part < 3)
    def _():
        qkv_ref[...] = values.T

    @pl.when(part == 3)
    def _():
        proj_ref[...] = values


def input_grad_kernel(
    places_ref, weight_ref, tokens_ref, grad_middle_ref, gain_ref, before_ref, stats_ref,
    router_ref, *refs,
):
    *packed_refs, input_grad_ref, copies_ref, small_ref = refs
    _, patch_rows, width = tokens_ref.shape
    grad = jnp.zeros((patch_rows, width), f32)
    for shift, packed_ref in enumerate(packed_refs):
        group = neighbour(places_ref, -shift, len(packed_refs))
        grad = grad + mm(packed_ref[0], weight_ref[group])
    normed, inv_root = normalize(tokens_ref[0].astype(f32))
    row_grad = norm_row_grad(grad, normed, inv_root, gain_ref[...])
    input_grad_ref[0] = (grad_middle_ref[0] + row_grad).astype(bf16)

    @pl.when(pl.program_id(0) == 0)
    def _():
        small_ref[0:2, :] = before_ref[0:2, :]
        small_ref[2:3, :] = before_ref[2:3, :] + stats_ref[...]
        small_ref[3:5, :] = jnp.zeros((2, width), f32)
        small_ref[5:8, :] = jnp.zeros((3, width), f32)
        small_ref[5:6, : router_ref.shape[-1]] = jnp.sum(router_ref[...], axis=0)

    small_ref[3:4, :] += jnp.sum(grad * normed, axis=0, keepdims=True)
    small_ref[4:5, :] += jnp.sum(grad, axis=0, keepdims=True)

    @pl.when(pl.program_id(0) == pl.num_programs(0) - 1)
    def _():
        copies_ref[...] = jnp.broadcast_to(small_ref[...][None], copies_ref.shape)


def expert_grad_kernel(*refs, row_pieces, row_blocks):
    rows_ref, cotangent_ref, first_ref, second_ref = refs[:4]
    first_grad_ref, second_grad_ref, done_ref, grad_pre_ref, hidden_ref, scaled_ref = refs[-6:]
    stride, width = rows_ref.shape[-2:]
    rows = grad_pre_ref.shape[1]

    def scale():
        share = rows // rows_ref.shape[0]
        for place in range(rows_ref.shape[0]):
            own = slice(place * share, (place + 1) * share)
            scaled_ref[own, :] = scaled_rows(rows_ref[place, :, 0], cotangent_ref[place, :, 0])

    if row_blocks == 1:
        pl.when(pl.program_id(0) == 0)(scale)
    else:
        scale()
    moe_rows = rows_ref[...].reshape(rows, width)
    piece = rows // row_pieces
    first = first_ref[...]
    second = second_ref[...]
    for at in range(row_pieces):
        own = slice(at * piece, (at + 1) * piece)
        hidden, slope = gelu_pair(mm_nt(first, moe_rows[own]))
        hidden_ref[:, own] = hidden.astype(bf16)
        grad_pre_ref[:, own] = (mm_nt(second, scaled_ref[own, :]) * slope).astype(bf16)
    if row_blocks > 1:

        @pl.when(pl.program_id(1) == 0)
        def _():
            second_grad_ref[...] = jnp.zeros(second_grad_ref.shape, f32)
            first_grad_ref[...] = jnp.zeros(first_grad_ref.shape, f32)

        second_grad_ref[...] += mm(hidden_ref[...], scaled_ref[...])
        first_grad_ref[...] += mm(grad_pre_ref[...], moe_rows)
    else:
        second_grad_ref[...] = mm(hidden_ref[...], scaled_ref[...])
        first_grad_ref[...] = mm(grad_pre_ref[...], moe_rows)
    done_ref[...] = jnp.zeros(done_ref.shape, f32)


smem = pl.BlockSpec(memory_space=pltpu.SMEM)
vmem = pl.BlockSpec(memory_space=pltpu.VMEM)
params = pltpu.CompilerParams(vmem_limit_bytes=60 * 1024 * 1024)


def cost(microseconds):
    return pl.CostEstimate(
        flops=int(microseconds * 6e8), transcendentals=0, bytes_accessed=int(microseconds * 1e5)
    )


def struct(shape, dtype):
    return jax.ShapeDtypeStruct(shape, dtype)


def per_device(
    tokens, routes, priority, hires, gain_one, shift_one, w_qkv, w_proj, gain_two, shift_two,
    w_router, expert_in, expert_out, cotangent,
):
    image_count, patch_rows, width = tokens.shape
    rows = image_count * patch_rows
    seq_count = lax.axis_size("seq")
    ep_count = lax.axis_size("ep")
    full_rows = patch_rows * seq_count
    head_width = width // HEADS
    group_heads = HEADS // seq_count
    group_width = group_heads * head_width
    local_experts = max(1, EXPERTS // ep_count)
    split = max(1, ep_count // EXPERTS)
    local_hidden = expert_in.shape[0] // local_experts
    capacity = max(2, (105 * TOP * rows + 100 * EXPERTS - 1) // (100 * EXPERTS))
    stride = (capacity + 3 + 15) // 16 * 16
    chunks = 2 if local_experts % 2 == 0 else 1
    each = local_experts // chunks
    seq_place = lax.axis_index("seq")
    ep_place = lax.axis_index("ep")
    places = jnp.stack([hires[0], seq_place.astype(jnp.int32), (ep_place % 2).astype(jnp.int32)])
    gain_one, shift_one, gain_two, shift_two = (
        vector.reshape(1, width) for vector in (gain_one, shift_one, gain_two, shift_two)
    )
    common = dict(image_count=image_count, patch_rows=patch_rows, stride=stride)

    def exchange(values, axis):
        return lax.all_to_all(values, axis, split_axis=0, concat_axis=0, tiled=True)

    def send_slots(chunk):
        if split > 1:
            chunk = jnp.broadcast_to(chunk[:, None], (EXPERTS, split) + chunk.shape[1:])
            chunk = chunk.reshape((ep_count,) + chunk.shape[2:])
        return exchange(chunk, "ep")

    def move(values, axis, shift):
        count = lax.axis_size(axis)
        if shift % count == 0:
            return values
        return lax.ppermute(values, axis, [(at, (at + shift) % count) for at in range(count)])

    def other_core(values):
        return lax.ppermute(values, "ep", [(at, at ^ 1) for at in range(ep_count)])

    def hold(values, *others):
        values = tuple(values)
        anywhere = pl.BlockSpec(memory_space=pl.ANY)
        return call(
            lambda *refs: None,
            "hold",
            waits=others,
            in_specs=[anywhere] * len(values),
            out_specs=[anywhere] * len(values),
            out_shape=[struct(value.shape, value.dtype) for value in values],
            input_output_aliases={at: at for at in range(len(values))},
            cost_estimate=cost(1),
        )(*values)

    def over_seq(values):
        return lax.all_gather(values, "seq", axis=0, tiled=False)

    def call(kernel, name, waits=(), **spec):
        waits = tuple(waits)

        def run(*operands):
            count = len(operands)

            def body(*refs):
                kernel(*refs[:count], *refs[count + len(waits) :])

            unread = [pl.BlockSpec(memory_space=pl.ANY)] * len(waits)
            if "grid_spec" in spec:
                grid_spec = dict(spec["grid_spec"])
                grid_spec["in_specs"] = grid_spec["in_specs"] + unread
                own = dict(spec, grid_spec=pltpu.PrefetchScalarGridSpec(**grid_spec))
            else:
                own = dict(spec, in_specs=spec["in_specs"] + unread)
            return pl.pallas_call(body, name=name, compiler_params=params, **own)(
                *operands, *waits
            )

        return run

    def slot_struct(experts):
        return struct((min(ep_count, EXPERTS), experts, stride, width), bf16)

    chunk_struct = slot_struct(each)
    moved_struct = struct((ep_count, each, stride, width), bf16)

    tokens_moved = [move(tokens, "seq", shift) for shift in range(seq_count)]
    pairs = jnp.concatenate([routes.reshape(rows, TOP).T, priority.reshape(1, rows)], axis=0)
    route_col, dest_col, dest_row = call(
        lambda *refs: routing_kernel(*refs, capacity=capacity, **common),
        "routing",
        in_specs=[smem, vmem],
        out_specs=[vmem] * 3,
        out_shape=[
            struct((rows, TOP), jnp.int32),
            struct((rows, TOP), jnp.int32),
            struct((TOP, rows), jnp.int32),
        ],
        cost_estimate=cost(3),
    )(places, pairs)
    cotangent_sent = call(
        lambda *refs: send_grads_kernel(*refs, stride=stride),
        "send_grads",
        in_specs=[vmem] * 2,
        out_specs=[vmem] * chunks,
        out_shape=[chunk_struct] * chunks,
        cost_estimate=cost(3),
    )(cotangent, dest_row)
    weight_groups = (
        w_qkv.reshape(width, 3, seq_count, group_width)
        .transpose(2, 1, 3, 0)
        .reshape(seq_count, 3 * group_width, width)
    )

    cotangent_slots = [send_slots(chunk) for chunk in cotangent_sent]

    row_block = pl.BlockSpec((1, full_rows, group_width), lambda i, *_: (i, 0, 0))
    probs_block = pl.BlockSpec((1, group_heads, full_rows, full_rows), lambda i, *_: (i, 0, 0, 0))
    normed_block = pl.BlockSpec((1, full_rows, width), lambda i, *_: (i, 0, 0))
    half_block = pl.BlockSpec((1, patch_rows // 2, 2 * group_width), lambda i, *_: (i, 0, 0))
    packed_block = pl.BlockSpec((1, patch_rows, 3 * group_width), lambda i, *_: (i, 0, 0))
    vector_block = pl.BlockSpec((1, width), lambda i, *_: (0, 0))
    image_block = pl.BlockSpec((1, patch_rows, width), lambda i, *_: (i, 0, 0))
    half_struct = struct((image_count, patch_rows // 2, 2 * group_width), bf16)
    row_struct = struct((image_count, full_rows, group_width), bf16)
    *attended, q, k, v, probs, attn_in = call(
        lambda *refs: attention_kernel(
            *refs, seq_count=seq_count, group_heads=group_heads, head_width=head_width
        ),
        "attention",
        waits=cotangent_sent,
        grid_spec=dict(
            num_scalar_prefetch=1,
            grid=(image_count,),
            in_specs=[
                vector_block,
                vector_block,
                pl.BlockSpec((1, 3 * group_width, width), lambda i, at: (at[1], 0, 0)),
            ]
            + [image_block] * seq_count,
            out_specs=[half_block] * seq_count
            + [row_block, row_block, row_block, probs_block, normed_block],
            scratch_shapes=[
                pltpu.VMEM((seq_count, patch_rows, group_width), bf16),
                pltpu.VMEM((seq_count, patch_rows, width), bf16),
            ],
        ),
        out_shape=[half_struct] * seq_count
        + [
            row_struct,
            row_struct,
            row_struct,
            struct((image_count, group_heads, full_rows, full_rows), bf16),
            struct((image_count, full_rows, width), bf16),
        ],
        cost_estimate=cost(16),
    )(places, gain_one, shift_one, weight_groups, *tokens_moved)
    attended_sent = attended
    attended = [move(block, "seq", shift) for shift, block in enumerate(attended)]
    cotangent_slots[:1] = hold(cotangent_slots[:1], attended_sent[0])
    cotangent_slots[1:] = hold(cotangent_slots[1:], attended_sent[1]) if chunks > 1 else []

    middle, gate, stats, *rows_sent = call(
        lambda *refs: dispatch_kernel(*refs, seq_count=seq_count, **common),
        "dispatch",
        waits=cotangent_slots,
        in_specs=[smem] + [vmem] * (7 + seq_count),
        out_specs=[vmem] * (3 + chunks),
        out_shape=[
            struct((rows, width), f32),
            struct((rows, EXPERTS), f32),
            struct((1, width), f32),
        ]
        + [chunk_struct] * chunks,
        cost_estimate=cost(9),
    )(
        places, tokens, w_proj, gain_two, shift_two, w_router, route_col, dest_row, *attended,
    )
    row_slots = [send_slots(chunk) for chunk in rows_sent]

    hidden_tile = local_hidden // 2
    tiles = local_hidden // hidden_tile
    moved_block = pl.BlockSpec((ep_count, 1, stride, width), lambda e, f: (0, e, 0, 0))
    cotangent_all = [over_seq(slots) for slots in cotangent_slots]
    grads_back, values_back = [], ()
    for at in range(chunks):
        weight_block = pl.BlockSpec(
            (hidden_tile, width), lambda e, f, at=at: ((e + at * each) * tiles + f, 0)
        )
        all_block = pl.BlockSpec(
            (ep_count, 1, stride, width), lambda e, f, at=at: (0, e + at * each, 0, 0)
        )
        value, back = call(
            lambda *refs: expert_kernel(*refs, pieces=max(1, hidden_tile // 768)),
            "experts",
            waits=cotangent_all[:1] * (at > 0),
            grid=(each, tiles),
            in_specs=[moved_block, moved_block, weight_block, weight_block]
            + [pl.BlockSpec(memory_space=pl.ANY)] * len(values_back),
            out_specs=[all_block, moved_block],
            out_shape=[struct((ep_count, local_experts, stride, width), bf16), moved_struct],
            scratch_shapes=[pltpu.VMEM((ep_count * stride, width), f32)] * 2
            + [pltpu.VMEM((ep_count * stride, width), bf16)],
            input_output_aliases={4: 0} if values_back else {},
            cost_estimate=cost(16),
        )(row_slots[at], cotangent_slots[at], expert_in, expert_out, *values_back)
        grads_back.append(exchange(back, "ep"))
        values_back = (value,)

    all_rows = seq_count * ep_count * stride
    grad_tile = min(768, local_hidden)
    grad_tiles = local_hidden // grad_tile
    anywhere = pl.BlockSpec(memory_space=pl.ANY)
    rows_all = [over_seq(slots) for slots in row_slots]
    grads = []

    row_blocks = max(1, all_rows // 1024)
    sources = ep_count // row_blocks
    block_rows = all_rows // row_blocks

    def expert_grads(expert, begin, count, *others):
        place = expert * grad_tiles + begin
        tile_block = pl.BlockSpec((grad_tile, width), lambda f, r: (place + f, 0))

        def source_block(own):
            return pl.BlockSpec(
                (seq_count, sources, 1, stride, width),
                lambda f, r: (0, r, own, 0, 0),
                pipeline_mode=pl.Buffered(1 if row_blocks == 1 else 2),
            )

        *grads[:], done = call(
            lambda *refs: expert_grad_kernel(
                *refs, row_pieces=max(1, block_rows // 512), row_blocks=row_blocks
            ),
            "expert_grads",
            waits=others,
            grid=(count, row_blocks),
            in_specs=[source_block(expert % each)] * 2 + [tile_block, tile_block]
            + [anywhere] * len(grads),
            out_specs=[tile_block, tile_block, pl.BlockSpec((8, 128), lambda f, r: (0, 0))],
            out_shape=[
                struct(expert_in.shape, f32),
                struct(expert_out.shape, f32),
                struct((8, 128), f32),
            ],
            scratch_shapes=[pltpu.VMEM((grad_tile, block_rows), bf16)] * 2
            + [pltpu.VMEM((block_rows, width), bf16)],
            input_output_aliases={4: 0, 5: 1} if grads else {},
            cost_estimate=cost(7 * count),
        )(rows_all[expert // each], cotangent_all[expert // each], expert_in, expert_out, *grads)
        return done

    work = [(expert, 0, grad_tiles) for expert in range(local_experts)]
    work = iter(work)

    def next_grads(*others):
        return [expert_grads(*part, *others) for part in itertools.islice(work, 1)]

    early = next_grads(values_back[0], grads_back[0]) if local_experts > 3 else []
    leaving_shape = ((rows + width) // 2, 2 * group_width)
    grad_middle, router_grad, small, *leaving = call(
        lambda *refs: combine_kernel(
            *refs, split=split, seq_count=seq_count, chunks=chunks, **common
        ),
        "combine",
        waits=early,
        in_specs=[smem] + [vmem] * (10 + seq_count + chunks),
        out_specs=[vmem] * (3 + seq_count),
        out_shape=[
            struct((rows, width), f32),
            struct((EXPERTS, width), f32),
            struct((3, width), f32),
        ]
        + [struct(leaving_shape, bf16)] * seq_count,
        cost_estimate=cost(10),
    )(
        places, middle, gate, cotangent, w_proj, gain_two, shift_two, w_router,
        route_col, dest_col, stats, *attended, *grads_back,
    )
    devices = seq_count * ep_count
    leaving = [move(block, "seq", -at) for at, block in enumerate(leaving)]
    piece = EXPERTS * width // devices
    router_grad = exchange(router_grad.reshape(devices, 1, piece), ("seq", "ep"))
    values_moved = exchange(values_back[0], "ep")
    middle_done = next_grads(grad_middle) if local_experts > 2 else []
    half = 2 * group_width
    pairs_along = ep_count // 2
    slab_shape = (pairs_along, 2, half // pairs_along, width)
    *packed_sent, slab = call(
        lambda *refs: attention_grad_kernel(
            *refs, group_heads=group_heads, head_width=head_width, seq_count=seq_count
        ),
        "attention_grad",
        waits=middle_done,
        grid=(image_count,),
        in_specs=[smem, row_block, row_block, row_block, probs_block, normed_block]
        + [pl.BlockSpec(leaving_shape, lambda i: (0, 0))] * seq_count,
        out_specs=[packed_block] * seq_count
        + [pl.BlockSpec(slab_shape, lambda i: (0, 0, 0, 0))],
        out_shape=[struct((image_count, patch_rows, 3 * group_width), bf16)] * seq_count
        + [struct(slab_shape, bf16)],
        scratch_shapes=[
            pltpu.VMEM((3 * group_width, width), f32),
            pltpu.VMEM((image_count, seq_count, patch_rows, group_width), bf16),
            pltpu.VMEM((seq_count, patch_rows, 3 * group_width), bf16),
        ],
        cost_estimate=cost(18),
    )(places, q, k, v, probs, attn_in, *leaving)
    packed = [move(block, "seq", shift) for shift, block in enumerate(packed_sent)]

    same_core = [[2 * at + core for at in range(pairs_along)] for core in range(2)]

    def along_core(values):
        return lax.all_to_all(
            values, "ep", split_axis=0, concat_axis=0, tiled=True, axis_index_groups=same_core
        )

    slab = lax.psum_scatter(
        slab.reshape(2 * half, width), "ep", scatter_dimension=0, tiled=True
    )
    late = next_grads(packed_sent[0], router_grad) if local_experts > 1 else []
    slab, packed[1] = hold([slab, packed[1]], *late, values_moved, *packed[2:])
    slab = jnp.broadcast_to(slab[None], (pairs_along, half // pairs_along, width))
    output, value_stats = call(
        lambda *refs: output_kernel(*refs, split=split, **common),
        "output",
        waits=[slab],
        in_specs=[smem] + [vmem] * 5,
        out_specs=[vmem] * 2,
        out_shape=[struct((image_count, patch_rows, width), bf16), struct((1, width), f32)],
        cost_estimate=cost(5),
    )(places, middle, gate, route_col, dest_col, values_moved)
    slab_moved = along_core(slab).reshape(half, width)
    own_slabs = [move(slab_moved, "seq", shift) for shift in range(seq_count)]
    input_grad, copies = call(
        input_grad_kernel,
        "input_grad",
        grid=(image_count,),
        in_specs=[
            smem,
            pl.BlockSpec((seq_count, 3 * group_width, width), lambda i: (0, 0, 0)),
            image_block,
            image_block,
            vector_block,
            pl.BlockSpec((3, width), lambda i: (0, 0)),
            pl.BlockSpec((1, width), lambda i: (0, 0)),
            pl.BlockSpec((devices, 1, piece), lambda i: (0, 0, 0)),
        ]
        + [packed_block] * seq_count,
        out_specs=[image_block, pl.BlockSpec((devices, 8, width), lambda i: (0, 0, 0))],
        out_shape=[
            struct((image_count, patch_rows, width), bf16),
            struct((devices, 8, width), f32),
        ],
        scratch_shapes=[pltpu.VMEM((8, width), f32)],
        cost_estimate=cost(7),
    )(
        places, weight_groups, tokens, grad_middle.reshape(image_count, patch_rows, width),
        gain_one, small, value_stats, router_grad, *packed,
    )
    own_slabs = hold(own_slabs, *next_grads(input_grad, slab_moved))
    other_slabs = [other_core(each_slab) for each_slab in own_slabs]
    qkv_grad, proj_grad = call(
        lambda *refs: assemble_kernel(*refs, seq_count=seq_count),
        "assemble",
        grid=(4,),
        in_specs=[smem] + [pl.BlockSpec((half, width), lambda i: (0, 0))] * (2 * seq_count),
        out_specs=[
            pl.BlockSpec((width, width), lambda i: (0, jnp.minimum(i, 2))),
            pl.BlockSpec((width, width), lambda i: (0, 0)),
        ],
        out_shape=[struct((width, 3 * width), f32), struct((width, width), f32)],
        scratch_shapes=[pltpu.VMEM((seq_count, 2 * half, width), bf16)],
        cost_estimate=cost(8),
    )(places, *own_slabs, *other_slabs)

    copies = exchange(copies, ("seq", "ep"))
    sums = jnp.sum(copies[:, :5], axis=0)
    router_grad = copies[:, 5, :piece].reshape(EXPERTS, width).T
    return (
        output,
        input_grad,
        sums[3],
        sums[4],
        qkv_grad,
        proj_grad,
        sums[0],
        sums[1],
        router_grad,
        grads[0],
        grads[1],
        jnp.sqrt(sums[2, :3] / sums[2, 3]),
    )


def solution(mesh):
    in_specs = (
        P("ep", "seq", None),
        P("ep", "seq", None),
        P("ep", "seq"),
        P("ep"),
        P(),
        P(),
        P(),
        P(),
        P(),
        P(),
        P(),
        P("ep", None),
        P("ep", None),
        P("ep", "seq", None),
    )
    out_specs = (
        P("ep", "seq", None),
        P("ep", "seq", None),
        P(),
        P(),
        P(),
        P(),
        P(),
        P(),
        P(),
        P("ep", None),
        P("ep", None),
        P(),
    )
    return jax.shard_map(
        per_device, mesh=mesh, in_specs=in_specs, out_specs=out_specs, check_vma=False
    )
```

```python
import itertools

import jax
import jax.numpy as jnp
from jax import lax
from jax.experimental import pallas as pl
from jax.experimental.pallas import tpu as pltpu
from jax.sharding import PartitionSpec as P

HEADS = 12
EXPERTS = 32
TOP = 2
PATCHES = 576
SHORT = 196

norm_eps = 1e-06
neg_big = -1e30
f32 = jnp.float32
bf16 = jnp.bfloat16

tail_slope = 0.33
tail_terms = (
    0.18635779800457905,
    0.18295602991113566,
    0.2012232872944192,
    0.04722279904104141,
    0.40849559831839843,
    -0.3511445702318978,
    0.46023391759858995,
    -0.13534486747679436,
)


def mm(a, b):
    return lax.dot_general(a, b, (((1,), (0,)), ((), ())), preferred_element_type=f32)


def mm_nt(a, b):
    return lax.dot_general(a, b, (((1,), (1,)), ((), ())), preferred_element_type=f32)


def mm_tn(a, b):
    return lax.dot_general(a, b, (((0,), (0,)), ((), ())), preferred_element_type=f32)


def gelu_pair(v):
    size = jnp.abs(v)
    bell = jnp.exp(v * v * -0.5)
    t = 1.0 / (1.0 + size * (tail_slope * 0.7071067811865476))
    poly = tail_terms[-1] * 0.5
    for term in tail_terms[-2::-1]:
        poly = poly * t + term * 0.5
    tail = poly * t * bell
    cdf = jnp.where(v >= 0.0, 1.0 - tail, tail)
    return v * cdf, cdf + v * bell * 0.3989422804014327


def normalize(values):
    centred = values - jnp.mean(values, axis=-1, keepdims=True)
    inv_root = lax.rsqrt(jnp.mean(centred * centred, axis=-1, keepdims=True) + norm_eps)
    return centred * inv_root, inv_root


def norm_row_grad(upstream, normed, inv_root, gain):
    scaled = upstream * gain
    return inv_root * (
        scaled
        - jnp.mean(scaled, axis=-1, keepdims=True)
        - normed * jnp.mean(scaled * normed, axis=-1, keepdims=True)
    )


def valid_rows(places_ref, image_count, patch_rows, shape, axis):
    row = lax.broadcasted_iota(jnp.int32, shape, axis)
    first_patch = places_ref[1] * patch_rows
    valid = row < 0
    for image in range(image_count):
        length = jnp.where(image < places_ref[0], PATCHES, SHORT)
        start = image * patch_rows
        stop = start + jnp.clip(length - first_patch, 0, patch_rows)
        valid = valid | ((row >= start) & (row < stop))
    return valid


def routing_kernel(
    places_ref, pairs_ref, route_col_ref, dest_col_ref, dest_row_ref,
    *, image_count, patch_rows, capacity, stride,
):
    rows = pairs_ref.shape[1]
    eye = lax.broadcasted_iota(jnp.int32, (rows, rows), 0) == lax.broadcasted_iota(
        jnp.int32, (rows, rows), 1
    )

    def as_column(line):
        return jnp.sum(jnp.where(eye, line.astype(f32), 0.0), axis=1, keepdims=True).astype(
            jnp.int32
        )

    e_row = [pairs_ref[k : k + 1, :] for k in range(TOP)]
    e_col = [as_column(line) for line in e_row]
    prio_row = pairs_ref[TOP : TOP + 1, :]
    prio_col = as_column(prio_row)
    for k in range(TOP):
        route_col_ref[:, k : k + 1] = e_col[k]
    valid_col = valid_rows(places_ref, image_count, patch_rows, (rows, 1), 0)
    valid_row = valid_rows(places_ref, image_count, patch_rows, (1, rows), 1)
    weight_col = valid_col.astype(f32)
    weight_row = valid_row.astype(f32)
    row_first = (prio_row < prio_col).astype(f32) * weight_row
    col_first = (prio_col < prio_row).astype(f32) * weight_col
    for k in range(TOP):
        count = jnp.where(e_col[k] == e_row[k], row_first, 0.0)
        for earlier in range(k):
            count = count + jnp.where(e_col[k] == e_row[earlier], weight_row, 0.0)
        slot = jnp.sum(count, axis=1, keepdims=True).astype(jnp.int32)
        keep = valid_col & (slot < capacity)
        dest_col_ref[:, k : k + 1] = jnp.where(keep, e_col[k] * stride + slot, -1)
        count = jnp.where(e_col[k] == e_row[k], col_first, 0.0)
        for earlier in range(k):
            count = count + jnp.where(e_col[earlier] == e_row[k], weight_col, 0.0)
        slot = jnp.sum(count, axis=0, keepdims=True).astype(jnp.int32)
        keep = valid_row & (slot < capacity)
        dest_row_ref[k : k + 1, :] = jnp.where(keep, e_row[k] * stride + slot, -1)


def side_by_side(values):
    half = values.shape[0] // 2
    return jnp.concatenate([values[:half], values[half:]], axis=1)


def stacked(values):
    width = values.shape[1] // 2
    return jnp.concatenate([values[:, :width], values[:, width:]], axis=0)


def neighbour(places_ref, shift, seq_count):
    return (places_ref[1] + (shift + seq_count)) % seq_count


def attention_kernel(
    places_ref, gain_ref, shift_ref, weight_ref, *refs,
    first_image, seq_count, group_heads, head_width,
):
    tokens_refs = refs[:seq_count]
    attended_refs = refs[seq_count : 2 * seq_count]
    q_ref, k_ref, v_ref, probs_ref, normed_ref, spread_ref, tokens_ref = refs[2 * seq_count :]
    _, patch_rows, width = tokens_refs[0].shape
    for shift, source_ref in enumerate(tokens_refs):
        tokens_ref[neighbour(places_ref, -shift, seq_count)] = source_ref[0]
    total_rows = seq_count * patch_rows
    group_width = group_heads * head_width
    values = tokens_ref[...].reshape(total_rows, width).astype(f32)
    normed, _ = normalize(values)
    attn_in = (normed * gain_ref[...] + shift_ref[...]).astype(bf16)
    normed_ref[0] = attn_in
    q, k, v = (
        mm_nt(attn_in, weight_ref[0, part * group_width : (part + 1) * group_width, :]).astype(bf16)
        for part in range(3)
    )
    q_ref[0] = q
    k_ref[0] = k
    v_ref[0] = v
    length = jnp.where(first_image + pl.program_id(0) < places_ref[0], PATCHES, SHORT)
    key_valid = lax.broadcasted_iota(jnp.int32, (1, total_rows), 1) < length
    lane = lax.broadcasted_iota(jnp.int32, (1, group_width), 1)
    scaled_q = (q.astype(f32) * head_width ** (-0.5)).astype(bf16)
    attended = jnp.zeros((total_rows, group_width), f32)
    for head in range(group_heads):
        in_head = (lane >= head * head_width) & (lane < (head + 1) * head_width)
        scores = mm_nt(jnp.where(in_head, scaled_q, jnp.zeros_like(scaled_q)), k)
        scores = jnp.where(key_valid, scores, neg_big)
        exp_scores = jnp.exp(scores - jnp.max(scores, axis=-1, keepdims=True))
        inverse = 1.0 / jnp.sum(exp_scores, axis=-1, keepdims=True)
        probs = (exp_scores * inverse).astype(bf16)
        probs_ref[0, head] = probs
        attended = jnp.where(in_head, mm(probs, v), attended)
    spread_ref[...] = attended.astype(bf16).reshape(spread_ref.shape)
    for shift, attended_ref in enumerate(attended_refs):
        attended_ref[0] = side_by_side(spread_ref[neighbour(places_ref, shift, seq_count)])


def slot_picks(dest_row_ref, stride, k):
    slot = lax.broadcasted_iota(jnp.int32, (EXPERTS * stride, 1), 0)
    return (slot == dest_row_ref[k : k + 1, :]).astype(f32).astype(bf16)


def send_grads_kernel(cotangent_ref, dest_row_ref, *sent_refs, stride):
    width = cotangent_ref.shape[-1]
    cotangent = cotangent_ref[...].reshape(-1, width)
    pick = slot_picks(dest_row_ref, stride, 0)
    for k in range(1, TOP):
        pick = pick + slot_picks(dest_row_ref, stride, k)
    sent = mm(pick, cotangent).astype(bf16)
    store_chunks(sent_refs, sent, stride)


def store_chunks(chunk_refs, table, stride):
    width = table.shape[-1]
    targets, each = chunk_refs[0].shape[:2]
    grouped = table.reshape(targets, len(chunk_refs) * each, stride, width)
    for at, chunk_ref in enumerate(chunk_refs):
        chunk_ref[...] = grouped[:, at * each : (at + 1) * each]


def three_terms(values):
    high = values.astype(bf16)
    rest = values - high.astype(f32)
    middle = rest.astype(bf16)
    return high, middle, (rest - middle.astype(f32)).astype(bf16)


def diagonal(stride):
    row = lax.broadcasted_iota(jnp.int32, (1, stride, stride), 1)
    return row == lax.broadcasted_iota(jnp.int32, (1, stride, stride), 2)


def row_scalars(block, stride):
    spare = block[:, stride - 3 : stride, :stride].astype(f32)
    line = spare[:, 0:1] + spare[:, 1:2] + spare[:, 2:3]
    return jnp.sum(jnp.where(diagonal(stride), line, 0.0), axis=2, keepdims=True)


def with_scalars(block, column, stride):
    width = block.shape[-1]
    line = jnp.sum(jnp.where(diagonal(stride), column, 0.0), axis=1, keepdims=True)
    line = jnp.concatenate(
        [line, jnp.zeros((line.shape[0], 1, width - stride), f32)], axis=2
    )
    row = lax.broadcasted_iota(jnp.int32, (1, stride, 1), 1)
    for at, term in enumerate(three_terms(line)):
        block = jnp.where(row == stride - 3 + at, term.astype(f32), block)
    return block


def unpacked(blocks_ref):
    return jnp.concatenate([stacked(blocks_ref[at]) for at in range(blocks_ref.shape[0])], axis=0)


def group_rows(places_ref, shift, seq_count, group_width):
    start = neighbour(places_ref, shift, seq_count) * group_width
    return pl.ds(pl.multiple_of(start, 16), group_width)


def dispatch_kernel(
    places_ref, tokens_ref, proj_ref, gain_ref, shift_ref,
    router_ref, route_col_ref, dest_row_ref, *refs, image_count, patch_rows, stride, seq_count,
):
    attended_refs = refs[:seq_count]
    middle_ref, gate_ref, stats_ref, *sent_refs = refs[seq_count:]
    rows, width = middle_ref.shape
    group_width = attended_refs[0].shape[-1] // 2
    attn_out = jnp.zeros((rows, width), f32)
    for shift, attended_ref in enumerate(attended_refs):
        attn_out = attn_out + mm(
            unpacked(attended_ref),
            proj_ref[group_rows(places_ref, -shift, seq_count, group_width), :],
        )
    valid = valid_rows(places_ref, image_count, patch_rows, (rows, 1), 0).astype(f32)
    stats_ref[...] = total_at(attn_out * attn_out * valid, 0)
    middle = tokens_ref[...].reshape(rows, width).astype(f32) + attn_out
    middle_ref[...] = middle
    normed, _ = normalize(middle)
    moe_in = (normed * gain_ref[...] + shift_ref[...]).astype(bf16)
    logits = mm(moe_in, router_ref[...])
    exp_logits = jnp.exp(logits - jnp.max(logits, axis=-1, keepdims=True))
    gate = exp_logits / jnp.sum(exp_logits, axis=-1, keepdims=True)
    gate_ref[...] = gate
    expert_lane = lax.broadcasted_iota(jnp.int32, (1, EXPERTS), 1)
    pick_any = jnp.zeros((EXPERTS * stride, rows), bf16)
    slot_gate = jnp.zeros((EXPERTS * stride, 128), f32)
    for k in range(TOP):
        chosen = jnp.sum(
            jnp.where(expert_lane == route_col_ref[:, k : k + 1], gate, 0.0),
            axis=-1,
            keepdims=True,
        )
        pick = slot_picks(dest_row_ref, stride, k)
        pick_any = pick_any + pick
        for term in three_terms(jnp.broadcast_to(chosen, (rows, 128))):
            slot_gate = slot_gate + mm(pick, term)
    sent = mm(pick_any, moe_in).reshape(EXPERTS, stride, width)
    slot_gate = slot_gate[:, 0:1].reshape(EXPERTS, stride, 1)
    sent = with_scalars(sent, slot_gate, stride).astype(bf16)
    store_chunks(sent_refs, sent.reshape(EXPERTS * stride, width), stride)


def scaled_rows(rows_block, grads_block):
    groups, stride, width = rows_block.shape
    scale = row_scalars(rows_block, stride)
    return (grads_block.astype(f32) * scale).astype(bf16).reshape(groups * stride, width)


def expert_kernel(
    rows_ref, cotangent_ref, first_ref, second_ref, *refs, pieces,
):
    value_ref, back_ref, value_acc, grad_acc, scaled_ref = refs[-5:]
    count, _, stride, width = rows_ref.shape
    rows = count * stride
    piece = first_ref.shape[0] // pieces
    step = pl.program_id(1)

    @pl.when(step == 0)
    def _():
        scaled_ref[...] = scaled_rows(rows_ref[:, 0], cotangent_ref[:, 0])

    moe_rows = rows_ref[:, 0].reshape(rows, width)
    grad_rows = scaled_ref[...]
    value = jnp.zeros((rows, width), f32)
    grad = jnp.zeros((rows, width), f32)
    for at in range(pieces):
        first = first_ref[at * piece : (at + 1) * piece, :]
        second = second_ref[at * piece : (at + 1) * piece, :]
        hidden, slope = gelu_pair(mm_nt(moe_rows, first))
        grad_pre = (mm_nt(grad_rows, second) * slope).astype(bf16)
        value = value + mm(hidden.astype(bf16), second)
        grad = grad + mm(grad_pre, first)

    @pl.when(step == 0)
    def _():
        value_acc[...] = value
        grad_acc[...] = grad

    @pl.when(step > 0)
    def _():
        value_acc[...] += value
        grad_acc[...] += grad

    @pl.when(step == pl.num_programs(1) - 1)
    def _():
        value_low = value_acc[...].astype(bf16).reshape(count, stride, width)
        value_ref[:, 0] = value_low
        gate_grad = jnp.sum(
            cotangent_ref[:, 0].astype(f32) * value_low.astype(f32), axis=-1, keepdims=True
        )
        grad_low = grad_acc[...].reshape(count, stride, width)
        back_ref[:, 0] = with_scalars(grad_low, gate_grad, stride).astype(bf16)


def table_part(chunk_refs, part):
    split = chunk_refs[0].shape[0] * chunk_refs[0].shape[1] * len(chunk_refs) // EXPERTS
    pieces = []
    for chunk_ref in chunk_refs:
        sources, each, stride, width = chunk_ref.shape
        block = chunk_ref[...].reshape(sources // split, split, each, stride, width)
        pieces.append(block[:, part])
    table = pieces[0] if len(pieces) == 1 else jnp.concatenate(pieces, axis=1)
    return table.reshape(EXPERTS, table.shape[2], table.shape[3])


def combine_kernel(
    places_ref, middle_ref, gate_ref, cotangent_ref, proj_ref, gain_ref,
    shift_ref, router_ref, route_col_ref, dest_col_ref, stats_ref, *refs,
    image_count, patch_rows, stride, split, seq_count, chunks,
):
    attended_refs = refs[:seq_count]
    back_refs = refs[seq_count : seq_count + chunks]
    grad_middle_ref, router_grad_ref, small_ref = refs[seq_count + chunks :][:3]
    leaving_refs = refs[seq_count + chunks + 3 :]
    rows, width = middle_ref.shape
    group_width = attended_refs[0].shape[-1] // 2
    slots = EXPERTS * stride
    middle = middle_ref[...]
    gate = gate_ref[...]
    valid = valid_rows(places_ref, image_count, patch_rows, (rows, 1), 0).astype(f32)
    grad_total = cotangent_ref[...].reshape(rows, width).astype(f32) * valid
    expert_lane = lax.broadcasted_iota(jnp.int32, (1, EXPERTS), 1)
    slot_lane = lax.broadcasted_iota(jnp.int32, (1, stride), 1)
    slot = lax.broadcasted_iota(jnp.int32, (1, slots), 1)
    pick_any = jnp.zeros((rows, slots), bf16)
    for k in range(TOP):
        pick_any = pick_any + (slot == dest_col_ref[:, k : k + 1]).astype(f32).astype(bf16)
    grad_dispatch = jnp.zeros((rows, width), f32)
    scalar_rows = [jnp.zeros((rows, stride), f32) for _ in range(TOP)]
    own = [
        (expert_lane == route_col_ref[:, k : k + 1]).astype(f32).astype(bf16) for k in range(TOP)
    ]
    for part in range(split):
        table = table_part(back_refs, part)
        grad_dispatch = grad_dispatch + mm(pick_any, table.reshape(slots, width))
        for at in range(stride - 3, stride):
            line = table[:, at, :stride]
            for k in range(TOP):
                scalar_rows[k] = scalar_rows[k] + mm(own[k], line)
    grad_probs = jnp.zeros((rows, EXPERTS), f32)
    for k in range(TOP):
        place = dest_col_ref[:, k : k + 1] - route_col_ref[:, k : k + 1] * stride
        grad_gate = jnp.sum(
            jnp.where(slot_lane == place, scalar_rows[k], 0.0), axis=-1, keepdims=True
        )
        grad_probs = grad_probs + own[k].astype(f32) * grad_gate
    grad_logits = (
        gate * (grad_probs - jnp.sum(grad_probs * gate, axis=-1, keepdims=True))
    ).astype(bf16)
    grad_moe_in = grad_dispatch + mm_nt(grad_logits, router_ref[...])
    normed, inv_root = normalize(middle)
    moe_in = (normed * gain_ref[...] + shift_ref[...]).astype(bf16)
    grad_middle = grad_total + norm_row_grad(grad_moe_in, normed, inv_root, gain_ref[...])
    grad_middle_ref[...] = grad_middle
    grad_attn = grad_middle.astype(bf16)
    for shift in range(seq_count):
        attended = unpacked(attended_refs[shift])
        own_rows = group_rows(places_ref, -shift, seq_count, group_width)
        grads = mm_nt(grad_attn, proj_ref[own_rows, :]).astype(bf16)
        leaving_refs[shift][: rows // 2, :] = side_by_side(grads)
        grads = mm_tn(grad_attn, attended).astype(bf16)
        leaving_refs[shift][rows // 2 :, :] = side_by_side(grads)
    router_grad_ref[...] = mm_tn(grad_logits, moe_in).reshape(router_grad_ref.shape)
    small_ref[0:1, :] = jnp.sum(grad_moe_in * normed, axis=0, keepdims=True)
    small_ref[1:2, :] = jnp.sum(grad_moe_in, axis=0, keepdims=True)
    lane = lax.broadcasted_iota(jnp.int32, (1, width), 1)
    count = jnp.sum(valid, axis=0, keepdims=True) * width
    small_ref[2:3, :] = stats_ref[...] + jnp.where(lane == 3, count, 0.0)


def total_at(values, place):
    lane = lax.broadcasted_iota(jnp.int32, (1, values.shape[-1]), 1)
    by_lane = jnp.sum(values, axis=0, keepdims=True)
    return jnp.where(lane == place, jnp.sum(by_lane, axis=1, keepdims=True), 0.0)


def output_kernel(
    places_ref, middle_ref, gate_ref, route_col_ref, dest_col_ref, *refs,
    image_count, patch_rows, stride, split,
):
    value_refs = refs[:-2]
    output_ref, stats_ref = refs[-2:]
    rows, width = middle_ref.shape
    slots = EXPERTS * stride
    gate = gate_ref[...]
    expert_lane = lax.broadcasted_iota(jnp.int32, (1, EXPERTS), 1)
    slot = lax.broadcasted_iota(jnp.int32, (1, slots), 1)
    moe_out = jnp.zeros((rows, width), f32)
    tables = [table_part(value_refs, part).reshape(slots, width) for part in range(split)]
    for k in range(TOP):
        pick = (slot == dest_col_ref[:, k : k + 1]).astype(f32).astype(bf16)
        pair_value = mm(pick, tables[0])
        for table in tables[1:]:
            pair_value = pair_value + mm(pick, table)
        own = expert_lane == route_col_ref[:, k : k + 1]
        moe_out = moe_out + jnp.sum(jnp.where(own, gate, 0.0), axis=-1, keepdims=True) * pair_value
    valid = valid_rows(places_ref, image_count, patch_rows, (rows, 1), 0).astype(f32)
    total = middle_ref[...] + moe_out
    output_ref[...] = (total * valid).astype(bf16).reshape(output_ref.shape)
    stats_ref[...] = total_at(moe_out * moe_out * valid, 1) + total_at(total * total * valid, 2)


def attention_grad_kernel(
    places_ref, q_ref, k_ref, v_ref, probs_ref, normed_ref, *refs,
    group_heads, head_width, seq_count,
):
    grad_refs = refs[:seq_count]
    packed_refs = refs[seq_count : 2 * seq_count]
    slab_ref, weight_acc, grad_spread, packed_spread = refs[2 * seq_count :]
    patch_rows = grad_spread.shape[2]
    rows = grad_spread.shape[0] * patch_rows
    total_rows = q_ref.shape[1]
    group_width = group_heads * head_width
    scale = head_width ** (-0.5)

    @pl.when(pl.program_id(0) == 0)
    def _():
        for shift, grad_ref in enumerate(grad_refs):
            place = neighbour(places_ref, shift, seq_count)
            grads = stacked(grad_ref[: rows // 2, :])
            for image in range(grad_spread.shape[0]):
                grad_spread[image, place] = grads[image * patch_rows : (image + 1) * patch_rows]

    grad_heads = grad_spread[pl.program_id(0)].reshape(total_rows, group_width)
    q, k, v = q_ref[0], k_ref[0], v_ref[0]
    lane = lax.broadcasted_iota(jnp.int32, (1, group_width), 1)
    nothing = jnp.zeros_like(q)
    grad_q = jnp.zeros((total_rows, group_width), f32)
    grad_k = jnp.zeros((total_rows, group_width), f32)
    grad_v = jnp.zeros((total_rows, group_width), f32)
    for head in range(group_heads):
        in_head = (lane >= head * head_width) & (lane < (head + 1) * head_width)
        own_grad = jnp.where(in_head, grad_heads, nothing)
        probs_low = probs_ref[0, head]
        probs = probs_low.astype(f32)
        grad_probs = mm_nt(own_grad, v)
        delta = jnp.sum(probs * grad_probs, axis=-1, keepdims=True)
        grad_scores = (probs * (grad_probs - delta)).astype(bf16)
        grad_q = jnp.where(in_head, mm(grad_scores, k), grad_q)
        grad_k = jnp.where(in_head, mm_tn(grad_scores, q), grad_k)
        grad_v = jnp.where(in_head, mm_tn(probs_low, grad_heads), grad_v)
    packed = jnp.concatenate([grad_q * scale, grad_k * scale, grad_v], axis=1).astype(bf16)
    packed_spread[...] = packed.reshape(packed_spread.shape)
    for shift, packed_ref in enumerate(packed_refs):
        packed_ref[0] = packed_spread[neighbour(places_ref, shift, seq_count)]
    weight_grad = mm_tn(packed, normed_ref[0])

    @pl.when(pl.program_id(0) == 0)
    def _():
        weight_acc[...] = weight_grad

    @pl.when(pl.program_id(0) > 0)
    def _():
        weight_acc[...] += weight_grad

    @pl.when(pl.program_id(0) == pl.num_programs(0) - 1)
    def _():
        width = weight_acc.shape[1]
        proj_grad = grad_refs[0][rows // 2 :, :].astype(f32)
        for grad_ref in grad_refs[1:]:
            proj_grad = proj_grad + grad_ref[rows // 2 :, :].astype(f32)
        proj_grad = stacked(proj_grad)
        slab = jnp.concatenate([weight_acc[...], proj_grad.T], axis=0).astype(bf16)
        along, cores, chunk, _ = slab_ref.shape
        for core in range(cores):
            for at in range(along):
                start = (core * along + at) * chunk
                slab_ref[at, core] = slab[start : start + chunk]


def assemble_kernel(places_ref, *refs, seq_count):
    own_refs = refs[:seq_count]
    other_refs = refs[seq_count : 2 * seq_count]
    qkv_ref, proj_ref, slabs = refs[2 * seq_count :]
    width = proj_ref.shape[0]
    group_width = width // seq_count
    half = own_refs[0].shape[0]
    @pl.when(pl.program_id(0) == 0)
    def _():
        for shift in range(seq_count):
            group = neighbour(places_ref, -shift, seq_count)
            for places, source_ref in (
                (places_ref[2], own_refs[shift]), (1 - places_ref[2], other_refs[shift]),
            ):
                start = pl.multiple_of(places * half, 16)
                slabs[group, pl.ds(start, half), :] = source_ref[...]

    part = pl.program_id(0)
    values = slabs[:, pl.ds(pl.multiple_of(part * group_width, 16), group_width), :]
    values = values.reshape(width, width).astype(f32)

    @pl.when(part < 3)
    def _():
        qkv_ref[...] = values.T

    @pl.when(part == 3)
    def _():
        proj_ref[...] = values


def input_grad_kernel(
    places_ref, weight_ref, tokens_ref, grad_middle_ref, gain_ref, before_ref, stats_ref,
    router_ref, *refs,
):
    *packed_refs, input_grad_ref, copies_ref, small_ref = refs
    _, patch_rows, width = tokens_ref.shape
    grad = jnp.zeros((patch_rows, width), f32)
    for shift, packed_ref in enumerate(packed_refs):
        group = neighbour(places_ref, -shift, len(packed_refs))
        grad = grad + mm(packed_ref[0], weight_ref[group])
    normed, inv_root = normalize(tokens_ref[0].astype(f32))
    row_grad = norm_row_grad(grad, normed, inv_root, gain_ref[...])
    input_grad_ref[0] = (grad_middle_ref[0] + row_grad).astype(bf16)

    @pl.when(pl.program_id(0) == 0)
    def _():
        small_ref[0:2, :] = before_ref[0:2, :]
        small_ref[2:3, :] = before_ref[2:3, :] + stats_ref[...]
        small_ref[3:5, :] = jnp.zeros((2, width), f32)
        small_ref[5:8, :] = jnp.zeros((3, width), f32)
        small_ref[5:6, : router_ref.shape[-1]] = jnp.sum(router_ref[...], axis=0)

    small_ref[3:4, :] += jnp.sum(grad * normed, axis=0, keepdims=True)
    small_ref[4:5, :] += jnp.sum(grad, axis=0, keepdims=True)

    @pl.when(pl.program_id(0) == pl.num_programs(0) - 1)
    def _():
        copies_ref[...] = jnp.broadcast_to(small_ref[...][None], copies_ref.shape)


def expert_grad_kernel(*refs, row_pieces, row_blocks):
    rows_ref, cotangent_ref, first_ref, second_ref = refs[:4]
    first_grad_ref, second_grad_ref, done_ref, grad_pre_ref, hidden_ref, scaled_ref = refs[-6:]
    stride, width = rows_ref.shape[-2:]
    rows = grad_pre_ref.shape[1]

    def scale():
        share = rows // rows_ref.shape[0]
        for place in range(rows_ref.shape[0]):
            own = slice(place * share, (place + 1) * share)
            scaled_ref[own, :] = scaled_rows(rows_ref[place, :, 0], cotangent_ref[place, :, 0])

    if row_blocks == 1:
        pl.when(pl.program_id(0) == 0)(scale)
    else:
        scale()
    moe_rows = rows_ref[...].reshape(rows, width)
    piece = rows // row_pieces
    first = first_ref[...]
    second = second_ref[...]
    for at in range(row_pieces):
        own = slice(at * piece, (at + 1) * piece)
        hidden, slope = gelu_pair(mm_nt(first, moe_rows[own]))
        hidden_ref[:, own] = hidden.astype(bf16)
        grad_pre_ref[:, own] = (mm_nt(second, scaled_ref[own, :]) * slope).astype(bf16)
    if row_blocks > 1:

        @pl.when(pl.program_id(1) == 0)
        def _():
            second_grad_ref[...] = jnp.zeros(second_grad_ref.shape, f32)
            first_grad_ref[...] = jnp.zeros(first_grad_ref.shape, f32)

        second_grad_ref[...] += mm(hidden_ref[...], scaled_ref[...])
        first_grad_ref[...] += mm(grad_pre_ref[...], moe_rows)
    else:
        second_grad_ref[...] = mm(hidden_ref[...], scaled_ref[...])
        first_grad_ref[...] = mm(grad_pre_ref[...], moe_rows)
    done_ref[...] = jnp.zeros(done_ref.shape, f32)


smem = pl.BlockSpec(memory_space=pltpu.SMEM)
vmem = pl.BlockSpec(memory_space=pltpu.VMEM)
params = pltpu.CompilerParams(vmem_limit_bytes=60 * 1024 * 1024)


def cost(microseconds):
    return pl.CostEstimate(
        flops=int(microseconds * 6e8), transcendentals=0, bytes_accessed=int(microseconds * 1e5)
    )


def struct(shape, dtype):
    return jax.ShapeDtypeStruct(shape, dtype)


def per_device(
    tokens, routes, priority, hires, gain_one, shift_one, w_qkv, w_proj, gain_two, shift_two,
    w_router, expert_in, expert_out, cotangent,
):
    image_count, patch_rows, width = tokens.shape
    rows = image_count * patch_rows
    seq_count = lax.axis_size("seq")
    ep_count = lax.axis_size("ep")
    full_rows = patch_rows * seq_count
    head_width = width // HEADS
    group_heads = HEADS // seq_count
    group_width = group_heads * head_width
    local_experts = max(1, EXPERTS // ep_count)
    split = max(1, ep_count // EXPERTS)
    local_hidden = expert_in.shape[0] // local_experts
    capacity = max(2, (105 * TOP * rows + 100 * EXPERTS - 1) // (100 * EXPERTS))
    stride = (capacity + 3 + 15) // 16 * 16
    chunks = 2 if local_experts % 2 == 0 else 1
    each = local_experts // chunks
    devices = seq_count * ep_count
    seq_place = lax.axis_index("seq")
    ep_place = lax.axis_index("ep")
    places = jnp.stack([hires[0], seq_place.astype(jnp.int32), (ep_place % 2).astype(jnp.int32)])
    gain_one, shift_one, gain_two, shift_two = (
        vector.reshape(1, width) for vector in (gain_one, shift_one, gain_two, shift_two)
    )
    common = dict(image_count=image_count, patch_rows=patch_rows, stride=stride)

    def exchange(values, axis):
        return lax.all_to_all(values, axis, split_axis=0, concat_axis=0, tiled=True)

    def send_slots(chunk):
        if split > 1:
            chunk = jnp.broadcast_to(chunk[:, None], (EXPERTS, split) + chunk.shape[1:])
            chunk = chunk.reshape((ep_count,) + chunk.shape[2:])
        return exchange(chunk, "ep")

    def move(values, axis, shift):
        count = lax.axis_size(axis)
        if shift % count == 0:
            return values
        return lax.ppermute(values, axis, [(at, (at + shift) % count) for at in range(count)])

    def other_core(values):
        return lax.ppermute(values, "ep", [(at, at ^ 1) for at in range(ep_count)])

    def hold(values, *others):
        values = tuple(values)
        anywhere = pl.BlockSpec(memory_space=pl.ANY)
        return call(
            lambda *refs: None,
            "hold",
            waits=others,
            in_specs=[anywhere] * len(values),
            out_specs=[anywhere] * len(values),
            out_shape=[struct(value.shape, value.dtype) for value in values],
            input_output_aliases={at: at for at in range(len(values))},
            cost_estimate=cost(1),
        )(*values)

    def over_seq(values):
        return lax.all_gather(values, "seq", axis=0, tiled=False)

    def call(kernel, name, waits=(), **spec):
        waits = tuple(waits)

        def run(*operands):
            count = len(operands)

            def body(*refs):
                kernel(*refs[:count], *refs[count + len(waits) :])

            unread = [pl.BlockSpec(memory_space=pl.ANY)] * len(waits)
            if "grid_spec" in spec:
                grid_spec = dict(spec["grid_spec"])
                grid_spec["in_specs"] = grid_spec["in_specs"] + unread
                own = dict(spec, grid_spec=pltpu.PrefetchScalarGridSpec(**grid_spec))
            else:
                own = dict(spec, in_specs=spec["in_specs"] + unread)
            return pl.pallas_call(body, name=name, compiler_params=params, **own)(
                *operands, *waits
            )

        return run

    def slot_struct(experts):
        return struct((min(ep_count, EXPERTS), experts, stride, width), bf16)

    chunk_struct = slot_struct(each)
    moved_struct = struct((ep_count, each, stride, width), bf16)

    tokens_moved = [move(tokens, "seq", shift) for shift in range(seq_count)]
    pairs = jnp.concatenate([routes.reshape(rows, TOP).T, priority.reshape(1, rows)], axis=0)
    route_col, dest_col, dest_row = call(
        lambda *refs: routing_kernel(*refs, capacity=capacity, **common),
        "routing",
        in_specs=[smem, vmem],
        out_specs=[vmem] * 3,
        out_shape=[
            struct((rows, TOP), jnp.int32),
            struct((rows, TOP), jnp.int32),
            struct((TOP, rows), jnp.int32),
        ],
        cost_estimate=cost(3),
    )(places, pairs)
    cotangent_sent = call(
        lambda *refs: send_grads_kernel(*refs, stride=stride),
        "send_grads",
        in_specs=[vmem] * 2,
        out_specs=[vmem] * chunks,
        out_shape=[chunk_struct] * chunks,
        cost_estimate=cost(3),
    )(cotangent, dest_row)
    weight_groups = (
        w_qkv.reshape(width, 3, seq_count, group_width)
        .transpose(2, 1, 3, 0)
        .reshape(seq_count, 3 * group_width, width)
    )

    cotangent_slots = [send_slots(chunk) for chunk in cotangent_sent]

    row_block = pl.BlockSpec((1, full_rows, group_width), lambda i, *_: (i, 0, 0))
    probs_block = pl.BlockSpec((1, group_heads, full_rows, full_rows), lambda i, *_: (i, 0, 0, 0))
    normed_block = pl.BlockSpec((1, full_rows, width), lambda i, *_: (i, 0, 0))
    half_block = pl.BlockSpec((1, patch_rows // 2, 2 * group_width), lambda i, *_: (i, 0, 0))
    packed_block = pl.BlockSpec((1, patch_rows, 3 * group_width), lambda i, *_: (i, 0, 0))
    vector_block = pl.BlockSpec((1, width), lambda i, *_: (0, 0))
    image_block = pl.BlockSpec((1, patch_rows, width), lambda i, *_: (i, 0, 0))
    half_struct = struct((image_count, patch_rows // 2, 2 * group_width), bf16)
    row_struct = struct((image_count, full_rows, group_width), bf16)
    def attention(first_image, count, previous, *others):
        def own(block):
            return pl.BlockSpec(
                block.block_shape, lambda i, *rest: block.index_map(first_image + i, *rest)
            )

        inputs = 4 + seq_count
        blocks = [half_block] * seq_count + [
            row_block, row_block, row_block, probs_block, normed_block,
        ]
        return call(
            lambda *refs: attention_kernel(
                *refs[:inputs],
                *refs[inputs + len(previous) :],
                first_image=first_image,
                seq_count=seq_count,
                group_heads=group_heads,
                head_width=head_width,
            ),
            "attention",
            waits=others,
            grid_spec=dict(
                num_scalar_prefetch=1,
                grid=(count,),
                in_specs=[
                    vector_block,
                    vector_block,
                    pl.BlockSpec((1, 3 * group_width, width), lambda i, at: (at[1], 0, 0)),
                ]
                + [own(image_block)] * seq_count
                + [pl.BlockSpec(memory_space=pl.ANY)] * len(previous),
                out_specs=[own(block) for block in blocks],
                scratch_shapes=[
                    pltpu.VMEM((seq_count, patch_rows, group_width), bf16),
                    pltpu.VMEM((seq_count, patch_rows, width), bf16),
                ],
            ),
            out_shape=[half_struct] * seq_count
            + [
                row_struct,
                row_struct,
                row_struct,
                struct((image_count, group_heads, full_rows, full_rows), bf16),
                struct((image_count, full_rows, width), bf16),
            ],
            input_output_aliases={inputs + at: at for at in range(len(previous))},
            cost_estimate=cost(30),
        )(places, gain_one, shift_one, weight_groups, *tokens_moved, *previous)

    started = attention(0, 1, (), *cotangent_sent)
    (watched,) = hold([cotangent_slots[0]], started[-1])
    cotangent_slots[0] = watched
    *attended, q, k, v, probs, attn_in = attention(1, image_count - 1, started, watched)
    attended_sent = attended
    attended = [move(block, "seq", shift) for shift, block in enumerate(attended)]
    cotangent_slots[1:] = hold(cotangent_slots[1:], attended_sent[1]) if chunks > 1 else []

    middle, gate, stats, *rows_sent = call(
        lambda *refs: dispatch_kernel(*refs, seq_count=seq_count, **common),
        "dispatch",
        waits=cotangent_slots,
        in_specs=[smem] + [vmem] * (7 + seq_count),
        out_specs=[vmem] * (3 + chunks),
        out_shape=[
            struct((rows, width), f32),
            struct((rows, EXPERTS), f32),
            struct((1, width), f32),
        ]
        + [chunk_struct] * chunks,
        cost_estimate=cost(9),
    )(
        places, tokens, w_proj, gain_two, shift_two, w_router, route_col, dest_row, *attended,
    )
    row_slots = [send_slots(chunk) for chunk in rows_sent]

    hidden_tile = local_hidden // 2
    tiles = local_hidden // hidden_tile
    moved_block = pl.BlockSpec((ep_count, 1, stride, width), lambda e, f: (0, e, 0, 0))
    cotangent_all = [over_seq(slots) for slots in cotangent_slots]
    grads_back, values_back = [], ()
    for at in range(chunks):
        weight_block = pl.BlockSpec(
            (hidden_tile, width), lambda e, f, at=at: ((e + at * each) * tiles + f, 0)
        )
        all_block = pl.BlockSpec(
            (ep_count, 1, stride, width), lambda e, f, at=at: (0, e + at * each, 0, 0)
        )
        value, back = call(
            lambda *refs: expert_kernel(*refs, pieces=max(1, hidden_tile // 768)),
            "experts",
            waits=cotangent_all[:1] * (at > 0),
            grid=(each, tiles),
            in_specs=[moved_block, moved_block, weight_block, weight_block]
            + [pl.BlockSpec(memory_space=pl.ANY)] * len(values_back),
            out_specs=[all_block, moved_block],
            out_shape=[struct((ep_count, local_experts, stride, width), bf16), moved_struct],
            scratch_shapes=[pltpu.VMEM((ep_count * stride, width), f32)] * 2
            + [pltpu.VMEM((ep_count * stride, width), bf16)],
            input_output_aliases={4: 0} if values_back else {},
            cost_estimate=cost(16),
        )(row_slots[at], cotangent_slots[at], expert_in, expert_out, *values_back)
        grads_back.append(exchange(back, "ep"))
        values_back = (value,)

    all_rows = seq_count * ep_count * stride
    grad_tile = min(768, local_hidden)
    grad_tiles = local_hidden // grad_tile
    anywhere = pl.BlockSpec(memory_space=pl.ANY)
    rows_all = [over_seq(slots) for slots in row_slots]
    grads = []

    row_blocks = max(1, all_rows // 1024)
    sources = ep_count // row_blocks
    block_rows = all_rows // row_blocks

    def expert_grads(expert, begin, count, *others):
        place = expert * grad_tiles + begin
        tile_block = pl.BlockSpec((grad_tile, width), lambda f, r: (place + f, 0))

        def source_block(own):
            return pl.BlockSpec(
                (seq_count, sources, 1, stride, width),
                lambda f, r: (0, r, own, 0, 0),
                pipeline_mode=pl.Buffered(1 if row_blocks == 1 else 2),
            )

        *grads[:], done = call(
            lambda *refs: expert_grad_kernel(
                *refs, row_pieces=max(1, block_rows // 512), row_blocks=row_blocks
            ),
            "expert_grads",
            waits=others,
            grid=(count, row_blocks),
            in_specs=[source_block(expert % each)] * 2 + [tile_block, tile_block]
            + [anywhere] * len(grads),
            out_specs=[tile_block, tile_block, pl.BlockSpec((8, 128), lambda f, r: (0, 0))],
            out_shape=[
                struct(expert_in.shape, f32),
                struct(expert_out.shape, f32),
                struct((8, 128), f32),
            ],
            scratch_shapes=[pltpu.VMEM((grad_tile, block_rows), bf16)] * 2
            + [pltpu.VMEM((block_rows, width), bf16)],
            input_output_aliases={4: 0, 5: 1} if grads else {},
            cost_estimate=cost(7 * count),
        )(rows_all[expert // each], cotangent_all[expert // each], expert_in, expert_out, *grads)
        return done

    work = [(expert, 0, grad_tiles) for expert in range(local_experts)]
    work = iter(work)

    def next_grads(*others):
        return [expert_grads(*part, *others) for part in itertools.islice(work, 1)]

    early = next_grads(values_back[0], grads_back[0]) if local_experts > 3 else []
    leaving_shape = ((rows + width) // 2, 2 * group_width)
    grad_middle, router_grad, small, *leaving = call(
        lambda *refs: combine_kernel(
            *refs, split=split, seq_count=seq_count, chunks=chunks, **common
        ),
        "combine",
        waits=early,
        in_specs=[smem] + [vmem] * (10 + seq_count + chunks),
        out_specs=[vmem] * (3 + seq_count),
        out_shape=[
            struct((rows, width), f32),
            struct((EXPERTS, 1, width) if devices == EXPERTS else (EXPERTS, width), f32),
            struct((3, width), f32),
        ]
        + [struct(leaving_shape, bf16)] * seq_count,
        cost_estimate=cost(10),
    )(
        places, middle, gate, cotangent, w_proj, gain_two, shift_two, w_router,
        route_col, dest_col, stats, *attended, *grads_back,
    )
    leaving = [move(block, "seq", -at) for at, block in enumerate(leaving)]
    piece = EXPERTS * width // devices
    router_grad = exchange(router_grad.reshape(devices, 1, piece), ("seq", "ep"))
    values_moved = exchange(values_back[0], "ep")
    middle_done = next_grads(grad_middle) if local_experts > 2 else []
    half = 2 * group_width
    pairs_along = ep_count // 2
    slab_shape = (pairs_along, 2, half // pairs_along, width)
    *packed_sent, slab = call(
        lambda *refs: attention_grad_kernel(
            *refs, group_heads=group_heads, head_width=head_width, seq_count=seq_count
        ),
        "attention_grad",
        waits=middle_done,
        grid=(image_count,),
        in_specs=[smem, row_block, row_block, row_block, probs_block, normed_block]
        + [pl.BlockSpec(leaving_shape, lambda i: (0, 0))] * seq_count,
        out_specs=[packed_block] * seq_count
        + [pl.BlockSpec(slab_shape, lambda i: (0, 0, 0, 0))],
        out_shape=[struct((image_count, patch_rows, 3 * group_width), bf16)] * seq_count
        + [struct(slab_shape, bf16)],
        scratch_shapes=[
            pltpu.VMEM((3 * group_width, width), f32),
            pltpu.VMEM((image_count, seq_count, patch_rows, group_width), bf16),
            pltpu.VMEM((seq_count, patch_rows, 3 * group_width), bf16),
        ],
        cost_estimate=cost(18),
    )(places, q, k, v, probs, attn_in, *leaving)
    packed = [move(block, "seq", shift) for shift, block in enumerate(packed_sent)]

    same_core = [[2 * at + core for at in range(pairs_along)] for core in range(2)]

    def along_core(values):
        return lax.all_to_all(
            values, "ep", split_axis=0, concat_axis=0, tiled=True, axis_index_groups=same_core
        )

    slab = lax.psum_scatter(
        slab.reshape(2 * half, width), "ep", scatter_dimension=0, tiled=True
    )
    late = next_grads(packed_sent[0], router_grad) if local_experts > 1 else []
    slab, packed[1] = hold([slab, packed[1]], *late, values_moved, *packed[2:])
    slab = jnp.broadcast_to(slab[None], (pairs_along, half // pairs_along, width))
    output, value_stats = call(
        lambda *refs: output_kernel(*refs, split=split, **common),
        "output",
        waits=[slab],
        in_specs=[smem] + [vmem] * 5,
        out_specs=[vmem] * 2,
        out_shape=[struct((image_count, patch_rows, width), bf16), struct((1, width), f32)],
        cost_estimate=cost(5),
    )(places, middle, gate, route_col, dest_col, values_moved)
    slab_moved = along_core(slab).reshape(half, width)
    own_slabs = [move(slab_moved, "seq", shift) for shift in range(seq_count)]
    input_grad, copies = call(
        input_grad_kernel,
        "input_grad",
        grid=(image_count,),
        in_specs=[
            smem,
            pl.BlockSpec((seq_count, 3 * group_width, width), lambda i: (0, 0, 0)),
            image_block,
            image_block,
            vector_block,
            pl.BlockSpec((3, width), lambda i: (0, 0)),
            pl.BlockSpec((1, width), lambda i: (0, 0)),
            pl.BlockSpec((devices, 1, piece), lambda i: (0, 0, 0)),
        ]
        + [packed_block] * seq_count,
        out_specs=[image_block, pl.BlockSpec((devices, 8, width), lambda i: (0, 0, 0))],
        out_shape=[
            struct((image_count, patch_rows, width), bf16),
            struct((devices, 8, width), f32),
        ],
        scratch_shapes=[pltpu.VMEM((8, width), f32)],
        cost_estimate=cost(7),
    )(
        places, weight_groups, tokens, grad_middle.reshape(image_count, patch_rows, width),
        gain_one, small, value_stats, router_grad, *packed,
    )
    own_slabs = hold(own_slabs, *next_grads(input_grad, slab_moved))
    other_slabs = [other_core(each_slab) for each_slab in own_slabs]
    qkv_grad, proj_grad = call(
        lambda *refs: assemble_kernel(*refs, seq_count=seq_count),
        "assemble",
        grid=(4,),
        in_specs=[smem] + [pl.BlockSpec((half, width), lambda i: (0, 0))] * (2 * seq_count),
        out_specs=[
            pl.BlockSpec((width, width), lambda i: (0, jnp.minimum(i, 2))),
            pl.BlockSpec((width, width), lambda i: (0, 0)),
        ],
        out_shape=[struct((width, 3 * width), f32), struct((width, width), f32)],
        scratch_shapes=[pltpu.VMEM((seq_count, 2 * half, width), bf16)],
        cost_estimate=cost(8),
    )(places, *own_slabs, *other_slabs)

    copies = exchange(copies, ("seq", "ep"))
    sums = jnp.sum(copies[:, :5], axis=0)
    router_grad = copies[:, 5, :piece].reshape(EXPERTS, width).T
    return (
        output,
        input_grad,
        sums[3],
        sums[4],
        qkv_grad,
        proj_grad,
        sums[0],
        sums[1],
        router_grad,
        grads[0],
        grads[1],
        jnp.sqrt(sums[2, :3] / sums[2, 3]),
    )


def solution(mesh):
    in_specs = (
        P("ep", "seq", None),
        P("ep", "seq", None),
        P("ep", "seq"),
        P("ep"),
        P(),
        P(),
        P(),
        P(),
        P(),
        P(),
        P(),
        P("ep", None),
        P("ep", None),
        P("ep", "seq", None),
    )
    out_specs = (
        P("ep", "seq", None),
        P("ep", "seq", None),
        P(),
        P(),
        P(),
        P(),
        P(),
        P(),
        P(),
        P("ep", None),
        P("ep", None),
        P(),
    )
    return jax.shard_map(
        per_device, mesh=mesh, in_specs=in_specs, out_specs=out_specs, check_vma=False
    )
```

```python
import itertools

import jax
import jax.numpy as jnp
from jax import lax
from jax.experimental import pallas as pl
from jax.experimental.pallas import tpu as pltpu
from jax.sharding import PartitionSpec as P

HEADS = 12
EXPERTS = 32
TOP = 2
PATCHES = 576
SHORT = 196

norm_eps = 1e-06
neg_big = -1e30
f32 = jnp.float32
bf16 = jnp.bfloat16

tail_slope = 0.33
tail_terms = (
    0.18635779800457905,
    0.18295602991113566,
    0.2012232872944192,
    0.04722279904104141,
    0.40849559831839843,
    -0.3511445702318978,
    0.46023391759858995,
    -0.13534486747679436,
)


def mm(a, b):
    return lax.dot_general(a, b, (((1,), (0,)), ((), ())), preferred_element_type=f32)


def mm_nt(a, b):
    return lax.dot_general(a, b, (((1,), (1,)), ((), ())), preferred_element_type=f32)


def mm_tn(a, b):
    return lax.dot_general(a, b, (((0,), (0,)), ((), ())), preferred_element_type=f32)


def gelu_pair(v):
    size = jnp.abs(v)
    bell = jnp.exp(v * v * -0.5)
    t = 1.0 / (1.0 + size * (tail_slope * 0.7071067811865476))
    poly = tail_terms[-1] * 0.5
    for term in tail_terms[-2::-1]:
        poly = poly * t + term * 0.5
    tail = poly * t * bell
    cdf = jnp.where(v >= 0.0, 1.0 - tail, tail)
    return v * cdf, cdf + v * bell * 0.3989422804014327


def normalize(values):
    centred = values - jnp.mean(values, axis=-1, keepdims=True)
    inv_root = lax.rsqrt(jnp.mean(centred * centred, axis=-1, keepdims=True) + norm_eps)
    return centred * inv_root, inv_root


def norm_row_grad(upstream, normed, inv_root, gain):
    scaled = upstream * gain
    return inv_root * (
        scaled
        - jnp.mean(scaled, axis=-1, keepdims=True)
        - normed * jnp.mean(scaled * normed, axis=-1, keepdims=True)
    )


def valid_rows(places_ref, image_count, patch_rows, shape, axis):
    row = lax.broadcasted_iota(jnp.int32, shape, axis)
    first_patch = places_ref[1] * patch_rows
    valid = row < 0
    for image in range(image_count):
        length = jnp.where(image < places_ref[0], PATCHES, SHORT)
        start = image * patch_rows
        stop = start + jnp.clip(length - first_patch, 0, patch_rows)
        valid = valid | ((row >= start) & (row < stop))
    return valid


def routing_kernel(
    places_ref, pairs_ref, route_col_ref, dest_col_ref, dest_row_ref,
    *, image_count, patch_rows, capacity, stride,
):
    rows = pairs_ref.shape[1]
    eye = lax.broadcasted_iota(jnp.int32, (rows, rows), 0) == lax.broadcasted_iota(
        jnp.int32, (rows, rows), 1
    )

    def as_column(line):
        return jnp.sum(jnp.where(eye, line.astype(f32), 0.0), axis=1, keepdims=True).astype(
            jnp.int32
        )

    e_row = [pairs_ref[k : k + 1, :] for k in range(TOP)]
    e_col = [as_column(line) for line in e_row]
    prio_row = pairs_ref[TOP : TOP + 1, :]
    prio_col = as_column(prio_row)
    for k in range(TOP):
        route_col_ref[:, k : k + 1] = e_col[k]
    valid_col = valid_rows(places_ref, image_count, patch_rows, (rows, 1), 0)
    valid_row = valid_rows(places_ref, image_count, patch_rows, (1, rows), 1)
    weight_col = valid_col.astype(f32)
    weight_row = valid_row.astype(f32)
    row_first = (prio_row < prio_col).astype(f32) * weight_row
    col_first = (prio_col < prio_row).astype(f32) * weight_col
    for k in range(TOP):
        count = jnp.where(e_col[k] == e_row[k], row_first, 0.0)
        for earlier in range(k):
            count = count + jnp.where(e_col[k] == e_row[earlier], weight_row, 0.0)
        slot = jnp.sum(count, axis=1, keepdims=True).astype(jnp.int32)
        keep = valid_col & (slot < capacity)
        dest_col_ref[:, k : k + 1] = jnp.where(keep, e_col[k] * stride + slot, -1)
        count = jnp.where(e_col[k] == e_row[k], col_first, 0.0)
        for earlier in range(k):
            count = count + jnp.where(e_col[earlier] == e_row[k], weight_col, 0.0)
        slot = jnp.sum(count, axis=0, keepdims=True).astype(jnp.int32)
        keep = valid_row & (slot < capacity)
        dest_row_ref[k : k + 1, :] = jnp.where(keep, e_row[k] * stride + slot, -1)


def side_by_side(values):
    half = values.shape[0] // 2
    return jnp.concatenate([values[:half], values[half:]], axis=1)


def stacked(values):
    width = values.shape[1] // 2
    return jnp.concatenate([values[:, :width], values[:, width:]], axis=0)


def neighbour(places_ref, shift, seq_count):
    return (places_ref[1] + (shift + seq_count)) % seq_count


def attention_kernel(
    places_ref, gain_ref, shift_ref, weight_ref, *refs,
    first_image, seq_count, group_heads, head_width,
):
    tokens_refs = refs[:seq_count]
    attended_refs = refs[seq_count : 2 * seq_count]
    q_ref, k_ref, v_ref, probs_ref, normed_ref, spread_ref, tokens_ref = refs[2 * seq_count :]
    _, patch_rows, width = tokens_refs[0].shape
    for shift, source_ref in enumerate(tokens_refs):
        tokens_ref[neighbour(places_ref, -shift, seq_count)] = source_ref[0]
    total_rows = seq_count * patch_rows
    group_width = group_heads * head_width
    values = tokens_ref[...].reshape(total_rows, width).astype(f32)
    normed, _ = normalize(values)
    attn_in = (normed * gain_ref[...] + shift_ref[...]).astype(bf16)
    normed_ref[0] = attn_in
    q, k, v = (
        mm_nt(attn_in, weight_ref[0, part * group_width : (part + 1) * group_width, :]).astype(bf16)
        for part in range(3)
    )
    q_ref[0] = q
    k_ref[0] = k
    v_ref[0] = v
    length = jnp.where(first_image + pl.program_id(0) < places_ref[0], PATCHES, SHORT)
    key_valid = lax.broadcasted_iota(jnp.int32, (1, total_rows), 1) < length
    lane = lax.broadcasted_iota(jnp.int32, (1, group_width), 1)
    scaled_q = (q.astype(f32) * head_width ** (-0.5)).astype(bf16)
    attended = jnp.zeros((total_rows, group_width), f32)
    for head in range(group_heads):
        in_head = (lane >= head * head_width) & (lane < (head + 1) * head_width)
        scores = mm_nt(jnp.where(in_head, scaled_q, jnp.zeros_like(scaled_q)), k)
        scores = jnp.where(key_valid, scores, neg_big)
        exp_scores = jnp.exp(scores - jnp.max(scores, axis=-1, keepdims=True))
        inverse = 1.0 / jnp.sum(exp_scores, axis=-1, keepdims=True)
        probs = (exp_scores * inverse).astype(bf16)
        probs_ref[0, head] = probs
        attended = jnp.where(in_head, mm(probs, v), attended)
    spread_ref[...] = attended.astype(bf16).reshape(spread_ref.shape)
    for shift, attended_ref in enumerate(attended_refs):
        attended_ref[0] = side_by_side(spread_ref[neighbour(places_ref, shift, seq_count)])


def slot_picks(dest_row_ref, stride, k):
    slot = lax.broadcasted_iota(jnp.int32, (EXPERTS * stride, 1), 0)
    return (slot == dest_row_ref[k : k + 1, :]).astype(f32).astype(bf16)


def send_grads_kernel(cotangent_ref, dest_row_ref, *sent_refs, stride):
    width = cotangent_ref.shape[-1]
    cotangent = cotangent_ref[...].reshape(-1, width)
    pick = slot_picks(dest_row_ref, stride, 0)
    for k in range(1, TOP):
        pick = pick + slot_picks(dest_row_ref, stride, k)
    sent = mm(pick, cotangent).astype(bf16)
    store_chunks(sent_refs, sent, stride)


def store_chunks(chunk_refs, table, stride):
    width = table.shape[-1]
    targets, each = chunk_refs[0].shape[:2]
    grouped = table.reshape(targets, len(chunk_refs) * each, stride, width)
    for at, chunk_ref in enumerate(chunk_refs):
        chunk_ref[...] = grouped[:, at * each : (at + 1) * each]


def three_terms(values):
    high = values.astype(bf16)
    rest = values - high.astype(f32)
    middle = rest.astype(bf16)
    return high, middle, (rest - middle.astype(f32)).astype(bf16)


def diagonal(stride):
    row = lax.broadcasted_iota(jnp.int32, (1, stride, stride), 1)
    return row == lax.broadcasted_iota(jnp.int32, (1, stride, stride), 2)


def row_scalars(block, stride):
    spare = block[:, stride - 3 : stride, :stride].astype(f32)
    line = spare[:, 0:1] + spare[:, 1:2] + spare[:, 2:3]
    return jnp.sum(jnp.where(diagonal(stride), line, 0.0), axis=2, keepdims=True)


def with_scalars(block, column, stride):
    width = block.shape[-1]
    line = jnp.sum(jnp.where(diagonal(stride), column, 0.0), axis=1, keepdims=True)
    line = jnp.concatenate(
        [line, jnp.zeros((line.shape[0], 1, width - stride), f32)], axis=2
    )
    row = lax.broadcasted_iota(jnp.int32, (1, stride, 1), 1)
    for at, term in enumerate(three_terms(line)):
        block = jnp.where(row == stride - 3 + at, term.astype(f32), block)
    return block


def unpacked(blocks_ref):
    return jnp.concatenate([stacked(blocks_ref[at]) for at in range(blocks_ref.shape[0])], axis=0)


def group_rows(places_ref, shift, seq_count, group_width):
    start = neighbour(places_ref, shift, seq_count) * group_width
    return pl.ds(pl.multiple_of(start, 16), group_width)


def dispatch_kernel(
    places_ref, tokens_ref, proj_ref, gain_ref, shift_ref,
    router_ref, route_col_ref, dest_row_ref, *refs, image_count, patch_rows, stride, seq_count,
):
    attended_refs = refs[:seq_count]
    middle_ref, gate_ref, stats_ref, *sent_refs = refs[seq_count:]
    rows, width = middle_ref.shape
    group_width = attended_refs[0].shape[-1] // 2
    attn_out = jnp.zeros((rows, width), f32)
    for shift, attended_ref in enumerate(attended_refs):
        attn_out = attn_out + mm(
            unpacked(attended_ref),
            proj_ref[group_rows(places_ref, -shift, seq_count, group_width), :],
        )
    valid = valid_rows(places_ref, image_count, patch_rows, (rows, 1), 0).astype(f32)
    stats_ref[...] = total_at(attn_out * attn_out * valid, 0)
    middle = tokens_ref[...].reshape(rows, width).astype(f32) + attn_out
    middle_ref[...] = middle
    normed, _ = normalize(middle)
    moe_in = (normed * gain_ref[...] + shift_ref[...]).astype(bf16)
    logits = mm(moe_in, router_ref[...])
    exp_logits = jnp.exp(logits - jnp.max(logits, axis=-1, keepdims=True))
    gate = exp_logits / jnp.sum(exp_logits, axis=-1, keepdims=True)
    gate_ref[...] = gate
    expert_lane = lax.broadcasted_iota(jnp.int32, (1, EXPERTS), 1)
    pick_any = jnp.zeros((EXPERTS * stride, rows), bf16)
    slot_gate = jnp.zeros((EXPERTS * stride, 128), f32)
    for k in range(TOP):
        chosen = jnp.sum(
            jnp.where(expert_lane == route_col_ref[:, k : k + 1], gate, 0.0),
            axis=-1,
            keepdims=True,
        )
        pick = slot_picks(dest_row_ref, stride, k)
        pick_any = pick_any + pick
        lane = lax.broadcasted_iota(jnp.int32, (1, 128), 1)
        terms = jnp.zeros((rows, 128), f32)
        for at, term in enumerate(three_terms(jnp.broadcast_to(chosen, (rows, 128)))):
            terms = jnp.where(lane == at, term.astype(f32), terms)
        slot_gate = slot_gate + mm(pick, terms.astype(bf16))
    sent = mm(pick_any, moe_in).reshape(EXPERTS, stride, width)
    slot_gate = jnp.sum(slot_gate, axis=1, keepdims=True).reshape(EXPERTS, stride, 1)
    sent = with_scalars(sent, slot_gate, stride).astype(bf16)
    store_chunks(sent_refs, sent.reshape(EXPERTS * stride, width), stride)


def scaled_rows(rows_block, grads_block):
    groups, stride, width = rows_block.shape
    scale = row_scalars(rows_block, stride)
    return (grads_block.astype(f32) * scale).astype(bf16).reshape(groups * stride, width)


def expert_kernel(
    rows_ref, cotangent_ref, first_ref, second_ref, *refs, pieces,
):
    value_ref, back_ref, value_acc, grad_acc, scaled_ref = refs[-5:]
    count, _, stride, width = rows_ref.shape
    rows = count * stride
    piece = first_ref.shape[0] // pieces
    step = pl.program_id(1)

    @pl.when(step == 0)
    def _():
        scaled_ref[...] = scaled_rows(rows_ref[:, 0], cotangent_ref[:, 0])

    moe_rows = rows_ref[:, 0].reshape(rows, width)
    grad_rows = scaled_ref[...]
    value = jnp.zeros((rows, width), f32)
    grad = jnp.zeros((rows, width), f32)
    for at in range(pieces):
        first = first_ref[at * piece : (at + 1) * piece, :]
        second = second_ref[at * piece : (at + 1) * piece, :]
        hidden, slope = gelu_pair(mm_nt(moe_rows, first))
        grad_pre = (mm_nt(grad_rows, second) * slope).astype(bf16)
        value = value + mm(hidden.astype(bf16), second)
        grad = grad + mm(grad_pre, first)

    @pl.when(step == 0)
    def _():
        value_acc[...] = value
        grad_acc[...] = grad

    @pl.when(step > 0)
    def _():
        value_acc[...] += value
        grad_acc[...] += grad

    @pl.when(step == pl.num_programs(1) - 1)
    def _():
        value_low = value_acc[...].astype(bf16).reshape(count, stride, width)
        value_ref[:, 0] = value_low
        gate_grad = jnp.sum(
            cotangent_ref[:, 0].astype(f32) * value_low.astype(f32), axis=-1, keepdims=True
        )
        grad_low = grad_acc[...].reshape(count, stride, width)
        back_ref[:, 0] = with_scalars(grad_low, gate_grad, stride).astype(bf16)


def table_part(chunk_refs, part):
    split = chunk_refs[0].shape[0] * chunk_refs[0].shape[1] * len(chunk_refs) // EXPERTS
    pieces = []
    for chunk_ref in chunk_refs:
        sources, each, stride, width = chunk_ref.shape
        block = chunk_ref[...].reshape(sources // split, split, each, stride, width)
        pieces.append(block[:, part])
    table = pieces[0] if len(pieces) == 1 else jnp.concatenate(pieces, axis=1)
    return table.reshape(EXPERTS, table.shape[2], table.shape[3])


def combine_kernel(
    places_ref, middle_ref, gate_ref, cotangent_ref, proj_ref, gain_ref,
    shift_ref, router_ref, route_col_ref, dest_col_ref, stats_ref, *refs,
    image_count, patch_rows, stride, split, seq_count, chunks,
):
    attended_refs = refs[:seq_count]
    back_refs = refs[seq_count : seq_count + chunks]
    grad_middle_ref, router_grad_ref, small_ref = refs[seq_count + chunks :][:3]
    leaving_refs = refs[seq_count + chunks + 3 :]
    rows, width = middle_ref.shape
    group_width = attended_refs[0].shape[-1] // 2
    slots = EXPERTS * stride
    middle = middle_ref[...]
    gate = gate_ref[...]
    valid = valid_rows(places_ref, image_count, patch_rows, (rows, 1), 0).astype(f32)
    grad_total = cotangent_ref[...].reshape(rows, width).astype(f32) * valid
    expert_lane = lax.broadcasted_iota(jnp.int32, (1, EXPERTS), 1)
    slot_lane = lax.broadcasted_iota(jnp.int32, (1, stride), 1)
    slot = lax.broadcasted_iota(jnp.int32, (1, slots), 1)
    pick_any = jnp.zeros((rows, slots), bf16)
    for k in range(TOP):
        pick_any = pick_any + (slot == dest_col_ref[:, k : k + 1]).astype(f32).astype(bf16)
    grad_dispatch = jnp.zeros((rows, width), f32)
    scalar_rows = [jnp.zeros((rows, stride), f32) for _ in range(TOP)]
    own = [
        (expert_lane == route_col_ref[:, k : k + 1]).astype(f32).astype(bf16) for k in range(TOP)
    ]
    for part in range(split):
        table = table_part(back_refs, part)
        grad_dispatch = grad_dispatch + mm(pick_any, table.reshape(slots, width))
        for at in range(stride - 3, stride):
            line = table[:, at, :stride]
            for k in range(TOP):
                scalar_rows[k] = scalar_rows[k] + mm(own[k], line)
    grad_probs = jnp.zeros((rows, EXPERTS), f32)
    for k in range(TOP):
        place = dest_col_ref[:, k : k + 1] - route_col_ref[:, k : k + 1] * stride
        grad_gate = jnp.sum(
            jnp.where(slot_lane == place, scalar_rows[k], 0.0), axis=-1, keepdims=True
        )
        grad_probs = grad_probs + own[k].astype(f32) * grad_gate
    grad_logits = (
        gate * (grad_probs - jnp.sum(grad_probs * gate, axis=-1, keepdims=True))
    ).astype(bf16)
    grad_moe_in = grad_dispatch + mm_nt(grad_logits, router_ref[...])
    normed, inv_root = normalize(middle)
    moe_in = (normed * gain_ref[...] + shift_ref[...]).astype(bf16)
    grad_middle = grad_total + norm_row_grad(grad_moe_in, normed, inv_root, gain_ref[...])
    grad_middle_ref[...] = grad_middle
    grad_attn = grad_middle.astype(bf16)
    for shift in range(seq_count):
        attended = unpacked(attended_refs[shift])
        own_rows = group_rows(places_ref, -shift, seq_count, group_width)
        grads = mm_nt(grad_attn, proj_ref[own_rows, :]).astype(bf16)
        leaving_refs[shift][: rows // 2, :] = side_by_side(grads)
        grads = mm_tn(grad_attn, attended).astype(bf16)
        leaving_refs[shift][rows // 2 :, :] = side_by_side(grads)
    router_grad_ref[...] = mm_tn(grad_logits, moe_in).reshape(router_grad_ref.shape)
    small_ref[0:1, :] = jnp.sum(grad_moe_in * normed, axis=0, keepdims=True)
    small_ref[1:2, :] = jnp.sum(grad_moe_in, axis=0, keepdims=True)
    lane = lax.broadcasted_iota(jnp.int32, (1, width), 1)
    count = jnp.sum(valid, axis=0, keepdims=True) * width
    small_ref[2:3, :] = stats_ref[...] + jnp.where(lane == 3, count, 0.0)


def total_at(values, place):
    lane = lax.broadcasted_iota(jnp.int32, (1, values.shape[-1]), 1)
    by_lane = jnp.sum(values, axis=0, keepdims=True)
    return jnp.where(lane == place, jnp.sum(by_lane, axis=1, keepdims=True), 0.0)


def output_kernel(
    places_ref, middle_ref, gate_ref, route_col_ref, dest_col_ref, *refs,
    image_count, patch_rows, stride, split,
):
    value_refs = refs[:-2]
    output_ref, stats_ref = refs[-2:]
    rows, width = middle_ref.shape
    slots = EXPERTS * stride
    gate = gate_ref[...]
    expert_lane = lax.broadcasted_iota(jnp.int32, (1, EXPERTS), 1)
    slot = lax.broadcasted_iota(jnp.int32, (1, slots), 1)
    moe_out = jnp.zeros((rows, width), f32)
    tables = [table_part(value_refs, part).reshape(slots, width) for part in range(split)]
    for k in range(TOP):
        pick = (slot == dest_col_ref[:, k : k + 1]).astype(f32).astype(bf16)
        pair_value = mm(pick, tables[0])
        for table in tables[1:]:
            pair_value = pair_value + mm(pick, table)
        own = expert_lane == route_col_ref[:, k : k + 1]
        moe_out = moe_out + jnp.sum(jnp.where(own, gate, 0.0), axis=-1, keepdims=True) * pair_value
    valid = valid_rows(places_ref, image_count, patch_rows, (rows, 1), 0).astype(f32)
    total = middle_ref[...] + moe_out
    output_ref[...] = (total * valid).astype(bf16).reshape(output_ref.shape)
    stats_ref[...] = total_at(moe_out * moe_out * valid, 1) + total_at(total * total * valid, 2)


def attention_grad_kernel(
    places_ref, q_ref, k_ref, v_ref, probs_ref, normed_ref, *refs,
    group_heads, head_width, seq_count,
):
    grad_refs = refs[:seq_count]
    packed_refs = refs[seq_count : 2 * seq_count]
    slab_ref, weight_acc, grad_spread, packed_spread = refs[2 * seq_count :]
    patch_rows = grad_spread.shape[2]
    rows = grad_spread.shape[0] * patch_rows
    total_rows = q_ref.shape[1]
    group_width = group_heads * head_width
    scale = head_width ** (-0.5)

    @pl.when(pl.program_id(0) == 0)
    def _():
        for shift, grad_ref in enumerate(grad_refs):
            place = neighbour(places_ref, shift, seq_count)
            grads = stacked(grad_ref[: rows // 2, :])
            for image in range(grad_spread.shape[0]):
                grad_spread[image, place] = grads[image * patch_rows : (image + 1) * patch_rows]

    grad_heads = grad_spread[pl.program_id(0)].reshape(total_rows, group_width)
    q, k, v = q_ref[0], k_ref[0], v_ref[0]
    lane = lax.broadcasted_iota(jnp.int32, (1, group_width), 1)
    nothing = jnp.zeros_like(q)
    grad_q = jnp.zeros((total_rows, group_width), f32)
    grad_k = jnp.zeros((total_rows, group_width), f32)
    grad_v = jnp.zeros((total_rows, group_width), f32)
    for head in range(group_heads):
        in_head = (lane >= head * head_width) & (lane < (head + 1) * head_width)
        own_grad = jnp.where(in_head, grad_heads, nothing)
        probs_low = probs_ref[0, head]
        probs = probs_low.astype(f32)
        grad_probs = mm_nt(own_grad, v)
        delta = jnp.sum(probs * grad_probs, axis=-1, keepdims=True)
        grad_scores = (probs * (grad_probs - delta)).astype(bf16)
        grad_q = jnp.where(in_head, mm(grad_scores, k), grad_q)
        grad_k = jnp.where(in_head, mm_tn(grad_scores, q), grad_k)
        grad_v = jnp.where(in_head, mm_tn(probs_low, grad_heads), grad_v)
    packed = jnp.concatenate([grad_q * scale, grad_k * scale, grad_v], axis=1).astype(bf16)
    packed_spread[...] = packed.reshape(packed_spread.shape)
    for shift, packed_ref in enumerate(packed_refs):
        packed_ref[0] = packed_spread[neighbour(places_ref, shift, seq_count)]
    weight_grad = mm_tn(packed, normed_ref[0])

    @pl.when(pl.program_id(0) == 0)
    def _():
        weight_acc[...] = weight_grad

    @pl.when(pl.program_id(0) > 0)
    def _():
        weight_acc[...] += weight_grad

    @pl.when(pl.program_id(0) == pl.num_programs(0) - 1)
    def _():
        width = weight_acc.shape[1]
        proj_grad = grad_refs[0][rows // 2 :, :].astype(f32)
        for grad_ref in grad_refs[1:]:
            proj_grad = proj_grad + grad_ref[rows // 2 :, :].astype(f32)
        proj_grad = stacked(proj_grad)
        slab = jnp.concatenate([weight_acc[...], proj_grad.T], axis=0).astype(bf16)
        along, cores, chunk, _ = slab_ref.shape
        for core in range(cores):
            for at in range(along):
                start = (core * along + at) * chunk
                slab_ref[at, core] = slab[start : start + chunk]


def assemble_kernel(places_ref, *refs, seq_count):
    own_refs = refs[:seq_count]
    other_refs = refs[seq_count : 2 * seq_count]
    qkv_ref, proj_ref, slabs = refs[2 * seq_count :]
    width = proj_ref.shape[0]
    group_width = width // seq_count
    half = own_refs[0].shape[0]
    @pl.when(pl.program_id(0) == 0)
    def _():
        for shift in range(seq_count):
            group = neighbour(places_ref, -shift, seq_count)
            for places, source_ref in (
                (places_ref[2], own_refs[shift]), (1 - places_ref[2], other_refs[shift]),
            ):
                start = pl.multiple_of(places * half, 16)
                slabs[group, pl.ds(start, half), :] = source_ref[...]

    part = pl.program_id(0)
    values = slabs[:, pl.ds(pl.multiple_of(part * group_width, 16), group_width), :]
    values = values.reshape(width, width).astype(f32)

    @pl.when(part < 3)
    def _():
        qkv_ref[...] = values.T

    @pl.when(part == 3)
    def _():
        proj_ref[...] = values


def input_grad_kernel(
    places_ref, weight_ref, tokens_ref, grad_middle_ref, gain_ref, before_ref, stats_ref,
    router_ref, *refs,
):
    *packed_refs, input_grad_ref, copies_ref, small_ref = refs
    _, patch_rows, width = tokens_ref.shape
    grad = jnp.zeros((patch_rows, width), f32)
    for shift, packed_ref in enumerate(packed_refs):
        group = neighbour(places_ref, -shift, len(packed_refs))
        grad = grad + mm(packed_ref[0], weight_ref[group])
    normed, inv_root = normalize(tokens_ref[0].astype(f32))
    row_grad = norm_row_grad(grad, normed, inv_root, gain_ref[...])
    input_grad_ref[0] = (grad_middle_ref[0] + row_grad).astype(bf16)

    @pl.when(pl.program_id(0) == 0)
    def _():
        small_ref[0:2, :] = before_ref[0:2, :]
        small_ref[2:3, :] = before_ref[2:3, :] + stats_ref[...]
        small_ref[3:5, :] = jnp.zeros((2, width), f32)
        small_ref[5:8, :] = jnp.zeros((3, width), f32)
        small_ref[5:6, : router_ref.shape[-1]] = jnp.sum(router_ref[...], axis=0)

    small_ref[3:4, :] += jnp.sum(grad * normed, axis=0, keepdims=True)
    small_ref[4:5, :] += jnp.sum(grad, axis=0, keepdims=True)

    @pl.when(pl.program_id(0) == pl.num_programs(0) - 1)
    def _():
        copies_ref[...] = jnp.broadcast_to(small_ref[...][None], copies_ref.shape)


def expert_grad_kernel(*refs, row_pieces, row_blocks):
    rows_ref, cotangent_ref, first_ref, second_ref = refs[:4]
    first_grad_ref, second_grad_ref, done_ref, grad_pre_ref, hidden_ref, scaled_ref = refs[-6:]
    stride, width = rows_ref.shape[-2:]
    rows = grad_pre_ref.shape[1]

    def scale():
        share = rows // rows_ref.shape[0]
        for place in range(rows_ref.shape[0]):
            own = slice(place * share, (place + 1) * share)
            scaled_ref[own, :] = scaled_rows(rows_ref[place, :, 0], cotangent_ref[place, :, 0])

    if row_blocks == 1:
        pl.when(pl.program_id(0) == 0)(scale)
    else:
        scale()
    moe_rows = rows_ref[...].reshape(rows, width)
    piece = rows // row_pieces
    first = first_ref[...]
    second = second_ref[...]
    for at in range(row_pieces):
        own = slice(at * piece, (at + 1) * piece)
        hidden, slope = gelu_pair(mm_nt(first, moe_rows[own]))
        hidden_ref[:, own] = hidden.astype(bf16)
        grad_pre_ref[:, own] = (mm_nt(second, scaled_ref[own, :]) * slope).astype(bf16)
    if row_blocks > 1:

        @pl.when(pl.program_id(1) == 0)
        def _():
            second_grad_ref[...] = jnp.zeros(second_grad_ref.shape, f32)
            first_grad_ref[...] = jnp.zeros(first_grad_ref.shape, f32)

        second_grad_ref[...] += mm(hidden_ref[...], scaled_ref[...])
        first_grad_ref[...] += mm(grad_pre_ref[...], moe_rows)
    else:
        second_grad_ref[...] = mm(hidden_ref[...], scaled_ref[...])
        first_grad_ref[...] = mm(grad_pre_ref[...], moe_rows)
    done_ref[...] = jnp.zeros(done_ref.shape, f32)


smem = pl.BlockSpec(memory_space=pltpu.SMEM)
vmem = pl.BlockSpec(memory_space=pltpu.VMEM)
params = pltpu.CompilerParams(vmem_limit_bytes=60 * 1024 * 1024)


def cost(microseconds):
    return pl.CostEstimate(
        flops=int(microseconds * 6e8), transcendentals=0, bytes_accessed=int(microseconds * 1e5)
    )


def struct(shape, dtype):
    return jax.ShapeDtypeStruct(shape, dtype)


def per_device(
    tokens, routes, priority, hires, gain_one, shift_one, w_qkv, w_proj, gain_two, shift_two,
    w_router, expert_in, expert_out, cotangent,
):
    image_count, patch_rows, width = tokens.shape
    rows = image_count * patch_rows
    seq_count = lax.axis_size("seq")
    ep_count = lax.axis_size("ep")
    full_rows = patch_rows * seq_count
    head_width = width // HEADS
    group_heads = HEADS // seq_count
    group_width = group_heads * head_width
    local_experts = max(1, EXPERTS // ep_count)
    split = max(1, ep_count // EXPERTS)
    local_hidden = expert_in.shape[0] // local_experts
    capacity = max(2, (105 * TOP * rows + 100 * EXPERTS - 1) // (100 * EXPERTS))
    stride = (capacity + 3 + 15) // 16 * 16
    chunks = 2 if local_experts % 2 == 0 else 1
    each = local_experts // chunks
    devices = seq_count * ep_count
    seq_place = lax.axis_index("seq")
    ep_place = lax.axis_index("ep")
    places = jnp.stack([hires[0], seq_place.astype(jnp.int32), (ep_place % 2).astype(jnp.int32)])
    gain_one, shift_one, gain_two, shift_two = (
        vector.reshape(1, width) for vector in (gain_one, shift_one, gain_two, shift_two)
    )
    common = dict(image_count=image_count, patch_rows=patch_rows, stride=stride)

    def exchange(values, axis):
        return lax.all_to_all(values, axis, split_axis=0, concat_axis=0, tiled=True)

    def send_slots(chunk):
        if split > 1:
            chunk = jnp.broadcast_to(chunk[:, None], (EXPERTS, split) + chunk.shape[1:])
            chunk = chunk.reshape((ep_count,) + chunk.shape[2:])
        return exchange(chunk, "ep")

    def move(values, axis, shift):
        count = lax.axis_size(axis)
        if shift % count == 0:
            return values
        return lax.ppermute(values, axis, [(at, (at + shift) % count) for at in range(count)])

    def other_core(values):
        return lax.ppermute(values, "ep", [(at, at ^ 1) for at in range(ep_count)])

    def hold(values, *others):
        values = tuple(values)
        anywhere = pl.BlockSpec(memory_space=pl.ANY)
        return call(
            lambda *refs: None,
            "hold",
            waits=others,
            in_specs=[anywhere] * len(values),
            out_specs=[anywhere] * len(values),
            out_shape=[struct(value.shape, value.dtype) for value in values],
            input_output_aliases={at: at for at in range(len(values))},
            cost_estimate=cost(1),
        )(*values)

    def over_seq(values):
        return lax.all_gather(values, "seq", axis=0, tiled=False)

    def call(kernel, name, waits=(), **spec):
        waits = tuple(waits)

        def run(*operands):
            count = len(operands)

            def body(*refs):
                kernel(*refs[:count], *refs[count + len(waits) :])

            unread = [pl.BlockSpec(memory_space=pl.ANY)] * len(waits)
            if "grid_spec" in spec:
                grid_spec = dict(spec["grid_spec"])
                grid_spec["in_specs"] = grid_spec["in_specs"] + unread
                own = dict(spec, grid_spec=pltpu.PrefetchScalarGridSpec(**grid_spec))
            else:
                own = dict(spec, in_specs=spec["in_specs"] + unread)
            return pl.pallas_call(body, name=name, compiler_params=params, **own)(
                *operands, *waits
            )

        return run

    def slot_struct(experts):
        return struct((min(ep_count, EXPERTS), experts, stride, width), bf16)

    chunk_struct = slot_struct(each)
    moved_struct = struct((ep_count, each, stride, width), bf16)

    tokens_moved = [move(tokens, "seq", shift) for shift in range(seq_count)]
    pairs = jnp.concatenate([routes.reshape(rows, TOP).T, priority.reshape(1, rows)], axis=0)
    route_col, dest_col, dest_row = call(
        lambda *refs: routing_kernel(*refs, capacity=capacity, **common),
        "routing",
        in_specs=[smem, vmem],
        out_specs=[vmem] * 3,
        out_shape=[
            struct((rows, TOP), jnp.int32),
            struct((rows, TOP), jnp.int32),
            struct((TOP, rows), jnp.int32),
        ],
        cost_estimate=cost(3),
    )(places, pairs)
    cotangent_sent = call(
        lambda *refs: send_grads_kernel(*refs, stride=stride),
        "send_grads",
        in_specs=[vmem] * 2,
        out_specs=[vmem] * chunks,
        out_shape=[chunk_struct] * chunks,
        cost_estimate=cost(3),
    )(cotangent, dest_row)
    weight_groups = (
        w_qkv.reshape(width, 3, seq_count, group_width)
        .transpose(2, 1, 3, 0)
        .reshape(seq_count, 3 * group_width, width)
    )

    cotangent_slots = [send_slots(chunk) for chunk in cotangent_sent]

    row_block = pl.BlockSpec((1, full_rows, group_width), lambda i, *_: (i, 0, 0))
    probs_block = pl.BlockSpec((1, group_heads, full_rows, full_rows), lambda i, *_: (i, 0, 0, 0))
    normed_block = pl.BlockSpec((1, full_rows, width), lambda i, *_: (i, 0, 0))
    half_block = pl.BlockSpec((1, patch_rows // 2, 2 * group_width), lambda i, *_: (i, 0, 0))
    packed_block = pl.BlockSpec((1, patch_rows, 3 * group_width), lambda i, *_: (i, 0, 0))
    vector_block = pl.BlockSpec((1, width), lambda i, *_: (0, 0))
    image_block = pl.BlockSpec((1, patch_rows, width), lambda i, *_: (i, 0, 0))
    half_struct = struct((image_count, patch_rows // 2, 2 * group_width), bf16)
    row_struct = struct((image_count, full_rows, group_width), bf16)
    def attention(first_image, count, previous, *others):
        def own(block):
            return pl.BlockSpec(
                block.block_shape, lambda i, *rest: block.index_map(first_image + i, *rest)
            )

        inputs = 4 + seq_count
        blocks = [half_block] * seq_count + [
            row_block, row_block, row_block, probs_block, normed_block,
        ]
        return call(
            lambda *refs: attention_kernel(
                *refs[:inputs],
                *refs[inputs + len(previous) :],
                first_image=first_image,
                seq_count=seq_count,
                group_heads=group_heads,
                head_width=head_width,
            ),
            "attention",
            waits=others,
            grid_spec=dict(
                num_scalar_prefetch=1,
                grid=(count,),
                in_specs=[
                    vector_block,
                    vector_block,
                    pl.BlockSpec((1, 3 * group_width, width), lambda i, at: (at[1], 0, 0)),
                ]
                + [own(image_block)] * seq_count
                + [pl.BlockSpec(memory_space=pl.ANY)] * len(previous),
                out_specs=[own(block) for block in blocks],
                scratch_shapes=[
                    pltpu.VMEM((seq_count, patch_rows, group_width), bf16),
                    pltpu.VMEM((seq_count, patch_rows, width), bf16),
                ],
            ),
            out_shape=[half_struct] * seq_count
            + [
                row_struct,
                row_struct,
                row_struct,
                struct((image_count, group_heads, full_rows, full_rows), bf16),
                struct((image_count, full_rows, width), bf16),
            ],
            input_output_aliases={inputs + at: at for at in range(len(previous))},
            cost_estimate=cost(30),
        )(places, gain_one, shift_one, weight_groups, *tokens_moved, *previous)

    started = attention(0, 1, (), *cotangent_sent)
    (watched,) = hold([cotangent_slots[0]], started[-1])
    cotangent_slots[0] = watched
    *attended, q, k, v, probs, attn_in = attention(1, image_count - 1, started, watched)
    attended_sent = attended
    attended = [move(block, "seq", shift) for shift, block in enumerate(attended)]
    cotangent_slots[1:] = hold(cotangent_slots[1:], attended_sent[1]) if chunks > 1 else []

    middle, gate, stats, *rows_sent = call(
        lambda *refs: dispatch_kernel(*refs, seq_count=seq_count, **common),
        "dispatch",
        waits=cotangent_slots,
        in_specs=[smem] + [vmem] * (7 + seq_count),
        out_specs=[vmem] * (3 + chunks),
        out_shape=[
            struct((rows, width), f32),
            struct((rows, EXPERTS), f32),
            struct((1, width), f32),
        ]
        + [chunk_struct] * chunks,
        cost_estimate=cost(9),
    )(
        places, tokens, w_proj, gain_two, shift_two, w_router, route_col, dest_row, *attended,
    )
    row_slots = [send_slots(chunk) for chunk in rows_sent]

    hidden_tile = local_hidden // 2
    tiles = local_hidden // hidden_tile
    moved_block = pl.BlockSpec((ep_count, 1, stride, width), lambda e, f: (0, e, 0, 0))
    cotangent_all = [over_seq(slots) for slots in cotangent_slots]
    grads_back, values_back = [], ()
    for at in range(chunks):
        weight_block = pl.BlockSpec(
            (hidden_tile, width), lambda e, f, at=at: ((e + at * each) * tiles + f, 0)
        )
        all_block = pl.BlockSpec(
            (ep_count, 1, stride, width), lambda e, f, at=at: (0, e + at * each, 0, 0)
        )
        value, back = call(
            lambda *refs: expert_kernel(*refs, pieces=max(1, hidden_tile // 768)),
            "experts",
            waits=cotangent_all[:1] * (at > 0),
            grid=(each, tiles),
            in_specs=[moved_block, moved_block, weight_block, weight_block]
            + [pl.BlockSpec(memory_space=pl.ANY)] * len(values_back),
            out_specs=[all_block, moved_block],
            out_shape=[struct((ep_count, local_experts, stride, width), bf16), moved_struct],
            scratch_shapes=[pltpu.VMEM((ep_count * stride, width), f32)] * 2
            + [pltpu.VMEM((ep_count * stride, width), bf16)],
            input_output_aliases={4: 0} if values_back else {},
            cost_estimate=cost(16),
        )(row_slots[at], cotangent_slots[at], expert_in, expert_out, *values_back)
        grads_back.append(exchange(back, "ep"))
        values_back = (value,)

    all_rows = seq_count * ep_count * stride
    grad_tile = min(768, local_hidden)
    grad_tiles = local_hidden // grad_tile
    anywhere = pl.BlockSpec(memory_space=pl.ANY)
    rows_all = [over_seq(slots) for slots in row_slots]
    grads = []

    row_blocks = max(1, all_rows // 1024)
    sources = ep_count // row_blocks
    block_rows = all_rows // row_blocks

    def expert_grads(expert, begin, count, *others):
        place = expert * grad_tiles + begin
        tile_block = pl.BlockSpec((grad_tile, width), lambda f, r: (place + f, 0))

        def source_block(own):
            return pl.BlockSpec(
                (seq_count, sources, 1, stride, width),
                lambda f, r: (0, r, own, 0, 0),
                pipeline_mode=pl.Buffered(1 if row_blocks == 1 else 2),
            )

        *grads[:], done = call(
            lambda *refs: expert_grad_kernel(
                *refs, row_pieces=max(1, block_rows // 512), row_blocks=row_blocks
            ),
            "expert_grads",
            waits=others,
            grid=(count, row_blocks),
            in_specs=[source_block(expert % each)] * 2 + [tile_block, tile_block]
            + [anywhere] * len(grads),
            out_specs=[tile_block, tile_block, pl.BlockSpec((8, 128), lambda f, r: (0, 0))],
            out_shape=[
                struct(expert_in.shape, f32),
                struct(expert_out.shape, f32),
                struct((8, 128), f32),
            ],
            scratch_shapes=[pltpu.VMEM((grad_tile, block_rows), bf16)] * 2
            + [pltpu.VMEM((block_rows, width), bf16)],
            input_output_aliases={4: 0, 5: 1} if grads else {},
            cost_estimate=cost(7 * count),
        )(rows_all[expert // each], cotangent_all[expert // each], expert_in, expert_out, *grads)
        return done

    work = [(expert, 0, grad_tiles) for expert in range(local_experts - 1)]
    rest = (grad_tiles + 3) // 4
    work += [(local_experts - 1, 0, grad_tiles - rest), (local_experts - 1, grad_tiles - rest, rest)]
    work = iter(work)

    def next_grads(*others):
        return [expert_grads(*part, *others) for part in itertools.islice(work, 1)]

    early = next_grads(values_back[0], grads_back[0]) if local_experts > 3 else []
    leaving_shape = ((rows + width) // 2, 2 * group_width)
    grad_middle, router_grad, small, *leaving = call(
        lambda *refs: combine_kernel(
            *refs, split=split, seq_count=seq_count, chunks=chunks, **common
        ),
        "combine",
        waits=early,
        in_specs=[smem] + [vmem] * (10 + seq_count + chunks),
        out_specs=[vmem] * (3 + seq_count),
        out_shape=[
            struct((rows, width), f32),
            struct((EXPERTS, 1, width) if devices == EXPERTS else (EXPERTS, width), f32),
            struct((3, width), f32),
        ]
        + [struct(leaving_shape, bf16)] * seq_count,
        cost_estimate=cost(10),
    )(
        places, middle, gate, cotangent, w_proj, gain_two, shift_two, w_router,
        route_col, dest_col, stats, *attended, *grads_back,
    )
    leaving = [move(block, "seq", -at) for at, block in enumerate(leaving)]
    piece = EXPERTS * width // devices
    router_grad = exchange(router_grad.reshape(devices, 1, piece), ("seq", "ep"))
    values_moved = exchange(values_back[0], "ep")
    middle_done = next_grads(grad_middle) if local_experts > 2 else []
    half = 2 * group_width
    pairs_along = ep_count // 2
    slab_shape = (pairs_along, 2, half // pairs_along, width)
    *packed_sent, slab = call(
        lambda *refs: attention_grad_kernel(
            *refs, group_heads=group_heads, head_width=head_width, seq_count=seq_count
        ),
        "attention_grad",
        waits=middle_done,
        grid=(image_count,),
        in_specs=[smem, row_block, row_block, row_block, probs_block, normed_block]
        + [pl.BlockSpec(leaving_shape, lambda i: (0, 0))] * seq_count,
        out_specs=[packed_block] * seq_count
        + [pl.BlockSpec(slab_shape, lambda i: (0, 0, 0, 0))],
        out_shape=[struct((image_count, patch_rows, 3 * group_width), bf16)] * seq_count
        + [struct(slab_shape, bf16)],
        scratch_shapes=[
            pltpu.VMEM((3 * group_width, width), f32),
            pltpu.VMEM((image_count, seq_count, patch_rows, group_width), bf16),
            pltpu.VMEM((seq_count, patch_rows, 3 * group_width), bf16),
        ],
        cost_estimate=cost(18),
    )(places, q, k, v, probs, attn_in, *leaving)
    packed = [move(block, "seq", shift) for shift, block in enumerate(packed_sent)]

    same_core = [[2 * at + core for at in range(pairs_along)] for core in range(2)]

    def along_core(values):
        return lax.all_to_all(
            values, "ep", split_axis=0, concat_axis=0, tiled=True, axis_index_groups=same_core
        )

    slab = lax.psum_scatter(
        slab.reshape(2 * half, width), "ep", scatter_dimension=0, tiled=True
    )
    late = next_grads(packed_sent[0], router_grad) if local_experts > 1 else []
    slab, packed[1] = hold([slab, packed[1]], *late, values_moved, *packed[2:])
    slab = jnp.broadcast_to(slab[None], (pairs_along, half // pairs_along, width))
    output, value_stats = call(
        lambda *refs: output_kernel(*refs, split=split, **common),
        "output",
        waits=[slab],
        in_specs=[smem] + [vmem] * 5,
        out_specs=[vmem] * 2,
        out_shape=[struct((image_count, patch_rows, width), bf16), struct((1, width), f32)],
        cost_estimate=cost(5),
    )(places, middle, gate, route_col, dest_col, values_moved)
    slab_moved = along_core(slab).reshape(half, width)
    own_slabs = [move(slab_moved, "seq", shift) for shift in range(seq_count)]
    input_grad, copies = call(
        input_grad_kernel,
        "input_grad",
        grid=(image_count,),
        in_specs=[
            smem,
            pl.BlockSpec((seq_count, 3 * group_width, width), lambda i: (0, 0, 0)),
            image_block,
            image_block,
            vector_block,
            pl.BlockSpec((3, width), lambda i: (0, 0)),
            pl.BlockSpec((1, width), lambda i: (0, 0)),
            pl.BlockSpec((devices, 1, piece), lambda i: (0, 0, 0)),
        ]
        + [packed_block] * seq_count,
        out_specs=[image_block, pl.BlockSpec((devices, 8, width), lambda i: (0, 0, 0))],
        out_shape=[
            struct((image_count, patch_rows, width), bf16),
            struct((devices, 8, width), f32),
        ],
        scratch_shapes=[pltpu.VMEM((8, width), f32)],
        cost_estimate=cost(7),
    )(
        places, weight_groups, tokens, grad_middle.reshape(image_count, patch_rows, width),
        gain_one, small, value_stats, router_grad, *packed,
    )
    own_slabs = hold(own_slabs, *next_grads(input_grad, slab_moved))
    other_slabs = [other_core(each_slab) for each_slab in own_slabs]
    qkv_grad, proj_grad = call(
        lambda *refs: assemble_kernel(*refs, seq_count=seq_count),
        "assemble",
        waits=next_grads(own_slabs[0]),
        grid=(4,),
        in_specs=[smem] + [pl.BlockSpec((half, width), lambda i: (0, 0))] * (2 * seq_count),
        out_specs=[
            pl.BlockSpec((width, width), lambda i: (0, jnp.minimum(i, 2))),
            pl.BlockSpec((width, width), lambda i: (0, 0)),
        ],
        out_shape=[struct((width, 3 * width), f32), struct((width, width), f32)],
        scratch_shapes=[pltpu.VMEM((seq_count, 2 * half, width), bf16)],
        cost_estimate=cost(8),
    )(places, *own_slabs, *other_slabs)

    copies = exchange(copies, ("seq", "ep"))
    sums = jnp.sum(copies[:, :5], axis=0)
    router_grad = copies[:, 5, :piece].reshape(EXPERTS, width).T
    return (
        output,
        input_grad,
        sums[3],
        sums[4],
        qkv_grad,
        proj_grad,
        sums[0],
        sums[1],
        router_grad,
        grads[0],
        grads[1],
        jnp.sqrt(sums[2, :3] / sums[2, 3]),
    )


def solution(mesh):
    in_specs = (
        P("ep", "seq", None),
        P("ep", "seq", None),
        P("ep", "seq"),
        P("ep"),
        P(),
        P(),
        P(),
        P(),
        P(),
        P(),
        P(),
        P("ep", None),
        P("ep", None),
        P("ep", "seq", None),
    )
    out_specs = (
        P("ep", "seq", None),
        P("ep", "seq", None),
        P(),
        P(),
        P(),
        P(),
        P(),
        P(),
        P(),
        P("ep", None),
        P("ep", None),
        P(),
    )
    return jax.shard_map(
        per_device, mesh=mesh, in_specs=in_specs, out_specs=out_specs, check_vma=False
    )
```

```python
import itertools

import jax
import jax.numpy as jnp
from jax import lax
from jax.experimental import pallas as pl
from jax.experimental.pallas import tpu as pltpu
from jax.sharding import PartitionSpec as P

HEADS = 12
EXPERTS = 32
TOP = 2
PATCHES = 576
SHORT = 196

norm_eps = 1e-06
neg_big = -1e30
f32 = jnp.float32
bf16 = jnp.bfloat16

tail_slope = 0.33
tail_terms = (
    0.18635779800457905,
    0.18295602991113566,
    0.2012232872944192,
    0.04722279904104141,
    0.40849559831839843,
    -0.3511445702318978,
    0.46023391759858995,
    -0.13534486747679436,
)


def mm(a, b):
    return lax.dot_general(a, b, (((1,), (0,)), ((), ())), preferred_element_type=f32)


def mm_nt(a, b):
    return lax.dot_general(a, b, (((1,), (1,)), ((), ())), preferred_element_type=f32)


def mm_tn(a, b):
    return lax.dot_general(a, b, (((0,), (0,)), ((), ())), preferred_element_type=f32)


def gelu_pair(v):
    size = jnp.abs(v)
    bell = jnp.exp(v * v * -0.5)
    t = 1.0 / (1.0 + size * (tail_slope * 0.7071067811865476))
    poly = tail_terms[-1] * 0.5
    for term in tail_terms[-2::-1]:
        poly = poly * t + term * 0.5
    tail = poly * t * bell
    cdf = jnp.where(v >= 0.0, 1.0 - tail, tail)
    return v * cdf, cdf + v * bell * 0.3989422804014327


def normalize(values):
    centred = values - jnp.mean(values, axis=-1, keepdims=True)
    inv_root = lax.rsqrt(jnp.mean(centred * centred, axis=-1, keepdims=True) + norm_eps)
    return centred * inv_root, inv_root


def norm_row_grad(upstream, normed, inv_root, gain):
    scaled = upstream * gain
    return inv_root * (
        scaled
        - jnp.mean(scaled, axis=-1, keepdims=True)
        - normed * jnp.mean(scaled * normed, axis=-1, keepdims=True)
    )


def valid_rows(places_ref, image_count, patch_rows, shape, axis):
    row = lax.broadcasted_iota(jnp.int32, shape, axis)
    first_patch = places_ref[1] * patch_rows
    valid = row < 0
    for image in range(image_count):
        length = jnp.where(image < places_ref[0], PATCHES, SHORT)
        start = image * patch_rows
        stop = start + jnp.clip(length - first_patch, 0, patch_rows)
        valid = valid | ((row >= start) & (row < stop))
    return valid


def routing_kernel(
    places_ref, pairs_ref, route_col_ref, dest_col_ref, dest_row_ref,
    *, image_count, patch_rows, capacity, stride,
):
    rows = pairs_ref.shape[1]
    eye = lax.broadcasted_iota(jnp.int32, (rows, rows), 0) == lax.broadcasted_iota(
        jnp.int32, (rows, rows), 1
    )

    def as_column(line):
        return jnp.sum(jnp.where(eye, line.astype(f32), 0.0), axis=1, keepdims=True).astype(
            jnp.int32
        )

    e_row = [pairs_ref[k : k + 1, :] for k in range(TOP)]
    e_col = [as_column(line) for line in e_row]
    prio_row = pairs_ref[TOP : TOP + 1, :]
    prio_col = as_column(prio_row)
    for k in range(TOP):
        route_col_ref[:, k : k + 1] = e_col[k]
    valid_col = valid_rows(places_ref, image_count, patch_rows, (rows, 1), 0)
    valid_row = valid_rows(places_ref, image_count, patch_rows, (1, rows), 1)
    weight_col = valid_col.astype(f32)
    weight_row = valid_row.astype(f32)
    row_first = (prio_row < prio_col).astype(f32) * weight_row
    col_first = (prio_col < prio_row).astype(f32) * weight_col
    for k in range(TOP):
        count = jnp.where(e_col[k] == e_row[k], row_first, 0.0)
        for earlier in range(k):
            count = count + jnp.where(e_col[k] == e_row[earlier], weight_row, 0.0)
        slot = jnp.sum(count, axis=1, keepdims=True).astype(jnp.int32)
        keep = valid_col & (slot < capacity)
        dest_col_ref[:, k : k + 1] = jnp.where(keep, e_col[k] * stride + slot, -1)
        count = jnp.where(e_col[k] == e_row[k], col_first, 0.0)
        for earlier in range(k):
            count = count + jnp.where(e_col[earlier] == e_row[k], weight_col, 0.0)
        slot = jnp.sum(count, axis=0, keepdims=True).astype(jnp.int32)
        keep = valid_row & (slot < capacity)
        dest_row_ref[k : k + 1, :] = jnp.where(keep, e_row[k] * stride + slot, -1)


def side_by_side(values):
    half = values.shape[0] // 2
    return jnp.concatenate([values[:half], values[half:]], axis=1)


def stacked(values):
    width = values.shape[1] // 2
    return jnp.concatenate([values[:, :width], values[:, width:]], axis=0)


def neighbour(places_ref, shift, seq_count):
    return (places_ref[1] + (shift + seq_count)) % seq_count


def attention_kernel(
    places_ref, gain_ref, shift_ref, weight_ref, *refs,
    first_image, seq_count, group_heads, head_width,
):
    tokens_refs = refs[:seq_count]
    attended_refs = refs[seq_count : 2 * seq_count]
    q_ref, k_ref, v_ref, probs_ref, normed_ref, spread_ref, tokens_ref = refs[2 * seq_count :]
    _, patch_rows, width = tokens_refs[0].shape
    for shift, source_ref in enumerate(tokens_refs):
        tokens_ref[neighbour(places_ref, -shift, seq_count)] = source_ref[0]
    total_rows = seq_count * patch_rows
    group_width = group_heads * head_width
    values = tokens_ref[...].reshape(total_rows, width).astype(f32)
    normed, _ = normalize(values)
    attn_in = (normed * gain_ref[...] + shift_ref[...]).astype(bf16)
    normed_ref[0] = attn_in
    q, k, v = (
        mm_nt(attn_in, weight_ref[0, part * group_width : (part + 1) * group_width, :]).astype(bf16)
        for part in range(3)
    )
    q_ref[0] = q
    k_ref[0] = k
    v_ref[0] = v
    length = jnp.where(first_image + pl.program_id(0) < places_ref[0], PATCHES, SHORT)
    key_valid = lax.broadcasted_iota(jnp.int32, (1, total_rows), 1) < length
    lane = lax.broadcasted_iota(jnp.int32, (1, group_width), 1)
    scaled_q = (q.astype(f32) * head_width ** (-0.5)).astype(bf16)
    attended = jnp.zeros((total_rows, group_width), f32)
    for head in range(group_heads):
        in_head = (lane >= head * head_width) & (lane < (head + 1) * head_width)
        scores = mm_nt(jnp.where(in_head, scaled_q, jnp.zeros_like(scaled_q)), k)
        scores = jnp.where(key_valid, scores, neg_big)
        exp_scores = jnp.exp(scores - jnp.max(scores, axis=-1, keepdims=True))
        inverse = 1.0 / jnp.sum(exp_scores, axis=-1, keepdims=True)
        probs = (exp_scores * inverse).astype(bf16)
        probs_ref[0, head] = probs
        attended = jnp.where(in_head, mm(probs, v), attended)
    spread_ref[...] = attended.astype(bf16).reshape(spread_ref.shape)
    for shift, attended_ref in enumerate(attended_refs):
        attended_ref[0] = side_by_side(spread_ref[neighbour(places_ref, shift, seq_count)])


def slot_picks(dest_row_ref, stride, k):
    slot = lax.broadcasted_iota(jnp.int32, (EXPERTS * stride, 1), 0)
    return (slot == dest_row_ref[k : k + 1, :]).astype(f32).astype(bf16)


def send_grads_kernel(cotangent_ref, dest_row_ref, *sent_refs, stride):
    width = cotangent_ref.shape[-1]
    cotangent = cotangent_ref[...].reshape(-1, width)
    pick = slot_picks(dest_row_ref, stride, 0)
    for k in range(1, TOP):
        pick = pick + slot_picks(dest_row_ref, stride, k)
    sent = mm(pick, cotangent).astype(bf16)
    store_chunks(sent_refs, sent, stride)


def store_chunks(chunk_refs, table, stride):
    width = table.shape[-1]
    targets, each = chunk_refs[0].shape[:2]
    grouped = table.reshape(targets, len(chunk_refs) * each, stride, width)
    for at, chunk_ref in enumerate(chunk_refs):
        chunk_ref[...] = grouped[:, at * each : (at + 1) * each]


def three_terms(values):
    high = values.astype(bf16)
    rest = values - high.astype(f32)
    middle = rest.astype(bf16)
    return high, middle, (rest - middle.astype(f32)).astype(bf16)


def diagonal(stride):
    row = lax.broadcasted_iota(jnp.int32, (1, stride, stride), 1)
    return row == lax.broadcasted_iota(jnp.int32, (1, stride, stride), 2)


def row_scalars(block, stride):
    spare = block[:, stride - 3 : stride, :stride].astype(f32)
    line = spare[:, 0:1] + spare[:, 1:2] + spare[:, 2:3]
    return jnp.sum(jnp.where(diagonal(stride), line, 0.0), axis=2, keepdims=True)


def with_scalars(block, column, stride):
    width = block.shape[-1]
    line = jnp.sum(jnp.where(diagonal(stride), column, 0.0), axis=1, keepdims=True)
    line = jnp.concatenate(
        [line, jnp.zeros((line.shape[0], 1, width - stride), f32)], axis=2
    )
    row = lax.broadcasted_iota(jnp.int32, (1, stride, 1), 1)
    for at, term in enumerate(three_terms(line)):
        block = jnp.where(row == stride - 3 + at, term.astype(f32), block)
    return block


def unpacked(blocks_ref):
    return jnp.concatenate([stacked(blocks_ref[at]) for at in range(blocks_ref.shape[0])], axis=0)


def group_rows(places_ref, shift, seq_count, group_width):
    start = neighbour(places_ref, shift, seq_count) * group_width
    return pl.ds(pl.multiple_of(start, 16), group_width)


def dispatch_kernel(
    places_ref, tokens_ref, proj_ref, gain_ref, shift_ref,
    router_ref, route_col_ref, dest_row_ref, *refs, image_count, patch_rows, stride, seq_count,
):
    attended_refs = refs[:seq_count]
    middle_ref, gate_ref, stats_ref, *sent_refs = refs[seq_count:]
    rows, width = middle_ref.shape
    group_width = attended_refs[0].shape[-1] // 2
    attn_out = jnp.zeros((rows, width), f32)
    for shift, attended_ref in enumerate(attended_refs):
        attn_out = attn_out + mm(
            unpacked(attended_ref),
            proj_ref[group_rows(places_ref, -shift, seq_count, group_width), :],
        )
    valid = valid_rows(places_ref, image_count, patch_rows, (rows, 1), 0).astype(f32)
    stats_ref[...] = total_at(attn_out * attn_out * valid, 0)
    middle = tokens_ref[...].reshape(rows, width).astype(f32) + attn_out
    middle_ref[...] = middle
    normed, _ = normalize(middle)
    moe_in = (normed * gain_ref[...] + shift_ref[...]).astype(bf16)
    logits = mm(moe_in, router_ref[...])
    exp_logits = jnp.exp(logits - jnp.max(logits, axis=-1, keepdims=True))
    gate = exp_logits / jnp.sum(exp_logits, axis=-1, keepdims=True)
    gate_ref[...] = gate
    expert_lane = lax.broadcasted_iota(jnp.int32, (1, EXPERTS), 1)
    pick_any = jnp.zeros((EXPERTS * stride, rows), bf16)
    slot_gate = jnp.zeros((EXPERTS * stride, 128), f32)
    for k in range(TOP):
        chosen = jnp.sum(
            jnp.where(expert_lane == route_col_ref[:, k : k + 1], gate, 0.0),
            axis=-1,
            keepdims=True,
        )
        pick = slot_picks(dest_row_ref, stride, k)
        pick_any = pick_any + pick
        lane = lax.broadcasted_iota(jnp.int32, (1, 128), 1)
        terms = jnp.zeros((rows, 128), f32)
        for at, term in enumerate(three_terms(jnp.broadcast_to(chosen, (rows, 128)))):
            terms = jnp.where(lane == at, term.astype(f32), terms)
        slot_gate = slot_gate + mm(pick, terms.astype(bf16))
    sent = mm(pick_any, moe_in).reshape(EXPERTS, stride, width)
    slot_gate = jnp.sum(slot_gate, axis=1, keepdims=True).reshape(EXPERTS, stride, 1)
    sent = with_scalars(sent, slot_gate, stride).astype(bf16)
    store_chunks(sent_refs, sent.reshape(EXPERTS * stride, width), stride)


def scaled_rows(rows_block, grads_block):
    groups, stride, width = rows_block.shape
    scale = row_scalars(rows_block, stride)
    return (grads_block.astype(f32) * scale).astype(bf16).reshape(groups * stride, width)


def expert_kernel(
    rows_ref, cotangent_ref, first_ref, second_ref, *refs, pieces,
):
    value_ref, back_ref, value_acc, grad_acc, scaled_ref = refs[-5:]
    count, _, stride, width = rows_ref.shape
    rows = count * stride
    piece = first_ref.shape[0] // pieces
    step = pl.program_id(1)

    @pl.when(step == 0)
    def _():
        scaled_ref[...] = scaled_rows(rows_ref[:, 0], cotangent_ref[:, 0])

    moe_rows = rows_ref[:, 0].reshape(rows, width)
    grad_rows = scaled_ref[...]
    value = jnp.zeros((rows, width), f32)
    grad = jnp.zeros((rows, width), f32)
    for at in range(pieces):
        first = first_ref[at * piece : (at + 1) * piece, :]
        second = second_ref[at * piece : (at + 1) * piece, :]
        hidden, slope = gelu_pair(mm_nt(moe_rows, first))
        grad_pre = (mm_nt(grad_rows, second) * slope).astype(bf16)
        value = value + mm(hidden.astype(bf16), second)
        grad = grad + mm(grad_pre, first)

    @pl.when(step == 0)
    def _():
        value_acc[...] = value
        grad_acc[...] = grad

    @pl.when(step > 0)
    def _():
        value_acc[...] += value
        grad_acc[...] += grad

    @pl.when(step == pl.num_programs(1) - 1)
    def _():
        value_low = value_acc[...].astype(bf16).reshape(count, stride, width)
        value_ref[:, 0] = value_low
        gate_grad = jnp.sum(
            cotangent_ref[:, 0].astype(f32) * value_low.astype(f32), axis=-1, keepdims=True
        )
        grad_low = grad_acc[...].reshape(count, stride, width)
        back_ref[:, 0] = with_scalars(grad_low, gate_grad, stride).astype(bf16)


def table_part(chunk_refs, part):
    split = chunk_refs[0].shape[0] * chunk_refs[0].shape[1] * len(chunk_refs) // EXPERTS
    pieces = []
    for chunk_ref in chunk_refs:
        sources, each, stride, width = chunk_ref.shape
        block = chunk_ref[...].reshape(sources // split, split, each, stride, width)
        pieces.append(block[:, part])
    table = pieces[0] if len(pieces) == 1 else jnp.concatenate(pieces, axis=1)
    return table.reshape(EXPERTS, table.shape[2], table.shape[3])


def combine_kernel(
    places_ref, middle_ref, gate_ref, cotangent_ref, proj_ref, gain_ref,
    shift_ref, router_ref, route_col_ref, dest_col_ref, stats_ref, *refs,
    image_count, patch_rows, stride, split, seq_count, chunks,
):
    attended_refs = refs[:seq_count]
    back_refs = refs[seq_count : seq_count + chunks]
    grad_middle_ref, router_grad_ref, small_ref = refs[seq_count + chunks :][:3]
    leaving_refs = refs[seq_count + chunks + 3 :]
    rows, width = middle_ref.shape
    group_width = attended_refs[0].shape[-1] // 2
    slots = EXPERTS * stride
    middle = middle_ref[...]
    gate = gate_ref[...]
    valid = valid_rows(places_ref, image_count, patch_rows, (rows, 1), 0).astype(f32)
    grad_total = cotangent_ref[...].reshape(rows, width).astype(f32) * valid
    expert_lane = lax.broadcasted_iota(jnp.int32, (1, EXPERTS), 1)
    slot_lane = lax.broadcasted_iota(jnp.int32, (1, stride), 1)
    slot = lax.broadcasted_iota(jnp.int32, (1, slots), 1)
    pick_any = jnp.zeros((rows, slots), bf16)
    for k in range(TOP):
        pick_any = pick_any + (slot == dest_col_ref[:, k : k + 1]).astype(f32).astype(bf16)
    grad_dispatch = jnp.zeros((rows, width), f32)
    scalar_rows = [jnp.zeros((rows, stride), f32) for _ in range(TOP)]
    own = [
        (expert_lane == route_col_ref[:, k : k + 1]).astype(f32).astype(bf16) for k in range(TOP)
    ]
    for part in range(split):
        table = table_part(back_refs, part)
        grad_dispatch = grad_dispatch + mm(pick_any, table.reshape(slots, width))
        for at in range(stride - 3, stride):
            line = table[:, at, :stride]
            for k in range(TOP):
                scalar_rows[k] = scalar_rows[k] + mm(own[k], line)
    grad_probs = jnp.zeros((rows, EXPERTS), f32)
    for k in range(TOP):
        place = dest_col_ref[:, k : k + 1] - route_col_ref[:, k : k + 1] * stride
        grad_gate = jnp.sum(
            jnp.where(slot_lane == place, scalar_rows[k], 0.0), axis=-1, keepdims=True
        )
        grad_probs = grad_probs + own[k].astype(f32) * grad_gate
    grad_logits = (
        gate * (grad_probs - jnp.sum(grad_probs * gate, axis=-1, keepdims=True))
    ).astype(bf16)
    grad_moe_in = grad_dispatch + mm_nt(grad_logits, router_ref[...])
    normed, inv_root = normalize(middle)
    moe_in = (normed * gain_ref[...] + shift_ref[...]).astype(bf16)
    grad_middle = grad_total + norm_row_grad(grad_moe_in, normed, inv_root, gain_ref[...])
    grad_middle_ref[...] = grad_middle
    grad_attn = grad_middle.astype(bf16)
    for shift in range(seq_count):
        attended = unpacked(attended_refs[shift])
        own_rows = group_rows(places_ref, -shift, seq_count, group_width)
        grads = mm_nt(grad_attn, proj_ref[own_rows, :]).astype(bf16)
        leaving_refs[shift][: rows // 2, :] = side_by_side(grads)
        grads = mm_tn(grad_attn, attended).astype(bf16)
        leaving_refs[shift][rows // 2 :, :] = side_by_side(grads)
    router_grad_ref[...] = mm_tn(grad_logits, moe_in).reshape(router_grad_ref.shape)
    small_ref[0:1, :] = jnp.sum(grad_moe_in * normed, axis=0, keepdims=True)
    small_ref[1:2, :] = jnp.sum(grad_moe_in, axis=0, keepdims=True)
    lane = lax.broadcasted_iota(jnp.int32, (1, width), 1)
    count = jnp.sum(valid, axis=0, keepdims=True) * width
    small_ref[2:3, :] = stats_ref[...] + jnp.where(lane == 3, count, 0.0)


def total_at(values, place):
    lane = lax.broadcasted_iota(jnp.int32, (1, values.shape[-1]), 1)
    by_lane = jnp.sum(values, axis=0, keepdims=True)
    return jnp.where(lane == place, jnp.sum(by_lane, axis=1, keepdims=True), 0.0)


def output_kernel(
    places_ref, middle_ref, gate_ref, route_col_ref, dest_col_ref, *refs,
    image_count, patch_rows, stride, split,
):
    value_refs = refs[:-2]
    output_ref, stats_ref = refs[-2:]
    rows, width = middle_ref.shape
    slots = EXPERTS * stride
    gate = gate_ref[...]
    expert_lane = lax.broadcasted_iota(jnp.int32, (1, EXPERTS), 1)
    slot = lax.broadcasted_iota(jnp.int32, (1, slots), 1)
    moe_out = jnp.zeros((rows, width), f32)
    tables = [table_part(value_refs, part).reshape(slots, width) for part in range(split)]
    for k in range(TOP):
        pick = (slot == dest_col_ref[:, k : k + 1]).astype(f32).astype(bf16)
        pair_value = mm(pick, tables[0])
        for table in tables[1:]:
            pair_value = pair_value + mm(pick, table)
        own = expert_lane == route_col_ref[:, k : k + 1]
        moe_out = moe_out + jnp.sum(jnp.where(own, gate, 0.0), axis=-1, keepdims=True) * pair_value
    valid = valid_rows(places_ref, image_count, patch_rows, (rows, 1), 0).astype(f32)
    total = middle_ref[...] + moe_out
    output_ref[...] = (total * valid).astype(bf16).reshape(output_ref.shape)
    stats_ref[...] = total_at(moe_out * moe_out * valid, 1) + total_at(total * total * valid, 2)


def attention_grad_kernel(
    places_ref, q_ref, k_ref, v_ref, probs_ref, normed_ref, *refs,
    group_heads, head_width, seq_count,
):
    grad_refs = refs[:seq_count]
    packed_refs = refs[seq_count : 2 * seq_count]
    slab_ref, weight_acc, grad_spread, packed_spread = refs[2 * seq_count :]
    patch_rows = grad_spread.shape[2]
    rows = grad_spread.shape[0] * patch_rows
    total_rows = q_ref.shape[1]
    group_width = group_heads * head_width
    scale = head_width ** (-0.5)

    @pl.when(pl.program_id(0) == 0)
    def _():
        for shift, grad_ref in enumerate(grad_refs):
            place = neighbour(places_ref, shift, seq_count)
            grads = stacked(grad_ref[: rows // 2, :])
            for image in range(grad_spread.shape[0]):
                grad_spread[image, place] = grads[image * patch_rows : (image + 1) * patch_rows]

    grad_heads = grad_spread[pl.program_id(0)].reshape(total_rows, group_width)
    q, k, v = q_ref[0], k_ref[0], v_ref[0]
    lane = lax.broadcasted_iota(jnp.int32, (1, group_width), 1)
    nothing = jnp.zeros_like(q)
    grad_q = jnp.zeros((total_rows, group_width), f32)
    grad_k = jnp.zeros((total_rows, group_width), f32)
    grad_v = jnp.zeros((total_rows, group_width), f32)
    for head in range(group_heads):
        in_head = (lane >= head * head_width) & (lane < (head + 1) * head_width)
        own_grad = jnp.where(in_head, grad_heads, nothing)
        probs_low = probs_ref[0, head]
        probs = probs_low.astype(f32)
        grad_probs = mm_nt(own_grad, v)
        delta = jnp.sum(probs * grad_probs, axis=-1, keepdims=True)
        grad_scores = (probs * (grad_probs - delta)).astype(bf16)
        grad_q = jnp.where(in_head, mm(grad_scores, k), grad_q)
        grad_k = jnp.where(in_head, mm_tn(grad_scores, q), grad_k)
        grad_v = jnp.where(in_head, mm_tn(probs_low, grad_heads), grad_v)
    packed = jnp.concatenate([grad_q * scale, grad_k * scale, grad_v], axis=1).astype(bf16)
    packed_spread[...] = packed.reshape(packed_spread.shape)
    for shift, packed_ref in enumerate(packed_refs):
        packed_ref[0] = packed_spread[neighbour(places_ref, shift, seq_count)]
    weight_grad = mm_tn(packed, normed_ref[0])

    @pl.when(pl.program_id(0) == 0)
    def _():
        weight_acc[...] = weight_grad

    @pl.when(pl.program_id(0) > 0)
    def _():
        weight_acc[...] += weight_grad

    @pl.when(pl.program_id(0) == pl.num_programs(0) - 1)
    def _():
        width = weight_acc.shape[1]
        proj_grad = grad_refs[0][rows // 2 :, :].astype(f32)
        for grad_ref in grad_refs[1:]:
            proj_grad = proj_grad + grad_ref[rows // 2 :, :].astype(f32)
        proj_grad = stacked(proj_grad)
        slab = jnp.concatenate([weight_acc[...], proj_grad.T], axis=0).astype(bf16)
        along, cores, chunk, _ = slab_ref.shape
        for core in range(cores):
            for at in range(along):
                start = (core * along + at) * chunk
                slab_ref[at, core] = slab[start : start + chunk]


def assemble_kernel(places_ref, *refs, seq_count):
    own_refs = refs[:seq_count]
    other_refs = refs[seq_count : 2 * seq_count]
    qkv_ref, proj_ref, slabs = refs[2 * seq_count :]
    width = proj_ref.shape[0]
    group_width = width // seq_count
    half = own_refs[0].shape[0]
    @pl.when(pl.program_id(0) == 0)
    def _():
        for shift in range(seq_count):
            group = neighbour(places_ref, -shift, seq_count)
            for places, source_ref in (
                (places_ref[2], own_refs[shift]), (1 - places_ref[2], other_refs[shift]),
            ):
                start = pl.multiple_of(places * half, 16)
                slabs[group, pl.ds(start, half), :] = source_ref[...]

    part = pl.program_id(0)
    values = slabs[:, pl.ds(pl.multiple_of(part * group_width, 16), group_width), :]
    values = values.reshape(width, width).astype(f32)

    @pl.when(part < 3)
    def _():
        qkv_ref[...] = values.T

    @pl.when(part == 3)
    def _():
        proj_ref[...] = values


def input_grad_kernel(
    places_ref, weight_ref, tokens_ref, grad_middle_ref, gain_ref, before_ref, stats_ref,
    router_ref, *refs,
):
    *packed_refs, input_grad_ref, copies_ref, small_ref = refs
    _, patch_rows, width = tokens_ref.shape
    grad = jnp.zeros((patch_rows, width), f32)
    for shift, packed_ref in enumerate(packed_refs):
        group = neighbour(places_ref, -shift, len(packed_refs))
        grad = grad + mm(packed_ref[0], weight_ref[group])
    normed, inv_root = normalize(tokens_ref[0].astype(f32))
    row_grad = norm_row_grad(grad, normed, inv_root, gain_ref[...])
    input_grad_ref[0] = (grad_middle_ref[0] + row_grad).astype(bf16)

    @pl.when(pl.program_id(0) == 0)
    def _():
        small_ref[0:2, :] = before_ref[0:2, :]
        small_ref[2:3, :] = before_ref[2:3, :] + stats_ref[...]
        small_ref[3:5, :] = jnp.zeros((2, width), f32)
        small_ref[5:8, :] = jnp.zeros((3, width), f32)
        small_ref[5:6, : router_ref.shape[-1]] = jnp.sum(router_ref[...], axis=0)

    small_ref[3:4, :] += jnp.sum(grad * normed, axis=0, keepdims=True)
    small_ref[4:5, :] += jnp.sum(grad, axis=0, keepdims=True)

    @pl.when(pl.program_id(0) == pl.num_programs(0) - 1)
    def _():
        copies_ref[...] = jnp.broadcast_to(small_ref[...][None], copies_ref.shape)


def expert_grad_kernel(*refs, row_pieces, row_blocks):
    rows_ref, cotangent_ref, first_ref, second_ref = refs[:4]
    first_grad_ref, second_grad_ref, done_ref, grad_pre_ref, hidden_ref, scaled_ref = refs[-6:]
    stride, width = rows_ref.shape[-2:]
    rows = grad_pre_ref.shape[1]

    def scale():
        share = rows // rows_ref.shape[0]
        for place in range(rows_ref.shape[0]):
            own = slice(place * share, (place + 1) * share)
            scaled_ref[own, :] = scaled_rows(rows_ref[place, :, 0], cotangent_ref[place, :, 0])

    if row_blocks == 1:
        pl.when(pl.program_id(0) == 0)(scale)
    else:
        scale()
    moe_rows = rows_ref[...].reshape(rows, width)
    piece = rows // row_pieces
    first = first_ref[...]
    second = second_ref[...]
    for at in range(row_pieces):
        own = slice(at * piece, (at + 1) * piece)
        hidden, slope = gelu_pair(mm_nt(first, moe_rows[own]))
        hidden_ref[:, own] = hidden.astype(bf16)
        grad_pre_ref[:, own] = (mm_nt(second, scaled_ref[own, :]) * slope).astype(bf16)
    if row_blocks > 1:

        @pl.when(pl.program_id(1) == 0)
        def _():
            second_grad_ref[...] = jnp.zeros(second_grad_ref.shape, f32)
            first_grad_ref[...] = jnp.zeros(first_grad_ref.shape, f32)

        second_grad_ref[...] += mm(hidden_ref[...], scaled_ref[...])
        first_grad_ref[...] += mm(grad_pre_ref[...], moe_rows)
    else:
        second_grad_ref[...] = mm(hidden_ref[...], scaled_ref[...])
        first_grad_ref[...] = mm(grad_pre_ref[...], moe_rows)
    done_ref[...] = jnp.zeros(done_ref.shape, f32)


smem = pl.BlockSpec(memory_space=pltpu.SMEM)
vmem = pl.BlockSpec(memory_space=pltpu.VMEM)
params = pltpu.CompilerParams(vmem_limit_bytes=60 * 1024 * 1024)


def cost(microseconds):
    return pl.CostEstimate(
        flops=int(microseconds * 6e8), transcendentals=0, bytes_accessed=int(microseconds * 1e5)
    )


def struct(shape, dtype):
    return jax.ShapeDtypeStruct(shape, dtype)


def per_device(
    tokens, routes, priority, hires, gain_one, shift_one, w_qkv, w_proj, gain_two, shift_two,
    w_router, expert_in, expert_out, cotangent,
):
    image_count, patch_rows, width = tokens.shape
    rows = image_count * patch_rows
    seq_count = lax.axis_size("seq")
    ep_count = lax.axis_size("ep")
    full_rows = patch_rows * seq_count
    head_width = width // HEADS
    group_heads = HEADS // seq_count
    group_width = group_heads * head_width
    local_experts = max(1, EXPERTS // ep_count)
    split = max(1, ep_count // EXPERTS)
    local_hidden = expert_in.shape[0] // local_experts
    capacity = max(2, (105 * TOP * rows + 100 * EXPERTS - 1) // (100 * EXPERTS))
    stride = (capacity + 3 + 15) // 16 * 16
    chunks = 2 if local_experts % 2 == 0 else 1
    each = local_experts // chunks
    devices = seq_count * ep_count
    seq_place = lax.axis_index("seq")
    ep_place = lax.axis_index("ep")
    places = jnp.stack([hires[0], seq_place.astype(jnp.int32), (ep_place % 2).astype(jnp.int32)])
    gain_one, shift_one, gain_two, shift_two = (
        vector.reshape(1, width) for vector in (gain_one, shift_one, gain_two, shift_two)
    )
    common = dict(image_count=image_count, patch_rows=patch_rows, stride=stride)

    def exchange(values, axis):
        return lax.all_to_all(values, axis, split_axis=0, concat_axis=0, tiled=True)

    def send_slots(chunk):
        if split > 1:
            chunk = jnp.broadcast_to(chunk[:, None], (EXPERTS, split) + chunk.shape[1:])
            chunk = chunk.reshape((ep_count,) + chunk.shape[2:])
        return exchange(chunk, "ep")

    def move(values, axis, shift):
        count = lax.axis_size(axis)
        if shift % count == 0:
            return values
        return lax.ppermute(values, axis, [(at, (at + shift) % count) for at in range(count)])

    def other_core(values):
        return lax.ppermute(values, "ep", [(at, at ^ 1) for at in range(ep_count)])

    def hold(values, *others):
        values = tuple(values)
        anywhere = pl.BlockSpec(memory_space=pl.ANY)
        return call(
            lambda *refs: None,
            "hold",
            waits=others,
            in_specs=[anywhere] * len(values),
            out_specs=[anywhere] * len(values),
            out_shape=[struct(value.shape, value.dtype) for value in values],
            input_output_aliases={at: at for at in range(len(values))},
            cost_estimate=cost(1),
        )(*values)

    def over_seq(values):
        return lax.all_gather(values, "seq", axis=0, tiled=False)

    def call(kernel, name, waits=(), **spec):
        waits = tuple(waits)

        def run(*operands):
            count = len(operands)

            def body(*refs):
                kernel(*refs[:count], *refs[count + len(waits) :])

            unread = [pl.BlockSpec(memory_space=pl.ANY)] * len(waits)
            if "grid_spec" in spec:
                grid_spec = dict(spec["grid_spec"])
                grid_spec["in_specs"] = grid_spec["in_specs"] + unread
                own = dict(spec, grid_spec=pltpu.PrefetchScalarGridSpec(**grid_spec))
            else:
                own = dict(spec, in_specs=spec["in_specs"] + unread)
            return pl.pallas_call(body, name=name, compiler_params=params, **own)(
                *operands, *waits
            )

        return run

    def slot_struct(experts):
        return struct((min(ep_count, EXPERTS), experts, stride, width), bf16)

    chunk_struct = slot_struct(each)
    moved_struct = struct((ep_count, each, stride, width), bf16)

    tokens_moved = [move(tokens, "seq", shift) for shift in range(seq_count)]
    pairs = jnp.concatenate([routes.reshape(rows, TOP).T, priority.reshape(1, rows)], axis=0)
    route_col, dest_col, dest_row = call(
        lambda *refs: routing_kernel(*refs, capacity=capacity, **common),
        "routing",
        in_specs=[smem, vmem],
        out_specs=[vmem] * 3,
        out_shape=[
            struct((rows, TOP), jnp.int32),
            struct((rows, TOP), jnp.int32),
            struct((TOP, rows), jnp.int32),
        ],
        cost_estimate=cost(3),
    )(places, pairs)
    cotangent_sent = call(
        lambda *refs: send_grads_kernel(*refs, stride=stride),
        "send_grads",
        in_specs=[vmem] * 2,
        out_specs=[vmem] * chunks,
        out_shape=[chunk_struct] * chunks,
        cost_estimate=cost(3),
    )(cotangent, dest_row)
    weight_groups = (
        w_qkv.reshape(width, 3, seq_count, group_width)
        .transpose(2, 1, 3, 0)
        .reshape(seq_count, 3 * group_width, width)
    )

    cotangent_slots = [send_slots(chunk) for chunk in cotangent_sent]

    row_block = pl.BlockSpec((1, full_rows, group_width), lambda i, *_: (i, 0, 0))
    probs_block = pl.BlockSpec((1, group_heads, full_rows, full_rows), lambda i, *_: (i, 0, 0, 0))
    normed_block = pl.BlockSpec((1, full_rows, width), lambda i, *_: (i, 0, 0))
    half_block = pl.BlockSpec((1, patch_rows // 2, 2 * group_width), lambda i, *_: (i, 0, 0))
    packed_block = pl.BlockSpec((1, patch_rows, 3 * group_width), lambda i, *_: (i, 0, 0))
    vector_block = pl.BlockSpec((1, width), lambda i, *_: (0, 0))
    image_block = pl.BlockSpec((1, patch_rows, width), lambda i, *_: (i, 0, 0))
    half_struct = struct((image_count, patch_rows // 2, 2 * group_width), bf16)
    row_struct = struct((image_count, full_rows, group_width), bf16)
    def attention(first_image, count, previous, *others):
        def own(block):
            return pl.BlockSpec(
                block.block_shape, lambda i, *rest: block.index_map(first_image + i, *rest)
            )

        inputs = 4 + seq_count
        blocks = [half_block] * seq_count + [
            row_block, row_block, row_block, probs_block, normed_block,
        ]
        return call(
            lambda *refs: attention_kernel(
                *refs[:inputs],
                *refs[inputs + len(previous) :],
                first_image=first_image,
                seq_count=seq_count,
                group_heads=group_heads,
                head_width=head_width,
            ),
            "attention",
            waits=others,
            grid_spec=dict(
                num_scalar_prefetch=1,
                grid=(count,),
                in_specs=[
                    vector_block,
                    vector_block,
                    pl.BlockSpec((1, 3 * group_width, width), lambda i, at: (at[1], 0, 0)),
                ]
                + [own(image_block)] * seq_count
                + [pl.BlockSpec(memory_space=pl.ANY)] * len(previous),
                out_specs=[own(block) for block in blocks],
                scratch_shapes=[
                    pltpu.VMEM((seq_count, patch_rows, group_width), bf16),
                    pltpu.VMEM((seq_count, patch_rows, width), bf16),
                ],
            ),
            out_shape=[half_struct] * seq_count
            + [
                row_struct,
                row_struct,
                row_struct,
                struct((image_count, group_heads, full_rows, full_rows), bf16),
                struct((image_count, full_rows, width), bf16),
            ],
            input_output_aliases={inputs + at: at for at in range(len(previous))},
            cost_estimate=cost(30),
        )(places, gain_one, shift_one, weight_groups, *tokens_moved, *previous)

    started = attention(0, 1, (), *cotangent_sent)
    (watched,) = hold([cotangent_slots[0]], started[-1])
    cotangent_slots[0] = watched
    *attended, q, k, v, probs, attn_in = attention(1, image_count - 1, started, watched)
    attended_sent = attended
    attended = [move(block, "seq", shift) for shift, block in enumerate(attended)]
    cotangent_slots[1:] = hold(cotangent_slots[1:], attended_sent[1]) if chunks > 1 else []

    middle, gate, stats, *rows_sent = call(
        lambda *refs: dispatch_kernel(*refs, seq_count=seq_count, **common),
        "dispatch",
        waits=cotangent_slots,
        in_specs=[smem] + [vmem] * (7 + seq_count),
        out_specs=[vmem] * (3 + chunks),
        out_shape=[
            struct((rows, width), f32),
            struct((rows, EXPERTS), f32),
            struct((1, width), f32),
        ]
        + [chunk_struct] * chunks,
        cost_estimate=cost(9),
    )(
        places, tokens, w_proj, gain_two, shift_two, w_router, route_col, dest_row, *attended,
    )
    row_slots = [send_slots(chunk) for chunk in rows_sent]

    hidden_tile = local_hidden // 2
    tiles = local_hidden // hidden_tile
    moved_block = pl.BlockSpec((ep_count, 1, stride, width), lambda e, f: (0, e, 0, 0))
    cotangent_all = [over_seq(slots) for slots in cotangent_slots]
    grads_back, values_back = [], ()
    for at in range(chunks):
        weight_block = pl.BlockSpec(
            (hidden_tile, width), lambda e, f, at=at: ((e + at * each) * tiles + f, 0)
        )
        all_block = pl.BlockSpec(
            (ep_count, 1, stride, width), lambda e, f, at=at: (0, e + at * each, 0, 0)
        )
        value, back = call(
            lambda *refs: expert_kernel(*refs, pieces=max(1, hidden_tile // 768)),
            "experts",
            waits=cotangent_all[:1] * (at > 0),
            grid=(each, tiles),
            in_specs=[moved_block, moved_block, weight_block, weight_block]
            + [pl.BlockSpec(memory_space=pl.ANY)] * len(values_back),
            out_specs=[all_block, moved_block],
            out_shape=[struct((ep_count, local_experts, stride, width), bf16), moved_struct],
            scratch_shapes=[pltpu.VMEM((ep_count * stride, width), f32)] * 2
            + [pltpu.VMEM((ep_count * stride, width), bf16)],
            input_output_aliases={4: 0} if values_back else {},
            cost_estimate=cost(16),
        )(row_slots[at], cotangent_slots[at], expert_in, expert_out, *values_back)
        grads_back.append(exchange(back, "ep"))
        values_back = (value,)

    all_rows = seq_count * ep_count * stride
    grad_tile = min(768, local_hidden)
    grad_tiles = local_hidden // grad_tile
    anywhere = pl.BlockSpec(memory_space=pl.ANY)
    rows_all = [over_seq(slots) for slots in row_slots]
    grads = []

    row_blocks = max(1, all_rows // 1024)
    sources = ep_count // row_blocks
    block_rows = all_rows // row_blocks

    def expert_grads(expert, begin, count, *others):
        place = expert * grad_tiles + begin
        tile_block = pl.BlockSpec((grad_tile, width), lambda f, r: (place + f, 0))

        def source_block(own):
            return pl.BlockSpec(
                (seq_count, sources, 1, stride, width),
                lambda f, r: (0, r, own, 0, 0),
                pipeline_mode=pl.Buffered(1 if row_blocks == 1 else 2),
            )

        *grads[:], done = call(
            lambda *refs: expert_grad_kernel(
                *refs, row_pieces=max(1, block_rows // 512), row_blocks=row_blocks
            ),
            "expert_grads",
            waits=others,
            grid=(count, row_blocks),
            in_specs=[source_block(expert % each)] * 2 + [tile_block, tile_block]
            + [anywhere] * len(grads),
            out_specs=[tile_block, tile_block, pl.BlockSpec((8, 128), lambda f, r: (0, 0))],
            out_shape=[
                struct(expert_in.shape, f32),
                struct(expert_out.shape, f32),
                struct((8, 128), f32),
            ],
            scratch_shapes=[pltpu.VMEM((grad_tile, block_rows), bf16)] * 2
            + [pltpu.VMEM((block_rows, width), bf16)],
            input_output_aliases={4: 0, 5: 1} if grads else {},
            cost_estimate=cost(7 * count),
        )(rows_all[expert // each], cotangent_all[expert // each], expert_in, expert_out, *grads)
        return done

    work = [(expert, 0, grad_tiles) for expert in range(local_experts)]
    work = iter(work)

    def next_grads(*others):
        return [expert_grads(*part, *others) for part in itertools.islice(work, 1)]

    early = next_grads(values_back[0], grads_back[0]) if local_experts > 3 else []
    leaving_shape = ((rows + width) // 2, 2 * group_width)
    grad_middle, router_grad, small, *leaving = call(
        lambda *refs: combine_kernel(
            *refs, split=split, seq_count=seq_count, chunks=chunks, **common
        ),
        "combine",
        waits=early,
        in_specs=[smem] + [vmem] * (10 + seq_count + chunks),
        out_specs=[vmem] * (3 + seq_count),
        out_shape=[
            struct((rows, width), f32),
            struct((EXPERTS, 1, width) if devices == EXPERTS else (EXPERTS, width), f32),
            struct((3, width), f32),
        ]
        + [struct(leaving_shape, bf16)] * seq_count,
        cost_estimate=cost(10),
    )(
        places, middle, gate, cotangent, w_proj, gain_two, shift_two, w_router,
        route_col, dest_col, stats, *attended, *grads_back,
    )
    leaving = [move(block, "seq", -at) for at, block in enumerate(leaving)]
    piece = EXPERTS * width // devices
    router_grad = exchange(router_grad.reshape(devices, 1, piece), ("seq", "ep"))
    values_moved = exchange(values_back[0], "ep")
    middle_done = next_grads(grad_middle) if local_experts > 2 else []
    half = 2 * group_width
    pairs_along = ep_count // 2
    slab_shape = (pairs_along, 2, half // pairs_along, width)
    *packed_sent, slab = call(
        lambda *refs: attention_grad_kernel(
            *refs, group_heads=group_heads, head_width=head_width, seq_count=seq_count
        ),
        "attention_grad",
        waits=middle_done,
        grid=(image_count,),
        in_specs=[smem, row_block, row_block, row_block, probs_block, normed_block]
        + [pl.BlockSpec(leaving_shape, lambda i: (0, 0))] * seq_count,
        out_specs=[packed_block] * seq_count
        + [pl.BlockSpec(slab_shape, lambda i: (0, 0, 0, 0))],
        out_shape=[struct((image_count, patch_rows, 3 * group_width), bf16)] * seq_count
        + [struct(slab_shape, bf16)],
        scratch_shapes=[
            pltpu.VMEM((3 * group_width, width), f32),
            pltpu.VMEM((image_count, seq_count, patch_rows, group_width), bf16),
            pltpu.VMEM((seq_count, patch_rows, 3 * group_width), bf16),
        ],
        cost_estimate=cost(18),
    )(places, q, k, v, probs, attn_in, *leaving)
    packed = [move(block, "seq", shift) for shift, block in enumerate(packed_sent)]

    same_core = [[2 * at + core for at in range(pairs_along)] for core in range(2)]

    def along_core(values):
        return lax.all_to_all(
            values, "ep", split_axis=0, concat_axis=0, tiled=True, axis_index_groups=same_core
        )

    slab = lax.psum_scatter(
        slab.reshape(2 * half, width), "ep", scatter_dimension=0, tiled=True
    )
    late = next_grads(packed_sent[0], router_grad) if local_experts > 1 else []
    slab, packed[1] = hold([slab, packed[1]], *late, values_moved, *packed[2:])
    slab = jnp.broadcast_to(slab[None], (pairs_along, half // pairs_along, width))
    output, value_stats = call(
        lambda *refs: output_kernel(*refs, split=split, **common),
        "output",
        waits=[slab],
        in_specs=[smem] + [vmem] * 5,
        out_specs=[vmem] * 2,
        out_shape=[struct((image_count, patch_rows, width), bf16), struct((1, width), f32)],
        cost_estimate=cost(5),
    )(places, middle, gate, route_col, dest_col, values_moved)
    slab_moved = along_core(slab).reshape(half, width)
    own_slabs = [move(slab_moved, "seq", shift) for shift in range(seq_count)]
    input_grad, copies = call(
        input_grad_kernel,
        "input_grad",
        grid=(image_count,),
        in_specs=[
            smem,
            pl.BlockSpec((seq_count, 3 * group_width, width), lambda i: (0, 0, 0)),
            image_block,
            image_block,
            vector_block,
            pl.BlockSpec((3, width), lambda i: (0, 0)),
            pl.BlockSpec((1, width), lambda i: (0, 0)),
            pl.BlockSpec((devices, 1, piece), lambda i: (0, 0, 0)),
        ]
        + [packed_block] * seq_count,
        out_specs=[image_block, pl.BlockSpec((devices, 8, width), lambda i: (0, 0, 0))],
        out_shape=[
            struct((image_count, patch_rows, width), bf16),
            struct((devices, 8, width), f32),
        ],
        scratch_shapes=[pltpu.VMEM((8, width), f32)],
        cost_estimate=cost(7),
    )(
        places, weight_groups, tokens, grad_middle.reshape(image_count, patch_rows, width),
        gain_one, small, value_stats, router_grad, *packed,
    )
    own_slabs[1:] = hold(own_slabs[1:], *next_grads(input_grad, slab_moved))
    other_slabs = [other_core(each_slab) for each_slab in own_slabs]
    qkv_grad, proj_grad = call(
        lambda *refs: assemble_kernel(*refs, seq_count=seq_count),
        "assemble",
        grid=(4,),
        in_specs=[smem] + [pl.BlockSpec((half, width), lambda i: (0, 0))] * (2 * seq_count),
        out_specs=[
            pl.BlockSpec((width, width), lambda i: (0, jnp.minimum(i, 2))),
            pl.BlockSpec((width, width), lambda i: (0, 0)),
        ],
        out_shape=[struct((width, 3 * width), f32), struct((width, width), f32)],
        scratch_shapes=[pltpu.VMEM((seq_count, 2 * half, width), bf16)],
        cost_estimate=cost(8),
    )(places, *own_slabs, *other_slabs)

    copies = exchange(copies, ("seq", "ep"))
    sums = jnp.sum(copies[:, :5], axis=0)
    router_grad = copies[:, 5, :piece].reshape(EXPERTS, width).T
    return (
        output,
        input_grad,
        sums[3],
        sums[4],
        qkv_grad,
        proj_grad,
        sums[0],
        sums[1],
        router_grad,
        grads[0],
        grads[1],
        jnp.sqrt(sums[2, :3] / sums[2, 3]),
    )


def solution(mesh):
    in_specs = (
        P("ep", "seq", None),
        P("ep", "seq", None),
        P("ep", "seq"),
        P("ep"),
        P(),
        P(),
        P(),
        P(),
        P(),
        P(),
        P(),
        P("ep", None),
        P("ep", None),
        P("ep", "seq", None),
    )
    out_specs = (
        P("ep", "seq", None),
        P("ep", "seq", None),
        P(),
        P(),
        P(),
        P(),
        P(),
        P(),
        P(),
        P("ep", None),
        P("ep", None),
        P(),
    )
    return jax.shard_map(
        per_device, mesh=mesh, in_specs=in_specs, out_specs=out_specs, check_vma=False
    )
```

```python
import itertools

import jax
import jax.numpy as jnp
from jax import lax
from jax.experimental import pallas as pl
from jax.experimental.pallas import tpu as pltpu
from jax.sharding import PartitionSpec as P

HEADS = 12
EXPERTS = 32
TOP = 2
PATCHES = 576
SHORT = 196

norm_eps = 1e-06
neg_big = -1e30
f32 = jnp.float32
bf16 = jnp.bfloat16

tail_slope = 0.33
tail_terms = (
    0.18635779800457905,
    0.18295602991113566,
    0.2012232872944192,
    0.04722279904104141,
    0.40849559831839843,
    -0.3511445702318978,
    0.46023391759858995,
    -0.13534486747679436,
)


def mm(a, b):
    return lax.dot_general(a, b, (((1,), (0,)), ((), ())), preferred_element_type=f32)


def mm_nt(a, b):
    return lax.dot_general(a, b, (((1,), (1,)), ((), ())), preferred_element_type=f32)


def mm_tn(a, b):
    return lax.dot_general(a, b, (((0,), (0,)), ((), ())), preferred_element_type=f32)


def gelu_pair(v):
    size = jnp.abs(v)
    bell = jnp.exp2(v * v * -0.7213475204444817)
    t = 1.0 / (1.0 + size * (tail_slope * 0.7071067811865476))
    poly = tail_terms[-1] * 0.5
    for term in tail_terms[-2::-1]:
        poly = poly * t + term * 0.5
    tail = poly * t * bell
    cdf = jnp.where(v >= 0.0, 1.0 - tail, tail)
    return v * cdf, cdf + v * bell * 0.3989422804014327


def normalize(values):
    centred = values - jnp.mean(values, axis=-1, keepdims=True)
    inv_root = lax.rsqrt(jnp.mean(centred * centred, axis=-1, keepdims=True) + norm_eps)
    return centred * inv_root, inv_root


def norm_row_grad(upstream, normed, inv_root, gain):
    scaled = upstream * gain
    return inv_root * (
        scaled
        - jnp.mean(scaled, axis=-1, keepdims=True)
        - normed * jnp.mean(scaled * normed, axis=-1, keepdims=True)
    )


def valid_rows(places_ref, image_count, patch_rows, shape, axis):
    row = lax.broadcasted_iota(jnp.int32, shape, axis)
    first_patch = places_ref[1] * patch_rows
    valid = row < 0
    for image in range(image_count):
        length = jnp.where(image < places_ref[0], PATCHES, SHORT)
        start = image * patch_rows
        stop = start + jnp.clip(length - first_patch, 0, patch_rows)
        valid = valid | ((row >= start) & (row < stop))
    return valid


def routing_kernel(
    places_ref, pairs_ref, route_col_ref, dest_col_ref, dest_row_ref,
    *, image_count, patch_rows, capacity, stride,
):
    rows = pairs_ref.shape[1]
    eye = lax.broadcasted_iota(jnp.int32, (rows, rows), 0) == lax.broadcasted_iota(
        jnp.int32, (rows, rows), 1
    )

    def as_column(line):
        return jnp.sum(jnp.where(eye, line.astype(f32), 0.0), axis=1, keepdims=True).astype(
            jnp.int32
        )

    e_row = [pairs_ref[k : k + 1, :] for k in range(TOP)]
    e_col = [as_column(line) for line in e_row]
    prio_row = pairs_ref[TOP : TOP + 1, :]
    prio_col = as_column(prio_row)
    for k in range(TOP):
        route_col_ref[:, k : k + 1] = e_col[k]
    valid_col = valid_rows(places_ref, image_count, patch_rows, (rows, 1), 0)
    valid_row = valid_rows(places_ref, image_count, patch_rows, (1, rows), 1)
    weight_col = valid_col.astype(f32)
    weight_row = valid_row.astype(f32)
    row_first = (prio_row < prio_col).astype(f32) * weight_row
    col_first = (prio_col < prio_row).astype(f32) * weight_col
    for k in range(TOP):
        count = jnp.where(e_col[k] == e_row[k], row_first, 0.0)
        for earlier in range(k):
            count = count + jnp.where(e_col[k] == e_row[earlier], weight_row, 0.0)
        slot = jnp.sum(count, axis=1, keepdims=True).astype(jnp.int32)
        keep = valid_col & (slot < capacity)
        dest_col_ref[:, k : k + 1] = jnp.where(keep, e_col[k] * stride + slot, -1)
        count = jnp.where(e_col[k] == e_row[k], col_first, 0.0)
        for earlier in range(k):
            count = count + jnp.where(e_col[earlier] == e_row[k], weight_col, 0.0)
        slot = jnp.sum(count, axis=0, keepdims=True).astype(jnp.int32)
        keep = valid_row & (slot < capacity)
        dest_row_ref[k : k + 1, :] = jnp.where(keep, e_row[k] * stride + slot, -1)


def side_by_side(values):
    half = values.shape[0] // 2
    return jnp.concatenate([values[:half], values[half:]], axis=1)


def stacked(values):
    width = values.shape[1] // 2
    return jnp.concatenate([values[:, :width], values[:, width:]], axis=0)


def neighbour(places_ref, shift, seq_count):
    return (places_ref[1] + (shift + seq_count)) % seq_count


def attention_kernel(
    places_ref, gain_ref, shift_ref, weight_ref, *refs,
    first_image, seq_count, group_heads, head_width,
):
    tokens_refs = refs[:seq_count]
    attended_refs = refs[seq_count : 2 * seq_count]
    q_ref, k_ref, v_ref, probs_ref, normed_ref, spread_ref, tokens_ref = refs[2 * seq_count :]
    _, patch_rows, width = tokens_refs[0].shape
    for shift, source_ref in enumerate(tokens_refs):
        tokens_ref[neighbour(places_ref, -shift, seq_count)] = source_ref[0]
    total_rows = seq_count * patch_rows
    group_width = group_heads * head_width
    values = tokens_ref[...].reshape(total_rows, width).astype(f32)
    normed, _ = normalize(values)
    attn_in = (normed * gain_ref[...] + shift_ref[...]).astype(bf16)
    normed_ref[0] = attn_in
    q, k, v = (
        mm_nt(attn_in, weight_ref[0, part * group_width : (part + 1) * group_width, :]).astype(bf16)
        for part in range(3)
    )
    q_ref[0] = q
    k_ref[0] = k
    v_ref[0] = v
    length = jnp.where(first_image + pl.program_id(0) < places_ref[0], PATCHES, SHORT)
    key_valid = lax.broadcasted_iota(jnp.int32, (1, total_rows), 1) < length
    lane = lax.broadcasted_iota(jnp.int32, (1, group_width), 1)
    scaled_q = (q.astype(f32) * head_width ** (-0.5)).astype(bf16)
    attended = jnp.zeros((total_rows, group_width), f32)
    for head in range(group_heads):
        in_head = (lane >= head * head_width) & (lane < (head + 1) * head_width)
        scores = mm_nt(jnp.where(in_head, scaled_q, jnp.zeros_like(scaled_q)), k)
        scores = jnp.where(key_valid, scores, neg_big)
        exp_scores = jnp.exp(scores - jnp.max(scores, axis=-1, keepdims=True))
        inverse = 1.0 / jnp.sum(exp_scores, axis=-1, keepdims=True)
        probs = (exp_scores * inverse).astype(bf16)
        probs_ref[0, head] = probs
        attended = jnp.where(in_head, mm(probs, v), attended)
    spread_ref[...] = attended.astype(bf16).reshape(spread_ref.shape)
    for shift, attended_ref in enumerate(attended_refs):
        attended_ref[0] = side_by_side(spread_ref[neighbour(places_ref, shift, seq_count)])


def slot_picks(dest_row_ref, stride, k):
    slot = lax.broadcasted_iota(jnp.int32, (EXPERTS * stride, 1), 0)
    return (slot == dest_row_ref[k : k + 1, :]).astype(f32).astype(bf16)


def send_grads_kernel(cotangent_ref, dest_row_ref, *sent_refs, stride):
    width = cotangent_ref.shape[-1]
    cotangent = cotangent_ref[...].reshape(-1, width)
    pick = slot_picks(dest_row_ref, stride, 0)
    for k in range(1, TOP):
        pick = pick + slot_picks(dest_row_ref, stride, k)
    sent = mm(pick, cotangent).astype(bf16)
    store_chunks(sent_refs, sent, stride)


def store_chunks(chunk_refs, table, stride):
    width = table.shape[-1]
    targets, each = chunk_refs[0].shape[:2]
    grouped = table.reshape(targets, len(chunk_refs) * each, stride, width)
    for at, chunk_ref in enumerate(chunk_refs):
        chunk_ref[...] = grouped[:, at * each : (at + 1) * each]


def three_terms(values):
    high = values.astype(bf16)
    rest = values - high.astype(f32)
    middle = rest.astype(bf16)
    return high, middle, (rest - middle.astype(f32)).astype(bf16)


def diagonal(stride):
    row = lax.broadcasted_iota(jnp.int32, (1, stride, stride), 1)
    return row == lax.broadcasted_iota(jnp.int32, (1, stride, stride), 2)


def row_scalars(block, stride):
    spare = block[:, stride - 3 : stride, :stride].astype(f32)
    line = spare[:, 0:1] + spare[:, 1:2] + spare[:, 2:3]
    return jnp.sum(jnp.where(diagonal(stride), line, 0.0), axis=2, keepdims=True)


def with_scalars(block, column, stride):
    width = block.shape[-1]
    line = jnp.sum(jnp.where(diagonal(stride), column, 0.0), axis=1, keepdims=True)
    line = jnp.concatenate(
        [line, jnp.zeros((line.shape[0], 1, width - stride), f32)], axis=2
    )
    row = lax.broadcasted_iota(jnp.int32, (1, stride, 1), 1)
    for at, term in enumerate(three_terms(line)):
        block = jnp.where(row == stride - 3 + at, term.astype(f32), block)
    return block


def unpacked(blocks_ref):
    return jnp.concatenate([stacked(blocks_ref[at]) for at in range(blocks_ref.shape[0])], axis=0)


def group_rows(places_ref, shift, seq_count, group_width):
    start = neighbour(places_ref, shift, seq_count) * group_width
    return pl.ds(pl.multiple_of(start, 16), group_width)


def dispatch_kernel(
    places_ref, tokens_ref, proj_ref, gain_ref, shift_ref,
    router_ref, route_col_ref, dest_row_ref, *refs, image_count, patch_rows, stride, seq_count,
):
    attended_refs = refs[:seq_count]
    middle_ref, gate_ref, stats_ref, *sent_refs = refs[seq_count:]
    rows, width = middle_ref.shape
    group_width = attended_refs[0].shape[-1] // 2
    attn_out = jnp.zeros((rows, width), f32)
    for shift, attended_ref in enumerate(attended_refs):
        attn_out = attn_out + mm(
            unpacked(attended_ref),
            proj_ref[group_rows(places_ref, -shift, seq_count, group_width), :],
        )
    valid = valid_rows(places_ref, image_count, patch_rows, (rows, 1), 0).astype(f32)
    stats_ref[...] = total_at(attn_out * attn_out * valid, 0)
    middle = tokens_ref[...].reshape(rows, width).astype(f32) + attn_out
    middle_ref[...] = middle
    normed, _ = normalize(middle)
    moe_in = (normed * gain_ref[...] + shift_ref[...]).astype(bf16)
    logits = mm(moe_in, router_ref[...])
    exp_logits = jnp.exp(logits - jnp.max(logits, axis=-1, keepdims=True))
    gate = exp_logits / jnp.sum(exp_logits, axis=-1, keepdims=True)
    gate_ref[...] = gate
    expert_lane = lax.broadcasted_iota(jnp.int32, (1, EXPERTS), 1)
    pick_any = jnp.zeros((EXPERTS * stride, rows), bf16)
    slot_gate = jnp.zeros((EXPERTS * stride, 128), f32)
    for k in range(TOP):
        chosen = jnp.sum(
            jnp.where(expert_lane == route_col_ref[:, k : k + 1], gate, 0.0),
            axis=-1,
            keepdims=True,
        )
        pick = slot_picks(dest_row_ref, stride, k)
        pick_any = pick_any + pick
        lane = lax.broadcasted_iota(jnp.int32, (1, 128), 1)
        terms = jnp.zeros((rows, 128), f32)
        for at, term in enumerate(three_terms(jnp.broadcast_to(chosen, (rows, 128)))):
            terms = jnp.where(lane == at, term.astype(f32), terms)
        slot_gate = slot_gate + mm(pick, terms.astype(bf16))
    sent = mm(pick_any, moe_in).reshape(EXPERTS, stride, width)
    slot_gate = jnp.sum(slot_gate, axis=1, keepdims=True).reshape(EXPERTS, stride, 1)
    sent = with_scalars(sent, slot_gate, stride).astype(bf16)
    store_chunks(sent_refs, sent.reshape(EXPERTS * stride, width), stride)


def scaled_rows(rows_block, grads_block):
    groups, stride, width = rows_block.shape
    scale = row_scalars(rows_block, stride)
    return (grads_block.astype(f32) * scale).astype(bf16).reshape(groups * stride, width)


def expert_kernel(
    rows_ref, cotangent_ref, first_ref, second_ref, *refs, pieces,
):
    value_ref, back_ref, value_acc, grad_acc, scaled_ref = refs[-5:]
    count, _, stride, width = rows_ref.shape
    rows = count * stride
    piece = first_ref.shape[0] // pieces
    step = pl.program_id(1)

    @pl.when(step == 0)
    def _():
        scaled_ref[...] = scaled_rows(rows_ref[:, 0], cotangent_ref[:, 0])

    moe_rows = rows_ref[:, 0].reshape(rows, width)
    grad_rows = scaled_ref[...]
    value = jnp.zeros((rows, width), f32)
    grad = jnp.zeros((rows, width), f32)
    for at in range(pieces):
        first = first_ref[at * piece : (at + 1) * piece, :]
        second = second_ref[at * piece : (at + 1) * piece, :]
        hidden, slope = gelu_pair(mm_nt(moe_rows, first))
        grad_pre = (mm_nt(grad_rows, second) * slope).astype(bf16)
        value = value + mm(hidden.astype(bf16), second)
        grad = grad + mm(grad_pre, first)

    @pl.when(step == 0)
    def _():
        value_acc[...] = value
        grad_acc[...] = grad

    @pl.when(step > 0)
    def _():
        value_acc[...] += value
        grad_acc[...] += grad

    @pl.when(step == pl.num_programs(1) - 1)
    def _():
        value_low = value_acc[...].astype(bf16).reshape(count, stride, width)
        value_ref[:, 0] = value_low
        gate_grad = jnp.sum(
            cotangent_ref[:, 0].astype(f32) * value_low.astype(f32), axis=-1, keepdims=True
        )
        grad_low = grad_acc[...].reshape(count, stride, width)
        back_ref[:, 0] = with_scalars(grad_low, gate_grad, stride).astype(bf16)


def table_part(chunk_refs, part):
    split = chunk_refs[0].shape[0] * chunk_refs[0].shape[1] * len(chunk_refs) // EXPERTS
    pieces = []
    for chunk_ref in chunk_refs:
        sources, each, stride, width = chunk_ref.shape
        block = chunk_ref[...].reshape(sources // split, split, each, stride, width)
        pieces.append(block[:, part])
    table = pieces[0] if len(pieces) == 1 else jnp.concatenate(pieces, axis=1)
    return table.reshape(EXPERTS, table.shape[2], table.shape[3])


def combine_kernel(
    places_ref, middle_ref, gate_ref, cotangent_ref, proj_ref, gain_ref,
    shift_ref, router_ref, route_col_ref, dest_col_ref, stats_ref, *refs,
    image_count, patch_rows, stride, split, seq_count, chunks,
):
    attended_refs = refs[:seq_count]
    back_refs = refs[seq_count : seq_count + chunks]
    grad_middle_ref, router_grad_ref, small_ref = refs[seq_count + chunks :][:3]
    leaving_refs = refs[seq_count + chunks + 3 :]
    rows, width = middle_ref.shape
    group_width = attended_refs[0].shape[-1] // 2
    slots = EXPERTS * stride
    middle = middle_ref[...]
    gate = gate_ref[...]
    valid = valid_rows(places_ref, image_count, patch_rows, (rows, 1), 0).astype(f32)
    grad_total = cotangent_ref[...].reshape(rows, width).astype(f32) * valid
    expert_lane = lax.broadcasted_iota(jnp.int32, (1, EXPERTS), 1)
    slot_lane = lax.broadcasted_iota(jnp.int32, (1, stride), 1)
    slot = lax.broadcasted_iota(jnp.int32, (1, slots), 1)
    pick_any = jnp.zeros((rows, slots), bf16)
    for k in range(TOP):
        pick_any = pick_any + (slot == dest_col_ref[:, k : k + 1]).astype(f32).astype(bf16)
    grad_dispatch = jnp.zeros((rows, width), f32)
    scalar_rows = [jnp.zeros((rows, stride), f32) for _ in range(TOP)]
    own = [
        (expert_lane == route_col_ref[:, k : k + 1]).astype(f32).astype(bf16) for k in range(TOP)
    ]
    for part in range(split):
        table = table_part(back_refs, part)
        grad_dispatch = grad_dispatch + mm(pick_any, table.reshape(slots, width))
        for at in range(stride - 3, stride):
            line = table[:, at, :stride]
            for k in range(TOP):
                scalar_rows[k] = scalar_rows[k] + mm(own[k], line)
    grad_probs = jnp.zeros((rows, EXPERTS), f32)
    for k in range(TOP):
        place = dest_col_ref[:, k : k + 1] - route_col_ref[:, k : k + 1] * stride
        grad_gate = jnp.sum(
            jnp.where(slot_lane == place, scalar_rows[k], 0.0), axis=-1, keepdims=True
        )
        grad_probs = grad_probs + own[k].astype(f32) * grad_gate
    grad_logits = (
        gate * (grad_probs - jnp.sum(grad_probs * gate, axis=-1, keepdims=True))
    ).astype(bf16)
    grad_moe_in = grad_dispatch + mm_nt(grad_logits, router_ref[...])
    normed, inv_root = normalize(middle)
    moe_in = (normed * gain_ref[...] + shift_ref[...]).astype(bf16)
    grad_middle = grad_total + norm_row_grad(grad_moe_in, normed, inv_root, gain_ref[...])
    grad_middle_ref[...] = grad_middle
    grad_attn = grad_middle.astype(bf16)
    for shift in range(seq_count):
        attended = unpacked(attended_refs[shift])
        own_rows = group_rows(places_ref, -shift, seq_count, group_width)
        grads = mm_nt(grad_attn, proj_ref[own_rows, :]).astype(bf16)
        leaving_refs[shift][: rows // 2, :] = side_by_side(grads)
        grads = mm_tn(grad_attn, attended).astype(bf16)
        leaving_refs[shift][rows // 2 :, :] = side_by_side(grads)
    router_grad_ref[...] = mm_tn(grad_logits, moe_in).reshape(router_grad_ref.shape)
    small_ref[0:1, :] = jnp.sum(grad_moe_in * normed, axis=0, keepdims=True)
    small_ref[1:2, :] = jnp.sum(grad_moe_in, axis=0, keepdims=True)
    lane = lax.broadcasted_iota(jnp.int32, (1, width), 1)
    count = jnp.sum(valid, axis=0, keepdims=True) * width
    small_ref[2:3, :] = stats_ref[...] + jnp.where(lane == 3, count, 0.0)


def total_at(values, place):
    lane = lax.broadcasted_iota(jnp.int32, (1, values.shape[-1]), 1)
    by_lane = jnp.sum(values, axis=0, keepdims=True)
    return jnp.where(lane == place, jnp.sum(by_lane, axis=1, keepdims=True), 0.0)


def output_kernel(
    places_ref, middle_ref, gate_ref, route_col_ref, dest_col_ref, *refs,
    image_count, patch_rows, stride, split,
):
    value_refs = refs[:-2]
    output_ref, stats_ref = refs[-2:]
    rows, width = middle_ref.shape
    slots = EXPERTS * stride
    gate = gate_ref[...]
    expert_lane = lax.broadcasted_iota(jnp.int32, (1, EXPERTS), 1)
    slot = lax.broadcasted_iota(jnp.int32, (1, slots), 1)
    moe_out = jnp.zeros((rows, width), f32)
    tables = [table_part(value_refs, part).reshape(slots, width) for part in range(split)]
    for k in range(TOP):
        pick = (slot == dest_col_ref[:, k : k + 1]).astype(f32).astype(bf16)
        pair_value = mm(pick, tables[0])
        for table in tables[1:]:
            pair_value = pair_value + mm(pick, table)
        own = expert_lane == route_col_ref[:, k : k + 1]
        moe_out = moe_out + jnp.sum(jnp.where(own, gate, 0.0), axis=-1, keepdims=True) * pair_value
    valid = valid_rows(places_ref, image_count, patch_rows, (rows, 1), 0).astype(f32)
    total = middle_ref[...] + moe_out
    output_ref[...] = (total * valid).astype(bf16).reshape(output_ref.shape)
    stats_ref[...] = total_at(moe_out * moe_out * valid, 1) + total_at(total * total * valid, 2)


def attention_grad_kernel(
    places_ref, q_ref, k_ref, v_ref, probs_ref, normed_ref, *refs,
    group_heads, head_width, seq_count,
):
    grad_refs = refs[:seq_count]
    packed_refs = refs[seq_count : 2 * seq_count]
    slab_ref, weight_acc, grad_spread, packed_spread = refs[2 * seq_count :]
    patch_rows = grad_spread.shape[2]
    rows = grad_spread.shape[0] * patch_rows
    total_rows = q_ref.shape[1]
    group_width = group_heads * head_width
    scale = head_width ** (-0.5)

    @pl.when(pl.program_id(0) == 0)
    def _():
        for shift, grad_ref in enumerate(grad_refs):
            place = neighbour(places_ref, shift, seq_count)
            grads = stacked(grad_ref[: rows // 2, :])
            for image in range(grad_spread.shape[0]):
                grad_spread[image, place] = grads[image * patch_rows : (image + 1) * patch_rows]

    grad_heads = grad_spread[pl.program_id(0)].reshape(total_rows, group_width)
    q, k, v = q_ref[0], k_ref[0], v_ref[0]
    lane = lax.broadcasted_iota(jnp.int32, (1, group_width), 1)
    nothing = jnp.zeros_like(q)
    grad_q = jnp.zeros((total_rows, group_width), f32)
    grad_k = jnp.zeros((total_rows, group_width), f32)
    grad_v = jnp.zeros((total_rows, group_width), f32)
    for head in range(group_heads):
        in_head = (lane >= head * head_width) & (lane < (head + 1) * head_width)
        own_grad = jnp.where(in_head, grad_heads, nothing)
        probs_low = probs_ref[0, head]
        probs = probs_low.astype(f32)
        grad_probs = mm_nt(own_grad, v)
        delta = jnp.sum(probs * grad_probs, axis=-1, keepdims=True)
        grad_scores = (probs * (grad_probs - delta)).astype(bf16)
        grad_q = jnp.where(in_head, mm(grad_scores, k), grad_q)
        grad_k = jnp.where(in_head, mm_tn(grad_scores, q), grad_k)
        grad_v = jnp.where(in_head, mm_tn(probs_low, grad_heads), grad_v)
    packed = jnp.concatenate([grad_q * scale, grad_k * scale, grad_v], axis=1).astype(bf16)
    packed_spread[...] = packed.reshape(packed_spread.shape)
    for shift, packed_ref in enumerate(packed_refs):
        packed_ref[0] = packed_spread[neighbour(places_ref, shift, seq_count)]
    weight_grad = mm_tn(packed, normed_ref[0])

    @pl.when(pl.program_id(0) == 0)
    def _():
        weight_acc[...] = weight_grad

    @pl.when(pl.program_id(0) > 0)
    def _():
        weight_acc[...] += weight_grad

    @pl.when(pl.program_id(0) == pl.num_programs(0) - 1)
    def _():
        width = weight_acc.shape[1]
        proj_grad = grad_refs[0][rows // 2 :, :].astype(f32)
        for grad_ref in grad_refs[1:]:
            proj_grad = proj_grad + grad_ref[rows // 2 :, :].astype(f32)
        proj_grad = stacked(proj_grad)
        slab = jnp.concatenate([weight_acc[...], proj_grad.T], axis=0).astype(bf16)
        along, cores, chunk, _ = slab_ref.shape
        for core in range(cores):
            for at in range(along):
                start = (core * along + at) * chunk
                slab_ref[at, core] = slab[start : start + chunk]


def assemble_kernel(places_ref, *refs, seq_count):
    own_refs = refs[:seq_count]
    other_refs = refs[seq_count : 2 * seq_count]
    qkv_ref, proj_ref, slabs = refs[2 * seq_count :]
    width = proj_ref.shape[0]
    group_width = width // seq_count
    half = own_refs[0].shape[0]
    @pl.when(pl.program_id(0) == 0)
    def _():
        for shift in range(seq_count):
            group = neighbour(places_ref, -shift, seq_count)
            for places, source_ref in (
                (places_ref[2], own_refs[shift]), (1 - places_ref[2], other_refs[shift]),
            ):
                start = pl.multiple_of(places * half, 16)
                slabs[group, pl.ds(start, half), :] = source_ref[...]

    part = pl.program_id(0)
    values = slabs[:, pl.ds(pl.multiple_of(part * group_width, 16), group_width), :]
    values = values.reshape(width, width).astype(f32)

    @pl.when(part < 3)
    def _():
        qkv_ref[...] = values.T

    @pl.when(part == 3)
    def _():
        proj_ref[...] = values


def input_grad_kernel(
    places_ref, weight_ref, tokens_ref, grad_middle_ref, gain_ref, before_ref, stats_ref,
    router_ref, *refs,
):
    *packed_refs, input_grad_ref, copies_ref, small_ref = refs
    _, patch_rows, width = tokens_ref.shape
    grad = jnp.zeros((patch_rows, width), f32)
    for shift, packed_ref in enumerate(packed_refs):
        group = neighbour(places_ref, -shift, len(packed_refs))
        grad = grad + mm(packed_ref[0], weight_ref[group])
    normed, inv_root = normalize(tokens_ref[0].astype(f32))
    row_grad = norm_row_grad(grad, normed, inv_root, gain_ref[...])
    input_grad_ref[0] = (grad_middle_ref[0] + row_grad).astype(bf16)

    @pl.when(pl.program_id(0) == 0)
    def _():
        small_ref[0:2, :] = before_ref[0:2, :]
        small_ref[2:3, :] = before_ref[2:3, :] + stats_ref[...]
        small_ref[3:5, :] = jnp.zeros((2, width), f32)
        small_ref[5:8, :] = jnp.zeros((3, width), f32)
        small_ref[5:6, : router_ref.shape[-1]] = jnp.sum(router_ref[...], axis=0)

    small_ref[3:4, :] += jnp.sum(grad * normed, axis=0, keepdims=True)
    small_ref[4:5, :] += jnp.sum(grad, axis=0, keepdims=True)

    @pl.when(pl.program_id(0) == pl.num_programs(0) - 1)
    def _():
        copies_ref[...] = jnp.broadcast_to(small_ref[...][None], copies_ref.shape)


def expert_grad_kernel(*refs, row_pieces, row_blocks):
    rows_ref, cotangent_ref, first_ref, second_ref = refs[:4]
    first_grad_ref, second_grad_ref, done_ref, grad_pre_ref, hidden_ref, scaled_ref = refs[-6:]
    stride, width = rows_ref.shape[-2:]
    rows = grad_pre_ref.shape[1]

    def scale():
        share = rows // rows_ref.shape[0]
        for place in range(rows_ref.shape[0]):
            own = slice(place * share, (place + 1) * share)
            scaled_ref[own, :] = scaled_rows(rows_ref[place, :, 0], cotangent_ref[place, :, 0])

    if row_blocks == 1:
        pl.when(pl.program_id(0) == 0)(scale)
    else:
        scale()
    moe_rows = rows_ref[...].reshape(rows, width)
    piece = rows // row_pieces
    first = first_ref[...]
    second = second_ref[...]
    for at in range(row_pieces):
        own = slice(at * piece, (at + 1) * piece)
        hidden, slope = gelu_pair(mm_nt(first, moe_rows[own]))
        hidden_ref[:, own] = hidden.astype(bf16)
        grad_pre_ref[:, own] = (mm_nt(second, scaled_ref[own, :]) * slope).astype(bf16)
    if row_blocks > 1:

        @pl.when(pl.program_id(1) == 0)
        def _():
            second_grad_ref[...] = jnp.zeros(second_grad_ref.shape, f32)
            first_grad_ref[...] = jnp.zeros(first_grad_ref.shape, f32)

        second_grad_ref[...] += mm(hidden_ref[...], scaled_ref[...])
        first_grad_ref[...] += mm(grad_pre_ref[...], moe_rows)
    else:
        second_grad_ref[...] = mm(hidden_ref[...], scaled_ref[...])
        first_grad_ref[...] = mm(grad_pre_ref[...], moe_rows)
    done_ref[...] = jnp.zeros(done_ref.shape, f32)


smem = pl.BlockSpec(memory_space=pltpu.SMEM)
vmem = pl.BlockSpec(memory_space=pltpu.VMEM)
params = pltpu.CompilerParams(vmem_limit_bytes=60 * 1024 * 1024)


def cost(microseconds):
    return pl.CostEstimate(
        flops=int(microseconds * 6e8), transcendentals=0, bytes_accessed=int(microseconds * 1e5)
    )


def struct(shape, dtype):
    return jax.ShapeDtypeStruct(shape, dtype)


def per_device(
    tokens, routes, priority, hires, gain_one, shift_one, w_qkv, w_proj, gain_two, shift_two,
    w_router, expert_in, expert_out, cotangent,
):
    image_count, patch_rows, width = tokens.shape
    rows = image_count * patch_rows
    seq_count = lax.axis_size("seq")
    ep_count = lax.axis_size("ep")
    full_rows = patch_rows * seq_count
    head_width = width // HEADS
    group_heads = HEADS // seq_count
    group_width = group_heads * head_width
    local_experts = max(1, EXPERTS // ep_count)
    split = max(1, ep_count // EXPERTS)
    local_hidden = expert_in.shape[0] // local_experts
    capacity = max(2, (105 * TOP * rows + 100 * EXPERTS - 1) // (100 * EXPERTS))
    stride = (capacity + 3 + 15) // 16 * 16
    chunks = 2 if local_experts % 2 == 0 else 1
    each = local_experts // chunks
    devices = seq_count * ep_count
    seq_place = lax.axis_index("seq")
    ep_place = lax.axis_index("ep")
    places = jnp.stack([hires[0], seq_place.astype(jnp.int32), (ep_place % 2).astype(jnp.int32)])
    gain_one, shift_one, gain_two, shift_two = (
        vector.reshape(1, width) for vector in (gain_one, shift_one, gain_two, shift_two)
    )
    common = dict(image_count=image_count, patch_rows=patch_rows, stride=stride)

    def exchange(values, axis):
        return lax.all_to_all(values, axis, split_axis=0, concat_axis=0, tiled=True)

    def send_slots(chunk):
        if split > 1:
            chunk = jnp.broadcast_to(chunk[:, None], (EXPERTS, split) + chunk.shape[1:])
            chunk = chunk.reshape((ep_count,) + chunk.shape[2:])
        return exchange(chunk, "ep")

    def move(values, axis, shift):
        count = lax.axis_size(axis)
        if shift % count == 0:
            return values
        return lax.ppermute(values, axis, [(at, (at + shift) % count) for at in range(count)])

    def other_core(values):
        return lax.ppermute(values, "ep", [(at, at ^ 1) for at in range(ep_count)])

    def hold(values, *others):
        values = tuple(values)
        anywhere = pl.BlockSpec(memory_space=pl.ANY)
        return call(
            lambda *refs: None,
            "hold",
            waits=others,
            in_specs=[anywhere] * len(values),
            out_specs=[anywhere] * len(values),
            out_shape=[struct(value.shape, value.dtype) for value in values],
            input_output_aliases={at: at for at in range(len(values))},
            cost_estimate=cost(1),
        )(*values)

    def over_seq(values):
        return lax.all_gather(values, "seq", axis=0, tiled=False)

    def call(kernel, name, waits=(), **spec):
        waits = tuple(waits)

        def run(*operands):
            count = len(operands)

            def body(*refs):
                kernel(*refs[:count], *refs[count + len(waits) :])

            unread = [pl.BlockSpec(memory_space=pl.ANY)] * len(waits)
            if "grid_spec" in spec:
                grid_spec = dict(spec["grid_spec"])
                grid_spec["in_specs"] = grid_spec["in_specs"] + unread
                own = dict(spec, grid_spec=pltpu.PrefetchScalarGridSpec(**grid_spec))
            else:
                own = dict(spec, in_specs=spec["in_specs"] + unread)
            return pl.pallas_call(body, name=name, compiler_params=params, **own)(
                *operands, *waits
            )

        return run

    def slot_struct(experts):
        return struct((min(ep_count, EXPERTS), experts, stride, width), bf16)

    chunk_struct = slot_struct(each)
    moved_struct = struct((ep_count, each, stride, width), bf16)

    tokens_moved = [move(tokens, "seq", shift) for shift in range(seq_count)]
    pairs = jnp.concatenate([routes.reshape(rows, TOP).T, priority.reshape(1, rows)], axis=0)
    route_col, dest_col, dest_row = call(
        lambda *refs: routing_kernel(*refs, capacity=capacity, **common),
        "routing",
        in_specs=[smem, vmem],
        out_specs=[vmem] * 3,
        out_shape=[
            struct((rows, TOP), jnp.int32),
            struct((rows, TOP), jnp.int32),
            struct((TOP, rows), jnp.int32),
        ],
        cost_estimate=cost(3),
    )(places, pairs)
    cotangent_sent = call(
        lambda *refs: send_grads_kernel(*refs, stride=stride),
        "send_grads",
        in_specs=[vmem] * 2,
        out_specs=[vmem] * chunks,
        out_shape=[chunk_struct] * chunks,
        cost_estimate=cost(3),
    )(cotangent, dest_row)
    weight_groups = (
        w_qkv.reshape(width, 3, seq_count, group_width)
        .transpose(2, 1, 3, 0)
        .reshape(seq_count, 3 * group_width, width)
    )

    cotangent_slots = [send_slots(chunk) for chunk in cotangent_sent]

    row_block = pl.BlockSpec((1, full_rows, group_width), lambda i, *_: (i, 0, 0))
    probs_block = pl.BlockSpec((1, group_heads, full_rows, full_rows), lambda i, *_: (i, 0, 0, 0))
    normed_block = pl.BlockSpec((1, full_rows, width), lambda i, *_: (i, 0, 0))
    half_block = pl.BlockSpec((1, patch_rows // 2, 2 * group_width), lambda i, *_: (i, 0, 0))
    packed_block = pl.BlockSpec((1, patch_rows, 3 * group_width), lambda i, *_: (i, 0, 0))
    vector_block = pl.BlockSpec((1, width), lambda i, *_: (0, 0))
    image_block = pl.BlockSpec((1, patch_rows, width), lambda i, *_: (i, 0, 0))
    half_struct = struct((image_count, patch_rows // 2, 2 * group_width), bf16)
    row_struct = struct((image_count, full_rows, group_width), bf16)
    def attention(first_image, count, previous, *others):
        def own(block):
            return pl.BlockSpec(
                block.block_shape, lambda i, *rest: block.index_map(first_image + i, *rest)
            )

        inputs = 4 + seq_count
        blocks = [half_block] * seq_count + [
            row_block, row_block, row_block, probs_block, normed_block,
        ]
        return call(
            lambda *refs: attention_kernel(
                *refs[:inputs],
                *refs[inputs + len(previous) :],
                first_image=first_image,
                seq_count=seq_count,
                group_heads=group_heads,
                head_width=head_width,
            ),
            "attention",
            waits=others,
            grid_spec=dict(
                num_scalar_prefetch=1,
                grid=(count,),
                in_specs=[
                    vector_block,
                    vector_block,
                    pl.BlockSpec((1, 3 * group_width, width), lambda i, at: (at[1], 0, 0)),
                ]
                + [own(image_block)] * seq_count
                + [pl.BlockSpec(memory_space=pl.ANY)] * len(previous),
                out_specs=[own(block) for block in blocks],
                scratch_shapes=[
                    pltpu.VMEM((seq_count, patch_rows, group_width), bf16),
                    pltpu.VMEM((seq_count, patch_rows, width), bf16),
                ],
            ),
            out_shape=[half_struct] * seq_count
            + [
                row_struct,
                row_struct,
                row_struct,
                struct((image_count, group_heads, full_rows, full_rows), bf16),
                struct((image_count, full_rows, width), bf16),
            ],
            input_output_aliases={inputs + at: at for at in range(len(previous))},
            cost_estimate=cost(30),
        )(places, gain_one, shift_one, weight_groups, *tokens_moved, *previous)

    started = attention(0, 1, (), *cotangent_sent)
    (watched,) = hold([cotangent_slots[0]], started[-1])
    cotangent_slots[0] = watched
    *attended, q, k, v, probs, attn_in = attention(1, image_count - 1, started, watched)
    attended_sent = attended
    attended = [move(block, "seq", shift) for shift, block in enumerate(attended)]
    cotangent_slots[1:] = hold(cotangent_slots[1:], attended_sent[1]) if chunks > 1 else []

    middle, gate, stats, *rows_sent = call(
        lambda *refs: dispatch_kernel(*refs, seq_count=seq_count, **common),
        "dispatch",
        waits=cotangent_slots,
        in_specs=[smem] + [vmem] * (7 + seq_count),
        out_specs=[vmem] * (3 + chunks),
        out_shape=[
            struct((rows, width), f32),
            struct((rows, EXPERTS), f32),
            struct((1, width), f32),
        ]
        + [chunk_struct] * chunks,
        cost_estimate=cost(9),
    )(
        places, tokens, w_proj, gain_two, shift_two, w_router, route_col, dest_row, *attended,
    )
    row_slots = [send_slots(chunk) for chunk in rows_sent]

    hidden_tile = local_hidden // 2
    tiles = local_hidden // hidden_tile
    moved_block = pl.BlockSpec((ep_count, 1, stride, width), lambda e, f: (0, e, 0, 0))
    cotangent_all = [over_seq(slots) for slots in cotangent_slots]
    grads_back, values_back = [], ()
    for at in range(chunks):
        weight_block = pl.BlockSpec(
            (hidden_tile, width), lambda e, f, at=at: ((e + at * each) * tiles + f, 0)
        )
        all_block = pl.BlockSpec(
            (ep_count, 1, stride, width), lambda e, f, at=at: (0, e + at * each, 0, 0)
        )
        value, back = call(
            lambda *refs: expert_kernel(*refs, pieces=max(1, hidden_tile // 768)),
            "experts",
            waits=cotangent_all[:1] * (at > 0),
            grid=(each, tiles),
            in_specs=[moved_block, moved_block, weight_block, weight_block]
            + [pl.BlockSpec(memory_space=pl.ANY)] * len(values_back),
            out_specs=[all_block, moved_block],
            out_shape=[struct((ep_count, local_experts, stride, width), bf16), moved_struct],
            scratch_shapes=[pltpu.VMEM((ep_count * stride, width), f32)] * 2
            + [pltpu.VMEM((ep_count * stride, width), bf16)],
            input_output_aliases={4: 0} if values_back else {},
            cost_estimate=cost(16),
        )(row_slots[at], cotangent_slots[at], expert_in, expert_out, *values_back)
        grads_back.append(exchange(back, "ep"))
        values_back = (value,)

    all_rows = seq_count * ep_count * stride
    grad_tile = min(768, local_hidden)
    grad_tiles = local_hidden // grad_tile
    anywhere = pl.BlockSpec(memory_space=pl.ANY)
    rows_all = [over_seq(slots) for slots in row_slots]
    grads = []

    row_blocks = max(1, all_rows // 1024)
    sources = ep_count // row_blocks
    block_rows = all_rows // row_blocks

    def expert_grads(expert, begin, count, *others):
        place = expert * grad_tiles + begin
        tile_block = pl.BlockSpec((grad_tile, width), lambda f, r: (place + f, 0))

        def source_block(own):
            return pl.BlockSpec(
                (seq_count, sources, 1, stride, width),
                lambda f, r: (0, r, own, 0, 0),
                pipeline_mode=pl.Buffered(1 if row_blocks == 1 else 2),
            )

        *grads[:], done = call(
            lambda *refs: expert_grad_kernel(
                *refs, row_pieces=max(1, block_rows // 512), row_blocks=row_blocks
            ),
            "expert_grads",
            waits=others,
            grid=(count, row_blocks),
            in_specs=[source_block(expert % each)] * 2 + [tile_block, tile_block]
            + [anywhere] * len(grads),
            out_specs=[tile_block, tile_block, pl.BlockSpec((8, 128), lambda f, r: (0, 0))],
            out_shape=[
                struct(expert_in.shape, f32),
                struct(expert_out.shape, f32),
                struct((8, 128), f32),
            ],
            scratch_shapes=[pltpu.VMEM((grad_tile, block_rows), bf16)] * 2
            + [pltpu.VMEM((block_rows, width), bf16)],
            input_output_aliases={4: 0, 5: 1} if grads else {},
            cost_estimate=cost(7 * count),
        )(rows_all[expert // each], cotangent_all[expert // each], expert_in, expert_out, *grads)
        return done

    work = [(expert, 0, grad_tiles) for expert in range(local_experts)]
    work = iter(work)

    def next_grads(*others):
        return [expert_grads(*part, *others) for part in itertools.islice(work, 1)]

    early = next_grads(values_back[0], grads_back[0]) if local_experts > 3 else []
    leaving_shape = ((rows + width) // 2, 2 * group_width)
    grad_middle, router_grad, small, *leaving = call(
        lambda *refs: combine_kernel(
            *refs, split=split, seq_count=seq_count, chunks=chunks, **common
        ),
        "combine",
        waits=early,
        in_specs=[smem] + [vmem] * (10 + seq_count + chunks),
        out_specs=[vmem] * (3 + seq_count),
        out_shape=[
            struct((rows, width), f32),
            struct((EXPERTS, 1, width) if devices == EXPERTS else (EXPERTS, width), f32),
            struct((3, width), f32),
        ]
        + [struct(leaving_shape, bf16)] * seq_count,
        cost_estimate=cost(10),
    )(
        places, middle, gate, cotangent, w_proj, gain_two, shift_two, w_router,
        route_col, dest_col, stats, *attended, *grads_back,
    )
    leaving = [move(block, "seq", -at) for at, block in enumerate(leaving)]
    piece = EXPERTS * width // devices
    router_grad = exchange(router_grad.reshape(devices, 1, piece), ("seq", "ep"))
    values_moved = exchange(values_back[0], "ep")
    middle_done = next_grads(grad_middle) if local_experts > 2 else []
    half = 2 * group_width
    pairs_along = ep_count // 2
    slab_shape = (pairs_along, 2, half // pairs_along, width)
    *packed_sent, slab = call(
        lambda *refs: attention_grad_kernel(
            *refs, group_heads=group_heads, head_width=head_width, seq_count=seq_count
        ),
        "attention_grad",
        waits=middle_done,
        grid=(image_count,),
        in_specs=[smem, row_block, row_block, row_block, probs_block, normed_block]
        + [pl.BlockSpec(leaving_shape, lambda i: (0, 0))] * seq_count,
        out_specs=[packed_block] * seq_count
        + [pl.BlockSpec(slab_shape, lambda i: (0, 0, 0, 0))],
        out_shape=[struct((image_count, patch_rows, 3 * group_width), bf16)] * seq_count
        + [struct(slab_shape, bf16)],
        scratch_shapes=[
            pltpu.VMEM((3 * group_width, width), f32),
            pltpu.VMEM((image_count, seq_count, patch_rows, group_width), bf16),
            pltpu.VMEM((seq_count, patch_rows, 3 * group_width), bf16),
        ],
        cost_estimate=cost(18),
    )(places, q, k, v, probs, attn_in, *leaving)
    packed = [move(block, "seq", shift) for shift, block in enumerate(packed_sent)]

    same_core = [[2 * at + core for at in range(pairs_along)] for core in range(2)]

    def along_core(values):
        return lax.all_to_all(
            values, "ep", split_axis=0, concat_axis=0, tiled=True, axis_index_groups=same_core
        )

    slab = lax.psum_scatter(
        slab.reshape(2 * half, width), "ep", scatter_dimension=0, tiled=True
    )
    late = next_grads(packed_sent[0], router_grad) if local_experts > 1 else []
    slab, packed[1] = hold([slab, packed[1]], *late, values_moved, *packed[2:])
    slab = jnp.broadcast_to(slab[None], (pairs_along, half // pairs_along, width))
    output, value_stats = call(
        lambda *refs: output_kernel(*refs, split=split, **common),
        "output",
        waits=[slab],
        in_specs=[smem] + [vmem] * 5,
        out_specs=[vmem] * 2,
        out_shape=[struct((image_count, patch_rows, width), bf16), struct((1, width), f32)],
        cost_estimate=cost(5),
    )(places, middle, gate, route_col, dest_col, values_moved)
    slab_moved = along_core(slab).reshape(half, width)
    own_slabs = [move(slab_moved, "seq", shift) for shift in range(seq_count)]
    input_grad, copies = call(
        input_grad_kernel,
        "input_grad",
        grid=(image_count,),
        in_specs=[
            smem,
            pl.BlockSpec((seq_count, 3 * group_width, width), lambda i: (0, 0, 0)),
            image_block,
            image_block,
            vector_block,
            pl.BlockSpec((3, width), lambda i: (0, 0)),
            pl.BlockSpec((1, width), lambda i: (0, 0)),
            pl.BlockSpec((devices, 1, piece), lambda i: (0, 0, 0)),
        ]
        + [packed_block] * seq_count,
        out_specs=[image_block, pl.BlockSpec((devices, 8, width), lambda i: (0, 0, 0))],
        out_shape=[
            struct((image_count, patch_rows, width), bf16),
            struct((devices, 8, width), f32),
        ],
        scratch_shapes=[pltpu.VMEM((8, width), f32)],
        cost_estimate=cost(7),
    )(
        places, weight_groups, tokens, grad_middle.reshape(image_count, patch_rows, width),
        gain_one, small, value_stats, router_grad, *packed,
    )
    own_slabs[1:] = hold(own_slabs[1:], *next_grads(input_grad, slab_moved))
    other_slabs = [other_core(each_slab) for each_slab in own_slabs]
    qkv_grad, proj_grad = call(
        lambda *refs: assemble_kernel(*refs, seq_count=seq_count),
        "assemble",
        grid=(4,),
        in_specs=[smem] + [pl.BlockSpec((half, width), lambda i: (0, 0))] * (2 * seq_count),
        out_specs=[
            pl.BlockSpec((width, width), lambda i: (0, jnp.minimum(i, 2))),
            pl.BlockSpec((width, width), lambda i: (0, 0)),
        ],
        out_shape=[struct((width, 3 * width), f32), struct((width, width), f32)],
        scratch_shapes=[pltpu.VMEM((seq_count, 2 * half, width), bf16)],
        cost_estimate=cost(8),
    )(places, *own_slabs, *other_slabs)

    copies = exchange(copies, ("seq", "ep"))
    sums = jnp.sum(copies[:, :5], axis=0)
    router_grad = copies[:, 5, :piece].reshape(EXPERTS, width).T
    return (
        output,
        input_grad,
        sums[3],
        sums[4],
        qkv_grad,
        proj_grad,
        sums[0],
        sums[1],
        router_grad,
        grads[0],
        grads[1],
        jnp.sqrt(sums[2, :3] / sums[2, 3]),
    )


def solution(mesh):
    in_specs = (
        P("ep", "seq", None),
        P("ep", "seq", None),
        P("ep", "seq"),
        P("ep"),
        P(),
        P(),
        P(),
        P(),
        P(),
        P(),
        P(),
        P("ep", None),
        P("ep", None),
        P("ep", "seq", None),
    )
    out_specs = (
        P("ep", "seq", None),
        P("ep", "seq", None),
        P(),
        P(),
        P(),
        P(),
        P(),
        P(),
        P(),
        P("ep", None),
        P("ep", None),
        P(),
    )
    return jax.shard_map(
        per_device, mesh=mesh, in_specs=in_specs, out_specs=out_specs, check_vma=False
    )
```
